32 devices in a mesh: shard: 8 (over y, x, core), rep: 4 (over z).
Axes of the slice: x: 2, y: 2, z: 4, core: 2. Of those that a mesh axis runs over, the one named last changes fastest.
Arguments:
- tokens: bfloat16 [2, 16384, 768], P(None, ('shard', 'rep')), may hold values from -6 to 6
- segment_ids: int32 [2, 16384], P(None, ('shard', 'rep')), may hold values from 0 to 7, as said below
- qkv_weight: bfloat16 [768, 2304], P('shard'), may hold values from -0.21875 to 0.21875
- out_weight: bfloat16 [768, 768], P('shard'), may hold values from -0.875 to 0.875
- gate_weight: bfloat16 [768, 3072], P('shard'), may hold values from -0.21875 to 0.21875
- up_weight: bfloat16 [768, 3072], P('shard'), may hold values from -0.21875 to 0.21875
- down_weight: bfloat16 [3072, 768], P('shard'), may hold values from -0.109375 to 0.109375
- norm1_gain: bfloat16 [768], P('shard'), may hold values from 0.5 to 1.5
- norm1_bias: bfloat16 [768], P('shard'), may hold values from -1 to 1
- norm2_gain: bfloat16 [768], P('shard'), may hold values from 0.5 to 1.5
- norm2_bias: bfloat16 [768], P('shard'), may hold values from -1 to 1
- out_grad: bfloat16 [2, 16384, 768], P(None, ('shard', 'rep')), may hold values from -6 to 6
Outputs:
- output: bfloat16 [2, 16384, 768], P(None, ('shard', 'rep'))
- input_grad: bfloat16 [2, 16384, 768], P(None, ('shard', 'rep'))
- qkv_weight_grad: float32 [768, 2304], P('shard')
- out_weight_grad: float32 [768, 768], P('shard')
- gate_weight_grad: float32 [768, 3072], P('shard')
- up_weight_grad: float32 [768, 3072], P('shard')
- down_weight_grad: float32 [3072, 768], P('shard')
- norm1_gain_grad: float32 [768], P('shard')
- norm1_bias_grad: float32 [768], P('shard')
- norm2_gain_grad: float32 [768], P('shard')
- norm2_bias_grad: float32 [768], P('shard')
The draws below stay inside these ranges and needn't reach their ends.
Inputs may be any that keep to these rules, and one draw needn't show every extreme that they name: Within each packed sequence of 512 tokens segment_ids never falls, starts at 0, and takes each value 0 to 7 on a run of one or more tokens.
All inputs are finite; a program needn't handle non-finite values.
Results may differ from the reference program's by a relative error of at most 0.02.
Values may be sent and summed in bfloat16 or wider, within the bound.
No kernel may reach another device: no remote copies, remote signals or barrier semaphores. Data moves between devices by JAX's collectives and lax.ppermute only.
A program may use at most 192 MiB of HBM per device.

```python
import math
import jax
import jax.numpy as jnp
from jax import lax

HEADS = 12
HEAD_DIM = 64
D = 768
FF = 3072
SEQ = 512
MB = 2
NDOC = 8
SEQS = 32


def doc_layout(key):
    tier_draw = jax.random.randint(jax.random.fold_in(key, 7), (MB, SEQS, NDOC), 0, 7)
    weights = jnp.left_shift(jnp.ones_like(tier_draw), tier_draw)
    spare_cells = SEQ - NDOC
    shares = weights * spare_cells // jnp.sum(weights, -1, keepdims=True)
    lengths = 1 + shares
    lengths = lengths.at[..., NDOC - 1].add(SEQ - jnp.sum(lengths, -1))
    zero_col = jnp.zeros((MB, SEQS, 1), jnp.int32)
    return jnp.concatenate([zero_col, jnp.cumsum(lengths, -1).astype(jnp.int32)], -1)


def draw_segment_ids(key, part):
    starts = doc_layout(key)
    places = jnp.arange(SEQ, dtype=jnp.int32)
    inner_starts = starts[:, :, 1:NDOC]
    segment = jnp.sum((places[None, None, :, None] >= inner_starts[:, :, None, :]).astype(jnp.int32), -1)
    return segment.reshape(MB, SEQS * SEQ).astype(jnp.int32)


def block_levels(key, dims, cuts, smallest, high):
    factor_of = 1.0
    for position, parts in cuts:
        heights = jax.random.uniform(jax.random.fold_in(jax.random.fold_in(key, 6), position), (parts,), jnp.float32, smallest / len(cuts), high / len(cuts))
        factor_of = factor_of * jnp.repeat(jnp.exp(heights), dims[position] // parts).reshape((-1,) + (1,) * (len(dims) - 1 - position))
    return factor_of


def bell_draw(stream_key, extent, deviation, most, shards=(), kind=jnp.bfloat16):
    gain = block_levels(stream_key, extent, shards, -0.22, 0.18) if shards else 1.0
    drawn = jax.random.normal(stream_key, extent, jnp.float32) * deviation * gain
    return jnp.minimum(jnp.maximum(drawn, -most), most).astype(kind)


def setup_inputs(seed: int = 0) -> dict:
    seeds = jax.random.split(jax.random.key(seed), 13)
    tokens = bell_draw(seeds[0], (MB, SEQS * SEQ, D), 1.0, 6.0, ((1, 32),))
    segment_ids = draw_segment_ids(jax.random.fold_in(seeds[12], 71), 0)
    qkv_weight = bell_draw(seeds[2], (D, 3 * D), D ** -0.5, 0.21875, ((0, 8),))
    out_weight = bell_draw(seeds[3], (D, D), (D // 16) ** -0.5, 0.875, ((0, 8),))
    gate_weight = bell_draw(seeds[4], (D, FF), D ** -0.5, 0.21875, ((0, 8),))
    up_weight = bell_draw(seeds[5], (D, FF), D ** -0.5, 0.21875, ((0, 8),))
    down_weight = bell_draw(seeds[6], (FF, D), FF ** -0.5, 0.109375, ((0, 8),))
    norm1_gain = jnp.clip(1.0 + 0.1 * jax.random.normal(seeds[7], (D,), jnp.float32), 0.5, 1.5).astype(jnp.bfloat16)
    norm1_bias = bell_draw(seeds[8], (D,), 0.2, 1.0, ((0, 8),))
    norm2_gain = jnp.clip(1.0 + 0.1 * jax.random.normal(seeds[9], (D,), jnp.float32), 0.5, 1.5).astype(jnp.bfloat16)
    norm2_bias = bell_draw(seeds[10], (D,), 0.2, 1.0, ((0, 8),))
    out_grad = bell_draw(seeds[11], (MB, SEQS * SEQ, D), 1.0, 6.0, ((1, 32),))
    return {"tokens": tokens, "segment_ids": segment_ids, "qkv_weight": qkv_weight, "out_weight": out_weight, "gate_weight": gate_weight, "up_weight": up_weight, "down_weight": down_weight, "norm1_gain": norm1_gain, "norm1_bias": norm1_bias, "norm2_gain": norm2_gain, "norm2_bias": norm2_bias, "out_grad": out_grad}


@jax.custom_vjp
def low(v):
    return lax.optimization_barrier(v.astype(jnp.bfloat16)).astype(jnp.float32)

@jax.custom_vjp
def low_back(v):
    return v

def low_keep(v):
    return (low(v), None)

def low_pass(kept, grad):
    return (grad,)

def back_keep(v):
    return (v, None)

def back_low(kept, grad):
    return (low(grad),)
low.defvjp(low_keep, low_pass)
low_back.defvjp(back_keep, back_low)
norm_eps = 1e-12
rope_base = 1000.0
masked_score = -1000000000.0
highest = lax.Precision.HIGHEST

def rope_tables(seq_len, head_dim):
    places = jnp.arange(seq_len, dtype=jnp.int32).astype(jnp.float32)
    frequency = rope_base ** (-jnp.arange(0, head_dim, 2, dtype=jnp.float32) / head_dim)
    angles = places[:, None] * frequency[None, :]
    cos_table = jnp.cos(angles)
    sin_table = jnp.sin(angles)
    return (jnp.concatenate([cos_table, cos_table], -1), jnp.concatenate([sin_table, sin_table], -1))

def rotate(values, cos_table, sin_table):
    half_dim = values.shape[-1] // 2
    turned = jnp.concatenate([-values[..., half_dim:], values[..., :half_dim]], -1)
    return values * cos_table + turned * sin_table

def layer_norm(hidden_in, gain_vec, shift_vec):
    centre = hidden_in - lax.optimization_barrier(jnp.mean(hidden_in, -1, keepdims=True))
    inv_std = lax.rsqrt(lax.optimization_barrier(jnp.mean(centre * centre, -1, keepdims=True)) + norm_eps)
    return centre * inv_std * gain_vec + shift_vec

def attend_pack(operands):
    query_s, key_s, value_s, segment = operands
    scores = jnp.einsum('shd,thd->hst', query_s, key_s, precision=highest) * 0.125
    scores = low_back(scores)
    same_doc = segment[:, None] == segment[None, :]
    scores = jnp.where(same_doc[None], scores, masked_score)
    row_max = lax.optimization_barrier(jnp.max(scores, -1, keepdims=True))
    expo = jnp.exp(scores - row_max)
    probs = low(expo / lax.optimization_barrier(jnp.sum(expo, -1, keepdims=True)))
    return jnp.einsum('hst,thd->shd', probs, value_s, precision=highest)

def forward(token_rows, segment, cos_table, sin_table, full_qkv, full_out, full_gate, full_up, full_down, gain_one, bias_one, gain_two, bias_two):
    group_size, seq_len, width = token_rows.shape
    shape_heads = (group_size, seq_len, HEADS, HEAD_DIM)
    joint = low_back(jnp.einsum('gsd,de->gse', token_rows, full_qkv, precision=highest))
    cos_heads = cos_table[None, :, None, :]
    sin_heads = sin_table[None, :, None, :]
    queries = low(rotate(joint[..., :width].reshape(shape_heads), cos_heads, sin_heads))
    key_rows = low(rotate(joint[..., width:2 * width].reshape(shape_heads), cos_heads, sin_heads))
    value_rows = low(joint[..., 2 * width:].reshape(shape_heads))
    attended = lax.map(jax.checkpoint(attend_pack), (queries, key_rows, value_rows, segment))
    attended = low(low_back(attended.reshape(group_size, seq_len, width)))
    branch = low_back(jnp.einsum('gsd,de->gse', attended, full_out, precision=highest))
    mixed = layer_norm(token_rows + branch, gain_one, bias_one)
    mixed_low = low(mixed)
    gate_pre = low_back(jnp.einsum('gsd,df->gsf', mixed_low, full_gate, precision=highest))
    up_pre = low_back(jnp.einsum('gsd,df->gsf', mixed_low, full_up, precision=highest))
    hidden_low = low(gate_pre * jax.nn.sigmoid(gate_pre) * up_pre)
    mlp_out = low_back(jnp.einsum('gsf,fd->gsd', hidden_low, full_down, precision=highest))
    return layer_norm(mixed + mlp_out, gain_two, bias_two)

def reference(tokens, segment_ids, qkv_weight, out_weight, gate_weight, up_weight, down_weight, norm1_gain, norm1_bias, norm2_gain, norm2_bias, out_grad):
    params = tuple((weight_arg.astype(jnp.float32) for weight_arg in (qkv_weight, out_weight, gate_weight, up_weight, down_weight, norm1_gain, norm1_bias, norm2_gain, norm2_bias)))
    group_size = math.gcd(SEQS, max(1, 4096 // SEQ))
    block_count = MB * SEQS // group_size
    token_blocks = tokens.astype(jnp.float32).reshape(block_count, group_size, SEQ, D)
    seg_blocks = segment_ids.reshape(block_count, group_size, SEQ)
    grad_blocks = out_grad.astype(jnp.float32).reshape(block_count, group_size, SEQ, D)
    cos_table, sin_table = rope_tables(SEQ, HEAD_DIM)

    def step_block(carry, item):
        token_rows, segment, cotangent = item

        def forward_fn(token_in, *weight_list):
            return forward(token_in, segment, cos_table, sin_table, *weight_list)
        result, pull_back = jax.vjp(forward_fn, token_rows, *params)
        grad_list = pull_back(cotangent)
        new_carry = tuple((left_sum + right_sum for left_sum, right_sum in zip(carry, grad_list[1:])))
        return (new_carry, (result.astype(jnp.bfloat16), grad_list[0].astype(jnp.bfloat16)))
    initial = tuple((jnp.zeros(param_arr.shape, jnp.float32) for param_arr in params))
    totals, (out_blocks, input_blocks) = lax.scan(step_block, initial, (token_blocks, seg_blocks, grad_blocks))
    return (out_blocks.reshape(MB, SEQS * SEQ, D), input_blocks.reshape(MB, SEQS * SEQ, D), totals[0], totals[1], totals[2], totals[3], totals[4], totals[5], totals[6], totals[7], totals[8])
```

```python
import functools

import jax
import jax.numpy as jnp
from jax import lax
from jax.experimental import pallas as pl
from jax.experimental.pallas import tpu as pltpu
from jax.sharding import PartitionSpec as P

HEAD_DIM = 64
norm_eps = 1e-12
rope_base = 1000.0
masked_score = -1e30
f32 = jnp.float32
bf16 = jnp.bfloat16
ANY = pl.BlockSpec(memory_space=pl.ANY)
SMEM = pl.BlockSpec(memory_space=pltpu.SMEM)


def dot_nn(a, b):
    return lax.dot_general(a, b, (((1,), (0,)), ((), ())), preferred_element_type=f32)


def dot_nt(a, b):
    return lax.dot_general(a, b, (((1,), (1,)), ((), ())), preferred_element_type=f32)


def dot_tn(a, b):
    return lax.dot_general(a, b, (((0,), (0,)), ((), ())), preferred_element_type=f32)


def whole(shape):
    return pl.BlockSpec(shape, lambda *_: (0,) * len(shape))


def xor_permute(x, bit):
    count = lax.axis_size("shard")
    return lax.ppermute(x, "shard", [(i, i ^ bit) for i in range(count)])


def gather_pieces(own):
    count = lax.axis_size("shard")
    rows = own.shape[0]
    if count == 8:
        half = rows // 2
        from_x = xor_permute(own, 2)
        from_y = xor_permute(own, 4)
        far_a = xor_permute(from_y[:half], 2)
        far_b = xor_permute(from_x[half:], 4)
        pieces = [(0, 0, own), (2, 0, from_x), (4, 0, from_y), (6, 0, far_a), (6, half, far_b)]
    else:
        pieces = [(0, 0, own)]
        bit = 2
        while bit < count:
            pieces += [(r | bit, lo, xor_permute(p, bit)) for r, lo, p in pieces]
            bit *= 2
    return pieces + [(r | 1, lo, xor_permute(p, 1)) for r, lo, p in pieces]


def reduce_own(keep, send):
    held = keep + xor_permute(send, 1)
    parts = [held[0].astype(f32)]
    for q in range(1, held.shape[0]):
        parts.append(xor_permute(held[q], 2 * q).astype(f32))
    return functools.reduce(jnp.add, parts).astype(bf16)


def start_loads(metas, refs, me, shard_rows, dst, lo, cols, sems):
    copies = []
    for i, ((rel, first, rows), ref) in enumerate(zip(metas, refs)):
        at = (me ^ rel) * shard_rows + first
        copy = pltpu.make_async_copy(
            ref.at[:, pl.ds(lo, cols)],
            dst.at[pl.ds(pl.multiple_of(at, 8), rows), :],
            sems.at[i],
        )
        copy.start()
        copies.append(copy)
    return copies


def wait_all(copies):
    for copy in copies:
        copy.wait()


def metas_of(pieces):
    return tuple((rel, first, p.shape[0]) for rel, first, p in pieces)


def arrays_of(pieces):
    return [p for _, _, p in pieces]


def half_mask(shape):
    lane = lax.broadcasted_iota(jnp.int32, shape, len(shape) - 1)
    return (lane % HEAD_DIM) < HEAD_DIM // 2


def normalize(h):
    centre = h - jnp.mean(h, -1, keepdims=True)
    inv = lax.rsqrt(jnp.mean(centre * centre, -1, keepdims=True) + norm_eps)
    return centre * inv, inv


def norm_back(e, n, inv):
    return inv * (e - jnp.mean(e, -1, keepdims=True) - n * jnp.mean(e * n, -1, keepdims=True))


def qkv_kernel(metas, shard_rows, me_ref, x_ref, cos_ref, sin_ref, *rest):
    refs, (out_ref, w_ref, sems) = rest[: len(metas)], rest[len(metas) :]
    width = x_ref.shape[1]

    @pl.when(pl.program_id(0) == 0)
    def _():
        wait_all(start_loads(metas, refs, me_ref[0], shard_rows, w_ref, 0, w_ref.shape[1], sems))

    block = out_ref.shape[1]
    j = pl.program_id(0)
    lo = pl.multiple_of(j * block, block)
    y = dot_nn(x_ref[...], w_ref[:, pl.ds(lo, block)])

    @pl.when(lo < 2 * width)
    def _():
        rows, reps = cos_ref.shape[0], y.shape[0] // cos_ref.shape[0]
        first = half_mask((rows, 128))
        scale = jnp.where(lo < width, 0.125, 1.0).astype(f32)
        cos = cos_ref[...] * scale
        sin = sin_ref[...] * scale
        sin = jnp.where(first, -sin, sin)
        for s in range(reps):
            for b in range(block // 128):
                u = y[s * rows : (s + 1) * rows, b * 128 : (b + 1) * 128]
                turned = jnp.where(first, pltpu.roll(u, 96, 1), pltpu.roll(u, 32, 1))
                out_ref[s * rows : (s + 1) * rows, b * 128 : (b + 1) * 128] = (
                    u * cos + turned * sin
                ).astype(bf16)

    @pl.when(lo >= 2 * width)
    def _():
        out_ref[...] = y.astype(bf16)


def qkv_forward(me, tokens, cos, sin, pieces, shard_rows):
    rows, width = tokens.shape
    metas = metas_of(pieces)
    block = 256
    total = 3 * width
    return pl.pallas_call(
        functools.partial(qkv_kernel, metas, shard_rows),
        grid=(total // block,),
        in_specs=[SMEM, whole(tokens.shape), whole(cos.shape), whole(sin.shape)]
        + [ANY] * len(metas),
        out_specs=pl.BlockSpec((rows, block), lambda j: (0, j)),
        out_shape=jax.ShapeDtypeStruct((rows, total), bf16),
        scratch_shapes=[
            pltpu.VMEM((width, total), bf16),
            pltpu.SemaphoreType.DMA((len(metas),)),
        ],
        cost_estimate=pl.CostEstimate(
            flops=2 * rows * width * total, bytes_accessed=10_000_000, transcendentals=0
        ),
        name="qkv_rope",
    )(me, tokens, cos, sin, *arrays_of(pieces))


def attend_kernel(q_ref, k_ref, v_ref, row_ref, col_ref, o_ref, p_ref, bias_ref):
    @pl.when(pl.program_id(1) == 0)
    def _():
        bias_ref[...] = jnp.where(row_ref[0] == col_ref[0], 0.0, masked_score).astype(f32)

    heads = p_ref.shape[1]
    lane = lax.broadcasted_iota(jnp.int32, (1, 128), 1)
    for pair in range(heads // 2):
        cols = slice(pair * 128, (pair + 1) * 128)
        q, k, v = q_ref[:, cols], k_ref[:, cols], v_ref[:, cols]
        acc = None
        for side in range(2):
            mine = ((lane // HEAD_DIM) == side).astype(bf16)
            s = dot_nt(q, k * mine) + bias_ref[...]
            e = jnp.exp(s - jnp.max(s, -1, keepdims=True))
            inv = 1.0 / jnp.sum(e, -1, keepdims=True)
            p = (e * inv).astype(bf16)
            p_ref[0, pair * 2 + side] = p
            part = dot_nn(p, v * mine)
            acc = part if acc is None else acc + part
        o_ref[:, cols] = acc.astype(bf16)


def attend_forward(joint, seg_row, seg_col, width, quad=4):
    rows = joint.shape[0]
    seqs, _, seq = seg_row.shape
    lanes = quad * HEAD_DIM
    groups = width // lanes
    heads = width // HEAD_DIM
    spec = lambda part: pl.BlockSpec((seq, lanes), lambda s, g: (s, part * groups + g))
    return pl.pallas_call(
        attend_kernel,
        grid=(seqs, groups),
        in_specs=[
            spec(0),
            spec(1),
            spec(2),
            pl.BlockSpec((1, 1, seq), lambda s, g: (s, 0, 0)),
            pl.BlockSpec((1, seq, 1), lambda s, g: (s, 0, 0)),
        ],
        out_specs=[
            pl.BlockSpec((seq, lanes), lambda s, g: (s, g)),
            pl.BlockSpec((1, quad, seq, seq), lambda s, g: (s, g, 0, 0)),
        ],
        out_shape=[
            jax.ShapeDtypeStruct((rows, width), bf16),
            jax.ShapeDtypeStruct((seqs, heads, seq, seq), bf16),
        ],
        scratch_shapes=[pltpu.VMEM((seq, seq), f32)],
        cost_estimate=pl.CostEstimate(
            flops=4 * seqs * heads * seq * seq * 256,
            bytes_accessed=20_000_000,
            transcendentals=seqs * heads * seq * seq,
        ),
        name="attend_fwd",
    )(joint, joint, joint, seg_row, seg_col)


def out_kernel(metas, shard_rows, lo, me_ref, att_ref, x_ref, *rest):
    refs = rest[: len(metas)]
    n1_ref, inv_ref, low_ref, vec_ref, w_ref, v_ref, sems = rest[len(metas) :]
    width = x_ref.shape[1]

    @pl.when(pl.program_id(0) == 0)
    def _():
        me = me_ref[0]
        copies = start_loads(metas, refs, me, shard_rows, w_ref, lo, width, sems.at[0])
        copies += start_loads(metas, refs, me, shard_rows, v_ref, lo + width, 128, sems.at[1])
        wait_all(copies)
        eye = (
            lax.broadcasted_iota(jnp.int32, (8, 128), 0)
            == lax.broadcasted_iota(jnp.int32, (8, 128), 1)
        ).astype(bf16)
        vec_ref[...] = dot_nt(eye, v_ref[...])

    h = x_ref[...].astype(f32) + dot_nn(att_ref[...], w_ref[...])
    n, inv = normalize(h)
    n1_ref[...] = n
    inv_ref[...] = jnp.broadcast_to(inv, inv_ref.shape)
    low_ref[...] = (n * vec_ref[0:1] + vec_ref[1:2]).astype(bf16)


def out_forward(me, attended, tokens, pieces, shard_rows):
    rows, width = tokens.shape
    metas = metas_of(pieces)
    block = 512
    by_row = lambda cols: pl.BlockSpec((block, cols), lambda i: (i, 0))
    return pl.pallas_call(
        functools.partial(out_kernel, metas, shard_rows, 3 * width),
        grid=(rows // block,),
        in_specs=[SMEM, by_row(width), by_row(width)] + [ANY] * len(metas),
        out_specs=[by_row(width), by_row(128), by_row(width), whole((8, width))],
        out_shape=[
            jax.ShapeDtypeStruct((rows, width), f32),
            jax.ShapeDtypeStruct((rows, 128), f32),
            jax.ShapeDtypeStruct((rows, width), bf16),
            jax.ShapeDtypeStruct((8, width), f32),
        ],
        scratch_shapes=[
            pltpu.VMEM((width, width), bf16),
            pltpu.VMEM((width, 128), bf16),
            pltpu.SemaphoreType.DMA((2, len(metas))),
        ],
        cost_estimate=pl.CostEstimate(
            flops=2 * rows * width * width, bytes_accessed=12_000_000, transcendentals=rows
        ),
        name="out_norm",
    )(me, attended, tokens, *arrays_of(pieces))


def gate_kernel(metas, shard_rows, me_ref, x_ref, *rest):
    refs, (h_ref, a_ref, b_ref, w_ref, sems) = rest[: len(metas)], rest[len(metas) :]

    @pl.when(pl.program_id(0) == 0)
    def _():
        wait_all(start_loads(metas, refs, me_ref[0], shard_rows, w_ref, 0, w_ref.shape[1], sems))

    hidden = w_ref.shape[1] // 2
    block = h_ref.shape[1]
    sub = 256
    x = x_ref[...]
    for c in range(block // sub):
        lo = pl.multiple_of(pl.program_id(0) * block + c * sub, sub)
        gate = dot_nn(x, w_ref[:, pl.ds(lo, sub)])
        up = dot_nn(x, w_ref[:, pl.ds(pl.multiple_of(hidden + lo, sub), sub)])
        s = 0.5 * jnp.tanh(0.5 * gate) + 0.5
        act = gate * s
        cols = slice(c * sub, (c + 1) * sub)
        h_ref[:, cols] = (act * up).astype(bf16)
        b_ref[:, cols] = act.astype(bf16)
        a_ref[:, cols] = (up * s * (1.0 + gate * (1.0 - s))).astype(bf16)


def gate_forward(me, low, pieces, shard_rows, hidden):
    rows, width = low.shape
    metas = metas_of(pieces)
    block = 768
    spec = pl.BlockSpec((rows, block), lambda j: (0, j))
    shape = jax.ShapeDtypeStruct((rows, hidden), bf16)
    return pl.pallas_call(
        functools.partial(gate_kernel, metas, shard_rows),
        grid=(hidden // block,),
        in_specs=[SMEM, whole(low.shape)] + [ANY] * len(metas),
        out_specs=[spec] * 3,
        out_shape=[shape] * 3,
        scratch_shapes=[
            pltpu.VMEM((width, 2 * hidden), bf16),
            pltpu.SemaphoreType.DMA((len(metas),)),
        ],
        cost_estimate=pl.CostEstimate(
            flops=4 * rows * width * hidden,
            bytes_accessed=30_000_000,
            transcendentals=rows * hidden,
        ),
        name="gate_up",
    )(me, low, *arrays_of(pieces))


def down_kernel(metas, shard_rows, me_ref, h_ref, n1_ref, cot_ref, vec_ref, *rest):
    refs = rest[: len(metas)]
    out_ref, g2_ref, g2low_ref, sums_ref, w_ref, sems = rest[len(metas) :]

    @pl.when(pl.program_id(0) == 0)
    def _():
        wait_all(start_loads(metas, refs, me_ref[0], shard_rows, w_ref, 0, w_ref.shape[1], sems))
        sums_ref[...] = jnp.zeros_like(sums_ref)

    mixed = n1_ref[...] * vec_ref[0:1] + vec_ref[1:2]
    n, inv = normalize(mixed + dot_nn(h_ref[...], w_ref[...]))
    out_ref[...] = (n * vec_ref[2:3] + vec_ref[3:4]).astype(bf16)
    cot = cot_ref[...].astype(f32)
    sums_ref[0:1] += jnp.sum(cot * n, 0, keepdims=True)
    sums_ref[1:2] += jnp.sum(cot, 0, keepdims=True)
    g = norm_back(cot * vec_ref[2:3], n, inv)
    g2_ref[...] = g
    g2low_ref[...] = g.astype(bf16)


def down_forward(me, hidden_low, n1, cot, vec, pieces, shard_rows):
    rows, hidden = hidden_low.shape
    width = n1.shape[1]
    metas = metas_of(pieces)
    block = 256
    by_row = lambda cols: pl.BlockSpec((block, cols), lambda i: (i, 0))
    return pl.pallas_call(
        functools.partial(down_kernel, metas, shard_rows),
        grid=(rows // block,),
        in_specs=[SMEM, by_row(hidden), by_row(width), by_row(width), whole(vec.shape)]
        + [ANY] * len(metas),
        out_specs=[by_row(width), by_row(width), by_row(width), whole((8, width))],
        out_shape=[
            jax.ShapeDtypeStruct((rows, width), bf16),
            jax.ShapeDtypeStruct((rows, width), f32),
            jax.ShapeDtypeStruct((rows, width), bf16),
            jax.ShapeDtypeStruct((8, width), f32),
        ],
        scratch_shapes=[
            pltpu.VMEM((hidden, width), bf16),
            pltpu.SemaphoreType.DMA((len(metas),)),
        ],
        cost_estimate=pl.CostEstimate(
            flops=2 * rows * width * hidden, bytes_accessed=20_000_000, transcendentals=rows
        ),
        name="down_norm",
    )(me, hidden_low, n1, cot, vec, *arrays_of(pieces))


def down_grad_kernel(me_ref, h_ref, g_ref, keep_ref, send_ref, acc_ref):
    rows = keep_ref.shape[1]
    core = me_ref[0] & 1
    acc_ref[...] = dot_tn(h_ref[...], g_ref[...])
    keep_ref[0] = acc_ref[pl.ds(pl.multiple_of(core * rows, 8), rows), :].astype(bf16)
    send_ref[0] = acc_ref[pl.ds(pl.multiple_of((1 - core) * rows, 8), rows), :].astype(bf16)


def down_grad(me, hidden_low, g2low, chips):
    rows, hidden = hidden_low.shape
    width = g2low.shape[1]
    per_chip = hidden // chips
    shape = jax.ShapeDtypeStruct((chips, per_chip // 2, width), bf16)
    spec = pl.BlockSpec((1, per_chip // 2, width), lambda q, me: (q, 0, 0))
    return pl.pallas_call(
        down_grad_kernel,
        grid_spec=pltpu.PrefetchScalarGridSpec(
            num_scalar_prefetch=1,
            grid=(chips,),
            in_specs=[
                pl.BlockSpec((rows, per_chip), lambda q, me: (0, (me[0] // 2) ^ q)),
                pl.BlockSpec((rows, width), lambda q, me: (0, 0)),
            ],
            out_specs=[spec, spec],
            scratch_shapes=[pltpu.VMEM((per_chip, width), f32)],
        ),
        out_shape=[shape, shape],
        cost_estimate=pl.CostEstimate(
            flops=2 * rows * width * hidden, bytes_accessed=13_000_000, transcendentals=0
        ),
        name="down_grad",
    )(me, hidden_low, g2low)


def spread(me, acc_ref, keep_ref, send_ref, cols):
    rows = keep_ref.shape[1]
    chip, core = me // 2, me & 1
    for q in range(keep_ref.shape[0]):
        base = (chip ^ q) * 2
        keep_ref[q, :, cols] = acc_ref[
            pl.ds(pl.multiple_of((base + core) * rows, 8), rows), :
        ].astype(bf16)
        send_ref[q, :, cols] = acc_ref[
            pl.ds(pl.multiple_of((base + 1 - core) * rows, 8), rows), :
        ].astype(bf16)


def hidden_grad_kernel(metas, shard_rows, me_ref, g_ref, a_ref, b_ref, *rest):
    refs, (gg_ref, gu_ref, w_ref, sems) = rest[: len(metas)], rest[len(metas) :]

    @pl.when(pl.program_id(0) == 0)
    def _():
        wait_all(start_loads(metas, refs, me_ref[0], shard_rows, w_ref, 0, w_ref.shape[1], sems))

    block = gg_ref.shape[1]
    sub = 256
    for c in range(block // sub):
        lo = pl.multiple_of(pl.program_id(0) * block + c * sub, sub)
        gh = dot_nt(g_ref[...], w_ref[pl.ds(lo, sub), :])
        cols = slice(c * sub, (c + 1) * sub)
        gg_ref[:, cols] = (gh * a_ref[:, cols].astype(f32)).astype(bf16)
        gu_ref[:, cols] = (gh * b_ref[:, cols].astype(f32)).astype(bf16)


def hidden_grad(me, g2low, a, b, pieces, shard_rows):
    rows, hidden = a.shape
    width = g2low.shape[1]
    metas = metas_of(pieces)
    block = 768
    spec = pl.BlockSpec((rows, block), lambda j: (0, j))
    shape = jax.ShapeDtypeStruct((rows, hidden), bf16)
    return pl.pallas_call(
        functools.partial(hidden_grad_kernel, metas, shard_rows),
        grid=(hidden // block,),
        in_specs=[SMEM, whole(g2low.shape), spec, spec] + [ANY] * len(metas),
        out_specs=[spec, spec],
        out_shape=[shape, shape],
        scratch_shapes=[
            pltpu.VMEM((hidden, width), bf16),
            pltpu.SemaphoreType.DMA((len(metas),)),
        ],
        cost_estimate=pl.CostEstimate(
            flops=2 * rows * width * hidden, bytes_accessed=32_000_000, transcendentals=0
        ),
        name="hidden_grad",
    )(me, g2low, a, b, *arrays_of(pieces))


def weight_grad_kernel(me_ref, x_ref, g_ref, keep_ref, send_ref, acc_ref):
    acc_ref[...] = dot_tn(x_ref[...], g_ref[...])
    spread(me_ref[0], acc_ref, keep_ref, send_ref, slice(None))


def weight_grad(me, x, g, count, name, block=768):
    rows, width = x.shape
    cols = g.shape[1]
    chips, shard_rows = count // 2, width // count
    shape = jax.ShapeDtypeStruct((chips, shard_rows, cols), bf16)
    spec = pl.BlockSpec((chips, shard_rows, block), lambda j: (0, 0, j))
    return pl.pallas_call(
        weight_grad_kernel,
        grid=(cols // block,),
        in_specs=[SMEM, whole(x.shape), pl.BlockSpec((rows, block), lambda j: (0, j))],
        out_specs=[spec, spec],
        out_shape=[shape, shape],
        scratch_shapes=[pltpu.VMEM((width, block), f32)],
        cost_estimate=pl.CostEstimate(
            flops=2 * rows * width * cols, bytes_accessed=13_000_000, transcendentals=0
        ),
        name=name,
    )(me, x, g)


def mixed_grad_kernel(
    metas, metas_out, shard_rows, out_lo,
    me_ref, gg_ref, gu_ref, g2_ref, n1_ref, inv_ref, vec_ref, *rest,
):
    refs, rest = rest[: len(metas)], rest[len(metas) :]
    refs_out, rest = rest[: len(metas_out)], rest[len(metas_out) :]
    g1_ref, g1low_ref, gatt_ref, sums_ref, w_ref, wo_ref, sems, sems_out = rest
    width = g1_ref.shape[1]
    hidden = w_ref.shape[1] // 2

    @pl.when(pl.program_id(0) == 0)
    def _():
        me = me_ref[0]
        copies = start_loads(metas, refs, me, shard_rows, w_ref, 0, 2 * hidden, sems)
        copies += start_loads(metas_out, refs_out, me, shard_rows, wo_ref, out_lo, width, sems_out)
        wait_all(copies)
        sums_ref[...] = jnp.zeros_like(sums_ref)

    gm = (
        g2_ref[...]
        + dot_nt(gg_ref[...], w_ref[:, :hidden])
        + dot_nt(gu_ref[...], w_ref[:, hidden:])
    )
    n = n1_ref[...]
    sums_ref[0:1] += jnp.sum(gm * n, 0, keepdims=True)
    sums_ref[1:2] += jnp.sum(gm, 0, keepdims=True)
    g = norm_back(gm * vec_ref[0:1], n, inv_ref[:, 0:1])
    g1_ref[...] = g
    low = g.astype(bf16)
    g1low_ref[...] = low
    gatt_ref[...] = dot_nt(low, wo_ref[...]).astype(bf16)


def mixed_grad(me, gg, gu, g2, n1, inv1, vec, pieces, pieces_out, shard_rows):
    rows, hidden = gg.shape
    width = g2.shape[1]
    metas, metas_out = metas_of(pieces), metas_of(pieces_out)
    block = 256
    by_row = lambda cols: pl.BlockSpec((block, cols), lambda i: (i, 0))
    return pl.pallas_call(
        functools.partial(mixed_grad_kernel, metas, metas_out, shard_rows, 3 * width),
        grid=(rows // block,),
        in_specs=[
            SMEM, by_row(hidden), by_row(hidden), by_row(width), by_row(width), by_row(128),
            whole(vec.shape),
        ]
        + [ANY] * (len(metas) + len(metas_out)),
        out_specs=[by_row(width), by_row(width), by_row(width), whole((8, width))],
        out_shape=[
            jax.ShapeDtypeStruct((rows, width), f32),
            jax.ShapeDtypeStruct((rows, width), bf16),
            jax.ShapeDtypeStruct((rows, width), bf16),
            jax.ShapeDtypeStruct((8, width), f32),
        ],
        scratch_shapes=[
            pltpu.VMEM((width, 2 * hidden), bf16),
            pltpu.VMEM((width, width), bf16),
            pltpu.SemaphoreType.DMA((len(metas),)),
            pltpu.SemaphoreType.DMA((len(metas_out),)),
        ],
        cost_estimate=pl.CostEstimate(
            flops=4 * rows * width * hidden + 2 * rows * width * width,
            bytes_accessed=36_000_000,
            transcendentals=0,
        ),
        name="mixed_grad",
    )(me, gg, gu, g2, n1, inv1, vec, *arrays_of(pieces), *arrays_of(pieces_out))


def up_out_grad_kernel(me_ref, x_ref, g_ref, att_ref, g1_ref, s2_ref, s1_ref, keep_ref, send_ref, acc_ref):
    me = me_ref[0]
    width = x_ref.shape[1]
    cols = g_ref.shape[1]
    for j in range(cols // width):
        acc_ref[...] = dot_tn(x_ref[...], g_ref[:, j * width : (j + 1) * width])
        spread(me, acc_ref, keep_ref, send_ref, slice(j * width, (j + 1) * width))
    acc_ref[...] = dot_tn(att_ref[...], g1_ref[...])
    spread(me, acc_ref, keep_ref, send_ref, slice(cols, cols + width))
    row = lax.broadcasted_iota(jnp.int32, (8, width), 0)
    rows = jnp.where(row < 2, s2_ref[...], pltpu.roll(s1_ref[...], 2, 0)).astype(bf16)
    eye = (
        lax.broadcasted_iota(jnp.int32, (8, 128), 0) == lax.broadcasted_iota(jnp.int32, (8, 128), 1)
    ).astype(bf16)
    acc_ref[:, :128] = dot_tn(rows, eye)
    spread(me, acc_ref.at[:, :128], keep_ref, send_ref, slice(cols + width, cols + width + 128))


def up_out_grad(me, low, gu, attended, g1low, sums2, sums1, count):
    rows, width = low.shape
    cols = gu.shape[1]
    chips, shard_rows = count // 2, width // count
    total = cols + width + 128
    shape = jax.ShapeDtypeStruct((chips, shard_rows, total), bf16)
    vmem = pl.BlockSpec(memory_space=pltpu.VMEM)
    return pl.pallas_call(
        up_out_grad_kernel,
        in_specs=[SMEM] + [vmem] * 6,
        out_specs=[vmem, vmem],
        out_shape=[shape, shape],
        scratch_shapes=[pltpu.VMEM((width, width), f32)],
        cost_estimate=pl.CostEstimate(
            flops=2 * rows * width * (cols + width), bytes_accessed=16_000_000, transcendentals=0
        ),
        name="up_out_grad",
    )(me, low, gu, attended, g1low, sums2, sums1)


def attend_back_kernel(q_ref, k_ref, v_ref, o_ref, g_ref, p_ref, cos_ref, sin_ref, dq_ref, dk_ref, dv_ref):
    heads = p_ref.shape[1]
    lane = lax.broadcasted_iota(jnp.int32, (1, 128), 1)
    first = half_mask((cos_ref.shape[0], 128))
    cos, sin = cos_ref[...], sin_ref[...]

    def unrotate(g):
        t = g * sin
        return g * cos + jnp.where(first, pltpu.roll(t, 96, 1), -pltpu.roll(t, 32, 1))

    for pair in range(heads // 2):
        cols = slice(pair * 128, (pair + 1) * 128)
        q, k, v, g = q_ref[:, cols], k_ref[:, cols], v_ref[:, cols], g_ref[:, cols]
        go = g.astype(f32) * o_ref[:, cols].astype(f32)
        dq = dk = dv = None
        for side in range(2):
            mine = (lane // HEAD_DIM) == side
            keep = mine.astype(bf16)
            p = p_ref[0, pair * 2 + side]
            row = jnp.sum(jnp.where(mine, go, 0.0), -1, keepdims=True)
            gp = dot_nt(g, v * keep)
            gs = (p.astype(f32) * (gp - row)).astype(bf16)
            parts = (dot_nn(gs, k * keep), dot_tn(gs, q * keep), dot_tn(p, g * keep))
            if dq is None:
                dq, dk, dv = parts
            else:
                dq, dk, dv = dq + parts[0], dk + parts[1], dv + parts[2]
        dq_ref[:, cols] = unrotate(dq * 0.125).astype(bf16)
        dk_ref[:, cols] = unrotate(dk).astype(bf16)
        dv_ref[:, cols] = dv.astype(bf16)


def attend_backward(joint, attended, gatt, probs, cos, sin):
    rows, width = attended.shape
    seqs, heads, seq, _ = probs.shape
    quad = 4
    lanes = quad * HEAD_DIM
    groups = width // lanes
    spec = lambda part: pl.BlockSpec((seq, lanes), lambda s, g: (s, part * groups + g))
    shape = jax.ShapeDtypeStruct((rows, width), bf16)
    return pl.pallas_call(
        attend_back_kernel,
        grid=(seqs, groups),
        in_specs=[
            spec(0), spec(1), spec(2), spec(0), spec(0),
            pl.BlockSpec((1, quad, seq, seq), lambda s, g: (s, g, 0, 0)),
            pl.BlockSpec(cos.shape, lambda s, g: (0, 0)),
            pl.BlockSpec(sin.shape, lambda s, g: (0, 0)),
        ],
        out_specs=[spec(0)] * 3,
        out_shape=[shape] * 3,
        cost_estimate=pl.CostEstimate(
            flops=8 * seqs * heads * seq * seq * 256, bytes_accessed=25_000_000, transcendentals=0
        ),
        name="attend_bwd",
    )(joint, joint, joint, attended, gatt, probs, cos, sin)


def qkv_grad_kernel(me_ref, x_ref, dq_ref, dk_ref, dv_ref, keep_ref, send_ref, acc_ref):
    width = x_ref.shape[1]
    for j, ref in enumerate((dq_ref, dk_ref, dv_ref)):
        acc_ref[...] = dot_tn(x_ref[...], ref[...])
        spread(me_ref[0], acc_ref, keep_ref, send_ref, slice(j * width, (j + 1) * width))


def qkv_grad(me, tokens, dq, dk, dv, count):
    rows, width = tokens.shape
    chips, shard_rows = count // 2, width // count
    shape = jax.ShapeDtypeStruct((chips, shard_rows, 3 * width), bf16)
    vmem = pl.BlockSpec(memory_space=pltpu.VMEM)
    return pl.pallas_call(
        qkv_grad_kernel,
        in_specs=[SMEM] + [vmem] * 4,
        out_specs=[vmem, vmem],
        out_shape=[shape, shape],
        scratch_shapes=[pltpu.VMEM((width, width), f32)],
        cost_estimate=pl.CostEstimate(
            flops=6 * rows * width * width, bytes_accessed=10_000_000, transcendentals=0
        ),
        name="qkv_grad",
    )(me, tokens, dq, dk, dv)


def input_grad_kernel(metas, shard_rows, me_ref, g1_ref, dq_ref, dk_ref, dv_ref, *rest):
    refs, (out_ref, w_ref, sems) = rest[: len(metas)], rest[len(metas) :]
    width = out_ref.shape[1]

    @pl.when(pl.program_id(0) == 0)
    def _():
        wait_all(start_loads(metas, refs, me_ref[0], shard_rows, w_ref, 0, 3 * width, sems))

    total = g1_ref[...]
    for j, ref in enumerate((dq_ref, dk_ref, dv_ref)):
        total += dot_nt(ref[...], w_ref[:, j * width : (j + 1) * width])
    out_ref[...] = total.astype(bf16)


def input_grad(me, g1, dq, dk, dv, pieces, shard_rows):
    rows, width = g1.shape
    metas = metas_of(pieces)
    block = 512
    by_row = pl.BlockSpec((block, width), lambda i: (i, 0))
    return pl.pallas_call(
        functools.partial(input_grad_kernel, metas, shard_rows),
        grid=(rows // block,),
        in_specs=[SMEM] + [by_row] * 4 + [ANY] * len(metas),
        out_specs=by_row,
        out_shape=jax.ShapeDtypeStruct((rows, width), bf16),
        scratch_shapes=[
            pltpu.VMEM((width, 3 * width), bf16),
            pltpu.SemaphoreType.DMA((len(metas),)),
        ],
        cost_estimate=pl.CostEstimate(
            flops=6 * rows * width * width, bytes_accessed=14_000_000, transcendentals=0
        ),
        name="input_grad",
    )(me, g1, dq, dk, dv, *arrays_of(pieces))


def rope_tables(seq_len):
    places = jnp.arange(seq_len, dtype=jnp.int32).astype(f32)
    frequency = rope_base ** (-jnp.arange(0, HEAD_DIM, 2, dtype=f32) / HEAD_DIM)
    angles = places[:, None] * frequency[None, :]
    return (jnp.tile(jnp.cos(angles), (1, 4)), jnp.tile(jnp.sin(angles), (1, 4)))


def shards(
    tokens, segment_ids, qkv_weight, out_weight, gate_weight, up_weight, down_weight,
    norm1_gain, norm1_bias, norm2_gain, norm2_bias, out_grad,
):
    count = lax.axis_size("shard")
    me = lax.axis_index("shard").astype(jnp.int32).reshape(1)
    batches, seq, width = tokens.shape
    shard_rows = qkv_weight.shape[0]
    hidden = gate_weight.shape[1]
    rows = batches * seq

    vectors = jnp.stack([norm1_gain, norm1_bias, norm2_gain, norm2_bias], 1)
    vectors = jnp.pad(vectors, ((0, 0), (0, 124)))
    pieces_a = gather_pieces(jnp.concatenate([qkv_weight, out_weight, vectors], 1))
    pieces_b = gather_pieces(jnp.concatenate([gate_weight, up_weight], 1))
    pieces_c = gather_pieces(down_weight)

    x = tokens.reshape(rows, width)
    cos, sin = rope_tables(seq)
    seg = segment_ids.reshape(batches, 1, seq)
    seg_col = segment_ids.reshape(batches, seq, 1)

    joint = qkv_forward(me, x, cos, sin, pieces_a, shard_rows)
    attended, probs = attend_forward(joint, seg, seg_col, width)
    n1, inv1, low, vec = out_forward(me, attended, x, pieces_a, shard_rows)
    hidden_low, back_gate, back_up = gate_forward(me, low, pieces_b, shard_rows, hidden)
    output, g2, g2low, sums2 = down_forward(
        me, hidden_low, n1, out_grad.reshape(rows, width), vec, pieces_c, down_weight.shape[0]
    )

    down_part = reduce_own(*down_grad(me, hidden_low, g2low, count // 2))
    gg, gu = hidden_grad(me, g2low, back_gate, back_up, pieces_c, down_weight.shape[0])
    gate_part = reduce_own(*weight_grad(me, low, gg, count, "gate_grad"))
    g1, g1low, gatt, sums1 = mixed_grad(
        me, gg, gu, g2, n1, inv1, vec, pieces_b, pieces_a, shard_rows
    )
    up_part = reduce_own(*up_out_grad(me, low, gu, attended, g1low, sums2, sums1, count))
    dq, dk, dv = attend_backward(joint, attended, gatt, probs, cos, sin)
    qkv_part = reduce_own(*qkv_grad(me, x, dq, dk, dv, count))
    in_grad = input_grad(me, g1, dq, dk, dv, pieces_a, shard_rows)

    total = lambda part: lax.psum(part, "rep").astype(f32)
    down_sum, gate_sum, up_sum, qkv_sum = map(total, (down_part, gate_part, up_part, qkv_part))
    vec_sum = up_sum[:, hidden + width :]
    return (
        output.reshape(tokens.shape),
        in_grad.reshape(tokens.shape),
        qkv_sum,
        up_sum[:, hidden : hidden + width],
        gate_sum,
        up_sum[:, :hidden],
        down_sum,
        vec_sum[:, 2],
        vec_sum[:, 3],
        vec_sum[:, 0],
        vec_sum[:, 1],
    )


def solution(mesh):
    rows3 = P(None, ("shard", "rep"), None)
    rows2 = P("shard", None)
    rows1 = P("shard")
    in_specs = (rows3, P(None, ("shard", "rep"))) + (rows2,) * 5 + (rows1,) * 4 + (rows3,)
    out_specs = (rows3, rows3) + (rows2,) * 5 + (rows1,) * 4
    return jax.shard_map(shards, mesh=mesh, in_specs=in_specs, out_specs=out_specs, check_vma=False)
```

```python
import functools

import jax
import jax.numpy as jnp
from jax import lax
from jax.experimental import pallas as pl
from jax.experimental.pallas import tpu as pltpu
from jax.sharding import PartitionSpec as P

HEAD_DIM = 64
norm_eps = 1e-12
rope_base = 1000.0
masked_score = -1e30
f32 = jnp.float32
bf16 = jnp.bfloat16
ANY = pl.BlockSpec(memory_space=pl.ANY)
SMEM = pl.BlockSpec(memory_space=pltpu.SMEM)


def dot_nn(a, b):
    return lax.dot_general(a, b, (((1,), (0,)), ((), ())), preferred_element_type=f32)


def dot_nt(a, b):
    return lax.dot_general(a, b, (((1,), (1,)), ((), ())), preferred_element_type=f32)


def dot_tn(a, b):
    return lax.dot_general(a, b, (((0,), (0,)), ((), ())), preferred_element_type=f32)


def whole(shape):
    return pl.BlockSpec(shape, lambda *_: (0,) * len(shape))


def tie(value, *deps):
    return lax.optimization_barrier((value, deps))[0]


def xor_permute(x, bit):
    count = lax.axis_size("shard")
    return lax.ppermute(x, "shard", [(i, i ^ bit) for i in range(count)])


def gather_first(own):
    return xor_permute(own, 2), xor_permute(own, 4)


def gather_second(from_x, from_y):
    half = from_x.shape[0] // 2
    return xor_permute(from_y[:half], 2), xor_permute(from_x[half:], 4)


def with_partner(pieces):
    return pieces + [(r | 1, lo, xor_permute(p, 1)) for r, lo, p in pieces]


def pieces_of(own, first, second):
    half = own.shape[0] // 2
    return [(0, 0, own), (2, 0, first[0]), (4, 0, first[1]), (6, 0, second[0]), (6, half, second[1])]


def gather_pieces(own):
    count = lax.axis_size("shard")
    pieces = [(0, 0, own)]
    bit = 2
    while bit < count:
        pieces += [(r | bit, lo, xor_permute(p, bit)) for r, lo, p in pieces]
        bit *= 2
    return with_partner(pieces)


def add_parts(parts):
    return functools.reduce(jnp.add, [p.astype(f32) for p in parts]).astype(bf16)


def rep_permute(x, pairs):
    return lax.ppermute(x, "rep", pairs)


class Flow:
    def __init__(self, keep, send):
        self.held = keep
        self.pending = xor_permute(send, 1)
        self.stage = 0
        self.line = lax.axis_size("rep") == 4

    def step(self, *deps):
        got = tie(self.pending, *deps) if deps else self.pending
        if self.stage == 0:
            self.ready = self.held + got
            chips = self.ready.shape[0]
            self.pending = [xor_permute(self.ready[q], 2 * q) for q in range(1, chips)]
        elif self.stage == 1:
            self.ready = add_parts([self.ready[0]] + got)
            if self.line:
                self.pending = rep_permute(self.ready, [(0, 1), (3, 2)])
            else:
                self.pending = lax.psum(self.ready, "rep")
        elif not self.line:
            self.ready = got
        elif self.stage == 2:
            self.ready = add_parts([self.ready, got])
            self.pending = rep_permute(self.ready, [(1, 2), (2, 1)])
        elif self.stage == 3:
            self.ready = add_parts([self.ready, got])
            self.pending = rep_permute(self.ready, [(1, 0), (2, 3)])
        else:
            place = lax.axis_index("rep")
            inner = (place == 1) | (place == 2)
            self.ready = jnp.where(inner, self.ready, got).astype(f32)
        self.stage += 1
        return self.ready

    def finish(self):
        while self.stage < 5:
            self.step()
        return self.ready.astype(f32)


def advance(dep, *flows):
    return tuple(flow.step(dep) for flow in flows)


def piece_copies(metas, refs, me, shard_rows, dst, src_lo, dst_lo, cols, sems):
    copies = []
    for i, ((rel, first, rows), ref) in enumerate(zip(metas, refs)):
        at = pl.multiple_of((me ^ rel) * shard_rows + first, 8)
        copies.append(
            pltpu.make_async_copy(
                ref.at[:, pl.ds(src_lo, cols)],
                dst.at[pl.ds(at, rows), pl.ds(dst_lo, cols)],
                sems.at[i],
            )
        )
    return copies


def start_all(copies):
    for copy in copies:
        copy.start()


def wait_all(copies):
    for copy in copies:
        copy.wait()


def metas_of(pieces):
    return tuple((rel, first, p.shape[0]) for rel, first, p in pieces)


def arrays_of(pieces):
    return [p for _, _, p in pieces]


def half_mask(shape):
    lane = lax.broadcasted_iota(jnp.int32, shape, len(shape) - 1)
    return (lane % HEAD_DIM) < HEAD_DIM // 2


def unit_rows():
    shape = (8, 128)
    return (
        lax.broadcasted_iota(jnp.int32, shape, 0) == lax.broadcasted_iota(jnp.int32, shape, 1)
    ).astype(bf16)


def normalize(h):
    centre = h - jnp.mean(h, -1, keepdims=True)
    inv = lax.rsqrt(jnp.mean(centre * centre, -1, keepdims=True) + norm_eps)
    return centre * inv, inv


def norm_back(e, n, inv):
    return inv * (e - jnp.mean(e, -1, keepdims=True) - n * jnp.mean(e * n, -1, keepdims=True))


def spread(me, acc_ref, keep_ref, send_ref, cols):
    rows = keep_ref.shape[1]
    chip, core = me // 2, me & 1
    for q in range(keep_ref.shape[0]):
        base = (chip ^ q) * 2
        keep_ref[q, :, cols] = acc_ref[
            pl.ds(pl.multiple_of((base + core) * rows, 8), rows), :
        ].astype(bf16)
        send_ref[q, :, cols] = acc_ref[
            pl.ds(pl.multiple_of((base + 1 - core) * rows, 8), rows), :
        ].astype(bf16)


def cost(flops, read, transcendentals=0):
    return pl.CostEstimate(flops=flops, bytes_accessed=read, transcendentals=transcendentals)


def front_kernel(metas, shard_rows, me_ref, x_ref, cos_ref, sin_ref, row_ref, col_ref, *rest):
    refs, rest = rest[: len(metas)], rest[len(metas) :]
    q_ref, k_ref, v_ref, att_ref, p_ref, n1_ref, inv_ref, low_ref, vec_ref, qkv_out, out_out = rest[:11]
    w_ref, wo_ref, wv_ref, mix_ref, bias_ref, sems, back_sems = rest[11:]
    s, g = pl.program_id(0), pl.program_id(1)
    last_group = pl.num_programs(1) - 1
    width = x_ref.shape[1]
    lanes = q_ref.shape[1]
    me = me_ref[0]
    qkv_copies = piece_copies(metas, refs, me, shard_rows, w_ref, 0, 0, 3 * width, sems.at[0])
    out_copies = piece_copies(metas, refs, me, shard_rows, wo_ref, 3 * width, 0, width, sems.at[1])
    vec_copies = piece_copies(metas, refs, me, shard_rows, wv_ref, 4 * width, 0, 128, sems.at[2])
    back = [
        pltpu.make_async_copy(w_ref, qkv_out, back_sems.at[0]),
        pltpu.make_async_copy(wo_ref, out_out, back_sems.at[1]),
    ]

    @pl.when((s == 0) & (g == 0))
    def _():
        start_all(qkv_copies)
        start_all(out_copies)
        start_all(vec_copies)
        wait_all(qkv_copies)
        back[0].start()

    @pl.when(g == 0)
    def _():
        bias_ref[...] = jnp.where(row_ref[0] == col_ref[0], 0.0, masked_score).astype(f32)

    x = x_ref[...]
    first = half_mask((x.shape[0], 128))
    cos = cos_ref[...]
    sin = jnp.where(first, -sin_ref[...], sin_ref[...])

    def turn(u):
        turned = jnp.where(first, pltpu.roll(u, 96, 1), pltpu.roll(u, 32, 1))
        return u * cos + turned * sin

    for part, ref in enumerate((q_ref, k_ref, v_ref)):
        lo = pl.multiple_of(part * width + g * lanes, 128)
        y = dot_nn(x, w_ref[:, pl.ds(lo, lanes)])
        for b in range(lanes // 128):
            cols = slice(b * 128, (b + 1) * 128)
            u = y[:, cols]
            if part == 0:
                u = turn(u) * 0.125
            elif part == 1:
                u = turn(u)
            ref[:, cols] = u.astype(bf16)

    lane = lax.broadcasted_iota(jnp.int32, (1, 128), 1)
    for pair in range(lanes // 128):
        cols = slice(pair * 128, (pair + 1) * 128)
        q, k, v = q_ref[:, cols], k_ref[:, cols], v_ref[:, cols]
        acc = None
        for side in range(2):
            mine = ((lane // HEAD_DIM) == side).astype(bf16)
            score = dot_nt(q, k * mine) + bias_ref[...]
            e = jnp.exp(score - jnp.max(score, -1, keepdims=True))
            inv = 1.0 / jnp.sum(e, -1, keepdims=True)
            p = (e * inv).astype(bf16)
            p_ref[0, pair * 2 + side] = p
            part = dot_nn(p, v * mine)
            acc = part if acc is None else acc + part
        low = acc.astype(bf16)
        att_ref[:, cols] = low
        mix_ref[:, pl.ds(pl.multiple_of(g * lanes + pair * 128, 128), 128)] = low

    @pl.when((s == 0) & (g == last_group))
    def _():
        wait_all(out_copies)
        wait_all(vec_copies)
        back[1].start()
        vec_ref[...] = dot_nt(unit_rows(), wv_ref[...])

    @pl.when(g == last_group)
    def _():
        n, inv = normalize(x.astype(f32) + dot_nn(mix_ref[...], wo_ref[...]))
        n1_ref[...] = n
        inv_ref[...] = jnp.broadcast_to(inv, inv_ref.shape)
        low_ref[...] = (n * vec_ref[0:1] + vec_ref[1:2]).astype(bf16)

    @pl.when((s == pl.num_programs(0) - 1) & (g == last_group))
    def _():
        wait_all(back)


def front(me, x, cos, sin, seg_row, seg_col, pieces, shard_rows):
    rows, width = x.shape
    metas = metas_of(pieces)
    seqs, _, seq = seg_row.shape
    heads = width // HEAD_DIM
    quad = 4
    lanes = quad * HEAD_DIM
    group = pl.BlockSpec((seq, lanes), lambda s, g: (s, g))
    by_seq = lambda cols: pl.BlockSpec((seq, cols), lambda s, g: (s, 0))
    wide = jax.ShapeDtypeStruct((rows, width), bf16)
    return pl.pallas_call(
        functools.partial(front_kernel, metas, shard_rows),
        grid=(seqs, width // lanes),
        in_specs=[
            SMEM, by_seq(width), whole(cos.shape), whole(sin.shape),
            pl.BlockSpec((1, 1, seq), lambda s, g: (s, 0, 0)),
            pl.BlockSpec((1, seq, 1), lambda s, g: (s, 0, 0)),
        ]
        + [ANY] * len(metas),
        out_specs=[group] * 4
        + [
            pl.BlockSpec((1, quad, seq, seq), lambda s, g: (s, g, 0, 0)),
            by_seq(width), by_seq(128), by_seq(width), whole((8, width)), ANY, ANY,
        ],
        out_shape=[wide] * 4
        + [
            jax.ShapeDtypeStruct((seqs, heads, seq, seq), bf16),
            jax.ShapeDtypeStruct((rows, width), f32),
            jax.ShapeDtypeStruct((rows, 128), f32),
            wide,
            jax.ShapeDtypeStruct((8, width), f32),
            jax.ShapeDtypeStruct((width, 3 * width), bf16),
            jax.ShapeDtypeStruct((width, width), bf16),
        ],
        scratch_shapes=[
            pltpu.VMEM((width, 3 * width), bf16),
            pltpu.VMEM((width, width), bf16),
            pltpu.VMEM((width, 128), bf16),
            pltpu.VMEM((seq, width), bf16),
            pltpu.VMEM((seq, seq), f32),
            pltpu.SemaphoreType.DMA((3, len(metas))),
            pltpu.SemaphoreType.DMA((2,)),
        ],
        cost_estimate=cost(
            8 * rows * width * width + 4 * seqs * heads * seq * seq * 256,
            40_000_000,
            seqs * heads * seq * seq,
        ),
        name="qkv_attend_out",
    )(me, x, cos, sin, seg_row, seg_col, *arrays_of(pieces))


def gate_kernel(metas, shard_rows, me_ref, x_ref, *rest):
    refs = rest[: len(metas)]
    h_ref, a_ref, b_ref, w_out, w_ref, sems, back_sem = rest[len(metas) :]
    hidden = w_ref.shape[1] // 2
    block = h_ref.shape[1]
    j = pl.program_id(0)
    me = me_ref[0]
    copies = []
    for c, (lo, cols) in enumerate(((0, block), (block, hidden - block))):
        copies.append(
            piece_copies(metas, refs, me, shard_rows, w_ref, lo, lo, cols, sems.at[2 * c])
            + piece_copies(
                metas, refs, me, shard_rows, w_ref, hidden + lo, hidden + lo, cols, sems.at[2 * c + 1]
            )
        )
    back = pltpu.make_async_copy(w_ref, w_out, back_sem)

    @pl.when(j == 0)
    def _():
        start_all(copies[0])
        start_all(copies[1])
        wait_all(copies[0])

    @pl.when(j == 1)
    def _():
        wait_all(copies[1])
        back.start()

    sub = 256
    x = x_ref[...]
    for c in range(block // sub):
        lo = pl.multiple_of(j * block + c * sub, sub)
        gate = dot_nn(x, w_ref[:, pl.ds(lo, sub)])
        up = dot_nn(x, w_ref[:, pl.ds(pl.multiple_of(hidden + lo, sub), sub)])
        s = 0.5 * jnp.tanh(0.5 * gate) + 0.5
        act = gate * s
        cols = slice(c * sub, (c + 1) * sub)
        h_ref[:, cols] = (act * up).astype(bf16)
        b_ref[:, cols] = act.astype(bf16)
        a_ref[:, cols] = (up * (s + act * (1.0 - s))).astype(bf16)

    @pl.when(j == pl.num_programs(0) - 1)
    def _():
        back.wait()


def gate_forward(me, low, pieces, shard_rows, hidden):
    rows, width = low.shape
    metas = metas_of(pieces)
    block = 768
    spec = pl.BlockSpec((rows, block), lambda j: (0, j))
    shape = jax.ShapeDtypeStruct((rows, hidden), bf16)
    return pl.pallas_call(
        functools.partial(gate_kernel, metas, shard_rows),
        grid=(hidden // block,),
        in_specs=[SMEM, whole(low.shape)] + [ANY] * len(metas),
        out_specs=[spec] * 3 + [ANY],
        out_shape=[shape] * 3 + [jax.ShapeDtypeStruct((width, 2 * hidden), bf16)],
        scratch_shapes=[
            pltpu.VMEM((width, 2 * hidden), bf16),
            pltpu.SemaphoreType.DMA((4, len(metas))),
            pltpu.SemaphoreType.DMA,
        ],
        cost_estimate=cost(4 * rows * width * hidden, 40_000_000, rows * hidden),
        name="gate_up",
    )(me, low, *arrays_of(pieces))


def down_kernel(metas, shard_rows, blocks, me_ref, h_any, n1_ref, cot_ref, vec_ref, *rest):
    refs = rest[: len(metas)]
    out_ref, g2_ref, g2low_ref, sums_ref, keep_ref, send_ref, w_out = rest[len(metas) : len(metas) + 7]
    w_ref, h_ref, acc_ref, sems, row_sems, back_sem = rest[len(metas) + 7 :]
    i = pl.program_id(0)
    me = me_ref[0]
    block = n1_ref.shape[0]
    w_copies = piece_copies(metas, refs, me, shard_rows, w_ref, 0, 0, w_ref.shape[1], sems)
    h_copies = [
        pltpu.make_async_copy(
            h_any.at[pl.ds(b * block, block), :], h_ref.at[pl.ds(b * block, block), :], row_sems.at[b]
        )
        for b in range(blocks)
    ]
    back = pltpu.make_async_copy(w_ref, w_out, back_sem)

    @pl.when(i == 0)
    def _():
        start_all(w_copies)
        start_all(h_copies)
        sums_ref[...] = jnp.zeros_like(sums_ref)
        wait_all(w_copies)
        back.start()

    for b in range(blocks):

        @pl.when(i == b)
        def _():
            h_copies[b].wait()

    @pl.when(i < blocks)
    def _():
        at = pl.ds(pl.multiple_of(i * block, block), block)
        mixed = n1_ref[...] * vec_ref[0:1] + vec_ref[1:2]
        n, inv = normalize(mixed + dot_nn(h_ref[at, :], w_ref[...]))
        out_ref[...] = (n * vec_ref[2:3] + vec_ref[3:4]).astype(bf16)
        cot = cot_ref[...].astype(f32)
        sums_ref[0:1] += jnp.sum(cot * n, 0, keepdims=True)
        sums_ref[1:2] += jnp.sum(cot, 0, keepdims=True)
        g = norm_back(cot * vec_ref[2:3], n, inv)
        g2_ref[...] = g
        g2low_ref[at, :] = g.astype(bf16)

    @pl.when(i >= blocks)
    def _():
        per_chip = acc_ref.shape[0]
        half = per_chip // 2
        core = me & 1
        lo = pl.multiple_of(((me // 2) ^ (i - blocks)) * per_chip, 128)
        acc_ref[...] = dot_tn(h_ref[:, pl.ds(lo, per_chip)], g2low_ref[...])
        keep_ref[0] = acc_ref[pl.ds(pl.multiple_of(core * half, 8), half), :].astype(bf16)
        send_ref[0] = acc_ref[pl.ds(pl.multiple_of((1 - core) * half, 8), half), :].astype(bf16)

    @pl.when(i == pl.num_programs(0) - 1)
    def _():
        back.wait()


def down_forward(me, hidden_low, n1, cot, vec, pieces, shard_rows, chips):
    rows, hidden = hidden_low.shape
    width = n1.shape[1]
    metas = metas_of(pieces)
    block = 256
    blocks = rows // block
    per_chip = hidden // chips
    by_row = pl.BlockSpec((block, width), lambda i: (jnp.minimum(i, blocks - 1), 0))
    by_chip = pl.BlockSpec((1, per_chip // 2, width), lambda i: (jnp.maximum(i - blocks, 0), 0, 0))
    part = jax.ShapeDtypeStruct((chips, per_chip // 2, width), bf16)
    return pl.pallas_call(
        functools.partial(down_kernel, metas, shard_rows, blocks),
        grid=(blocks + chips,),
        in_specs=[SMEM, ANY, by_row, by_row, whole(vec.shape)] + [ANY] * len(metas),
        out_specs=[by_row, by_row, whole((rows, width)), whole((8, width)), by_chip, by_chip, ANY],
        out_shape=[
            jax.ShapeDtypeStruct((rows, width), bf16),
            jax.ShapeDtypeStruct((rows, width), f32),
            jax.ShapeDtypeStruct((rows, width), bf16),
            jax.ShapeDtypeStruct((8, width), f32),
            part,
            part,
            jax.ShapeDtypeStruct((hidden, width), bf16),
        ],
        scratch_shapes=[
            pltpu.VMEM((hidden, width), bf16),
            pltpu.VMEM((rows, hidden), bf16),
            pltpu.VMEM((per_chip, width), f32),
            pltpu.SemaphoreType.DMA((len(metas),)),
            pltpu.SemaphoreType.DMA((blocks,)),
            pltpu.SemaphoreType.DMA,
        ],
        cost_estimate=cost(4 * rows * width * hidden, 30_000_000, rows),
        name="down_norm_grad",
    )(me, hidden_low, n1, cot, vec, *arrays_of(pieces))


def hidden_grad_kernel(me_ref, g_ref, x_ref, a_ref, b_ref, w_ref, gg_ref, gu_ref, keep_ref, send_ref, acc_ref):
    block = gg_ref.shape[1]
    sub = 256
    for c in range(block // sub):
        cols = slice(c * sub, (c + 1) * sub)
        gh = dot_nt(g_ref[...], w_ref[cols, :])
        gg_ref[:, cols] = (gh * a_ref[:, cols].astype(f32)).astype(bf16)
        gu_ref[:, cols] = (gh * b_ref[:, cols].astype(f32)).astype(bf16)
    for part, ref in enumerate((gg_ref, gu_ref)):
        acc_ref[part] = dot_tn(x_ref[...], ref[...])
        spread(
            me_ref[0], acc_ref.at[part], keep_ref, send_ref, slice(part * block, (part + 1) * block)
        )


def hidden_grad(me, g2low, low, a, b, w_down, first, steps, count, name):
    rows, width = g2low.shape
    block = 768
    chips, shard_rows = count // 2, width // count
    spec_in = pl.BlockSpec((rows, block), lambda j: (0, first + j))
    spec = pl.BlockSpec((rows, block), lambda j: (0, j))
    shape = jax.ShapeDtypeStruct((rows, block * steps), bf16)
    part = jax.ShapeDtypeStruct((chips, shard_rows, 2 * block * steps), bf16)
    part_spec = pl.BlockSpec((chips, shard_rows, 2 * block), lambda j: (0, 0, j))
    return pl.pallas_call(
        hidden_grad_kernel,
        grid=(steps,),
        in_specs=[
            SMEM, whole(g2low.shape), whole(low.shape), spec_in, spec_in,
            pl.BlockSpec((block, width), lambda j: (first + j, 0)),
        ],
        out_specs=[spec, spec, part_spec, part_spec],
        out_shape=[shape, shape, part, part],
        scratch_shapes=[pltpu.VMEM((2, width, block), f32)],
        cost_estimate=cost(6 * rows * width * block * steps, 22_000_000),
        name=name,
    )(me, g2low, low, a, b, w_down)


def mixed_grad_kernel(halves, *refs):
    acts, rest = refs[: 2 * halves], refs[2 * halves :]
    g2_ref, n1_ref, inv_ref, vec_ref, wo_ref, w_any = rest[:6]
    g1_ref, g1low_ref, gatt_ref, sums_ref, w_ref, sems = rest[6:]
    hidden = w_ref.shape[1] // 2
    cols = hidden // halves
    i = pl.program_id(0)
    spans = [(a, part * hidden + h * cols) for h in range(halves) for part, a in enumerate((2 * h, 2 * h + 1))]
    copies = [
        pltpu.make_async_copy(w_any.at[:, pl.ds(lo, cols)], w_ref.at[:, pl.ds(lo, cols)], sems.at[c])
        for c, (_, lo) in enumerate(spans)
    ]

    @pl.when(i == 0)
    def _():
        start_all(copies)
        sums_ref[...] = jnp.zeros_like(sums_ref)

    gm = g2_ref[...]
    for c, (a, lo) in enumerate(spans):

        @pl.when(i == 0)
        def _():
            copies[c].wait()

        gm += dot_nt(acts[a][...], w_ref[:, lo : lo + cols])
    n = n1_ref[...]
    sums_ref[0:1] += jnp.sum(gm * n, 0, keepdims=True)
    sums_ref[1:2] += jnp.sum(gm, 0, keepdims=True)
    g = norm_back(gm * vec_ref[0:1], n, inv_ref[:, 0:1])
    g1_ref[...] = g
    low = g.astype(bf16)
    g1low_ref[...] = low
    gatt_ref[...] = dot_nt(low, wo_ref[...]).astype(bf16)


def mixed_grad(acts, g2, n1, inv1, vec, w_out, w_gate):
    rows, width = g2.shape
    cols = acts[0].shape[1]
    halves = len(acts) // 2
    hidden = cols * halves
    block = 256
    by_row = lambda n: pl.BlockSpec((block, n), lambda i: (i, 0))
    return pl.pallas_call(
        functools.partial(mixed_grad_kernel, halves),
        grid=(rows // block,),
        in_specs=[by_row(cols)] * len(acts)
        + [by_row(width), by_row(width), by_row(128), whole(vec.shape), whole(w_out.shape), ANY],
        out_specs=[by_row(width), by_row(width), by_row(width), whole((8, width))],
        out_shape=[
            jax.ShapeDtypeStruct((rows, width), f32),
            jax.ShapeDtypeStruct((rows, width), bf16),
            jax.ShapeDtypeStruct((rows, width), bf16),
            jax.ShapeDtypeStruct((8, width), f32),
        ],
        scratch_shapes=[
            pltpu.VMEM((width, 2 * hidden), bf16),
            pltpu.SemaphoreType.DMA((2 * halves,)),
        ],
        cost_estimate=cost(4 * rows * width * hidden + 2 * rows * width * width, 36_000_000),
        name="mixed_grad",
    )(*acts, g2, n1, inv1, vec, w_out, w_gate)


def attend_back_kernel(
    q_ref, k_ref, v_ref, o_ref, g_ref, p_ref, cos_ref, sin_ref, dq_ref, dk_ref, dv_ref
):
    heads = p_ref.shape[1]
    lane = lax.broadcasted_iota(jnp.int32, (1, 128), 1)
    first = half_mask((cos_ref.shape[0], 128))
    cos, sin = cos_ref[...], sin_ref[...]

    def unrotate(g):
        t = g * sin
        return g * cos + jnp.where(first, pltpu.roll(t, 96, 1), -pltpu.roll(t, 32, 1))

    for pair in range(heads // 2):
        cols = slice(pair * 128, (pair + 1) * 128)
        q, k, v, g = q_ref[:, cols], k_ref[:, cols], v_ref[:, cols], g_ref[:, cols]
        go = g.astype(f32) * o_ref[:, cols].astype(f32)
        dq = dk = dv = None
        for side in range(2):
            mine = (lane // HEAD_DIM) == side
            keep = mine.astype(bf16)
            p = p_ref[0, pair * 2 + side]
            row = jnp.sum(jnp.where(mine, go, 0.0), -1, keepdims=True)
            gp = dot_nt(g, v * keep)
            gs = (p.astype(f32) * (gp - row)).astype(bf16)
            parts = (dot_nn(gs, k * keep), dot_tn(gs, q * keep), dot_tn(p, g * keep))
            if dq is None:
                dq, dk, dv = parts
            else:
                dq, dk, dv = dq + parts[0], dk + parts[1], dv + parts[2]
        dq_ref[:, cols] = unrotate(dq * 0.125).astype(bf16)
        dk_ref[:, cols] = unrotate(dk).astype(bf16)
        dv_ref[:, cols] = dv.astype(bf16)


def attend_backward(q, k, v, attended, gatt, probs, cos, sin, first, steps, name):
    rows, _ = attended.shape
    seqs, _, seq, _ = probs.shape
    quad = 4
    lanes = quad * HEAD_DIM
    spec_in = pl.BlockSpec((seq, lanes), lambda s, g: (s, first + g))
    spec = pl.BlockSpec((seq, lanes), lambda s, g: (s, g))
    shape = jax.ShapeDtypeStruct((rows, lanes * steps), bf16)
    return pl.pallas_call(
        attend_back_kernel,
        grid=(seqs, steps),
        in_specs=[spec_in] * 5
        + [
            pl.BlockSpec((1, quad, seq, seq), lambda s, g: (s, first + g, 0, 0)),
            pl.BlockSpec(cos.shape, lambda s, g: (0, 0)),
            pl.BlockSpec(sin.shape, lambda s, g: (0, 0)),
        ],
        out_specs=[spec] * 3,
        out_shape=[shape] * 3,
        cost_estimate=cost(8 * seqs * quad * steps * seq * seq * 256, 9_000_000 * steps),
        name=name,
    )(q, k, v, attended, gatt, probs, cos, sin)


def qkv_grad_kernel(extra, me_ref, x_ref, dq_ref, dk_ref, dv_ref, *rest):
    me = me_ref[0]
    if extra:
        att_ref, g1_ref, s2_ref, s1_ref = rest[:4]
    keep_ref, send_ref, acc_ref = rest[-3:]
    width = x_ref.shape[1]
    lo = 0

    def put(value, lo):
        cols = value.shape[1]
        acc_ref[:, :cols] = value
        spread(me, acc_ref.at[:, :cols], keep_ref, send_ref, slice(lo, lo + cols))
        return lo + cols

    for ref in (dq_ref, dk_ref, dv_ref):
        lo = put(dot_tn(x_ref[...], ref[...]), lo)
    if extra:
        lo = put(dot_tn(att_ref[...], g1_ref[...]), lo)
        row = lax.broadcasted_iota(jnp.int32, (8, width), 0)
        rows = jnp.where(row < 2, s2_ref[...], pltpu.roll(s1_ref[...], 2, 0)).astype(bf16)
        put(dot_tn(rows, unit_rows()), lo)


def qkv_grad(me, x, parts, extra, count, name):
    rows, width = x.shape
    cols = parts[0].shape[1]
    chips, shard_rows = count // 2, width // count
    total = 3 * cols + (width + 128 if extra else 0)
    shape = jax.ShapeDtypeStruct((chips, shard_rows, total), bf16)
    vmem = pl.BlockSpec(memory_space=pltpu.VMEM)
    return pl.pallas_call(
        functools.partial(qkv_grad_kernel, bool(extra)),
        in_specs=[SMEM] + [vmem] * (4 + len(extra)),
        out_specs=[vmem, vmem],
        out_shape=[shape, shape],
        scratch_shapes=[pltpu.VMEM((width, width), f32)],
        cost_estimate=cost(2 * rows * width * total, 12_000_000),
        name=name,
    )(me, x, *parts, *extra)


def input_grad_kernel(count, g1_ref, w_ref, *rest):
    out_ref = rest[-1]
    width = out_ref.shape[1]
    total = g1_ref[...]
    lo = 0
    for p in range(3):
        for h in range(count):
            ref = rest[3 * h + p]
            total += dot_nt(ref[...], w_ref[:, lo : lo + ref.shape[1]])
            lo += ref.shape[1]
    out_ref[...] = total.astype(bf16)


def input_grad(g1, w_qkv, parts):
    rows, width = g1.shape
    block = 512
    by_row = lambda n: pl.BlockSpec((block, n), lambda i: (i, 0))
    flat = [p for three in parts for p in three]
    return pl.pallas_call(
        functools.partial(input_grad_kernel, len(parts)),
        grid=(rows // block,),
        in_specs=[by_row(width), whole(w_qkv.shape)] + [by_row(p.shape[1]) for p in flat],
        out_specs=by_row(width),
        out_shape=jax.ShapeDtypeStruct((rows, width), bf16),
        cost_estimate=cost(6 * rows * width * width, 14_000_000),
        name="input_grad",
    )(g1, w_qkv, *flat)


def rope_tables(seq_len):
    places = jnp.arange(seq_len, dtype=jnp.int32).astype(f32)
    frequency = rope_base ** (-jnp.arange(0, HEAD_DIM, 2, dtype=f32) / HEAD_DIM)
    angles = places[:, None] * frequency[None, :]
    return (jnp.tile(jnp.cos(angles), (1, 4)), jnp.tile(jnp.sin(angles), (1, 4)))


def shards(
    tokens, segment_ids, qkv_weight, out_weight, gate_weight, up_weight, down_weight,
    norm1_gain, norm1_bias, norm2_gain, norm2_bias, out_grad,
):
    count = lax.axis_size("shard")
    me = lax.axis_index("shard").astype(jnp.int32).reshape(1)
    batches, seq, width = tokens.shape
    shard_rows = qkv_weight.shape[0]
    down_rows = down_weight.shape[0]
    hidden = gate_weight.shape[1]
    rows = batches * seq
    chips = count // 2

    x = tokens.reshape(rows, width)
    cos, sin = rope_tables(seq)
    seg = segment_ids.reshape(batches, 1, seq)
    seg_col = segment_ids.reshape(batches, seq, 1)
    vectors = jnp.stack([norm1_gain, norm1_bias, norm2_gain, norm2_bias], 1)
    vectors = jnp.pad(vectors, ((0, 0), (0, 124)))
    own_a = jnp.concatenate([qkv_weight, out_weight, vectors], 1)
    own_b = jnp.concatenate([gate_weight, up_weight], 1)
    own_c = down_weight

    run_front = lambda pieces: front(me, x, cos, sin, seg, seg_col, pieces, shard_rows)
    run_gate = lambda low, pieces: gate_forward(me, low, pieces, shard_rows, hidden)
    if count == 8:
        a1 = gather_first(own_a)
        a2 = gather_second(*a1)
        b1 = gather_first(tie(own_b, a2))
        c1 = gather_first(tie(own_c, a2))
        q, k, v, attended, probs, n1, inv1, low, vec, w_qkv, w_out = run_front(
            with_partner(pieces_of(own_a, a1, a2))
        )
        b1 = tie(b1, low)
        b2 = gather_second(*b1)
        c1 = tie(c1, b2)
        c2 = gather_second(*c1)
        hidden_low, back_gate, back_up, w_gate = run_gate(low, with_partner(pieces_of(own_b, b1, b2)))
        c2 = tie(c2, hidden_low)
        pieces_c = with_partner(pieces_of(own_c, c1, c2))
    else:
        q, k, v, attended, probs, n1, inv1, low, vec, w_qkv, w_out = run_front(gather_pieces(own_a))
        hidden_low, back_gate, back_up, w_gate = run_gate(low, gather_pieces(own_b))
        pieces_c = gather_pieces(own_c)

    output, g2, g2low, sums2, d_keep, d_send, w_down = down_forward(
        me, hidden_low, n1, out_grad.reshape(rows, width), vec, pieces_c, down_rows, chips
    )
    steps = hidden // 768 // 2
    flow_d = Flow(d_keep, d_send)
    grads1 = hidden_grad(me, g2low, low, back_gate, back_up, w_down, 0, steps, count, "hidden_grad_1")
    flow_e = Flow(*grads1[2:])
    ready = advance(grads1[0], flow_d)
    grads2 = hidden_grad(
        me, tie(g2low, ready), low, back_gate, back_up, w_down, steps, steps, count, "hidden_grad_2"
    )
    flow_f = Flow(*grads2[2:])
    ready = advance(grads2[0], flow_e)
    g1, g1low, gatt, sums1 = mixed_grad(
        grads1[:2] + grads2[:2], tie(g2, ready), n1, inv1, vec, w_out, w_gate
    )
    ready = advance(g1low, flow_d, flow_f)
    back_a = attend_backward(
        q, k, v, attended, tie(gatt, ready), probs, cos, sin, 0, 2, "attend_bwd_1"
    )
    ready = advance(back_a[0], flow_d, flow_e)
    flow_a = Flow(
        *qkv_grad(me, x, tie(back_a, ready), (attended, g1low, sums2, sums1), count, "qkv_out_grad_1")
    )
    ready = advance(flow_a.held, flow_d, flow_e)
    back_b = attend_backward(
        q, k, v, attended, tie(gatt, ready), probs, cos, sin, 2, 1, "attend_bwd_2"
    )
    ready = advance(back_b[0], flow_f, flow_a, flow_d, flow_e)
    flow_b = Flow(*qkv_grad(me, x, tie(back_b, ready), (), count, "qkv_grad_2"))
    ready = advance(flow_b.held, flow_f, flow_e)
    in_grad = input_grad(tie(g1, ready), w_qkv, [back_a, back_b])
    advance(in_grad, flow_b, flow_a, flow_f)
    d_sum, e_sum, f_sum, a_sum, b_sum = [
        flow.finish() for flow in (flow_d, flow_e, flow_f, flow_a, flow_b)
    ]

    block = 768
    hidden_sums = (e_sum, f_sum)
    pick = lambda part: jnp.concatenate(
        [
            s[:, (2 * j + part) * block : (2 * j + part + 1) * block]
            for s in hidden_sums
            for j in range(steps)
        ],
        1,
    )
    cols_a, cols_b = back_a[0].shape[1], back_b[0].shape[1]
    qkv_sum = jnp.concatenate(
        [
            s[:, p * c : (p + 1) * c]
            for p in range(3)
            for s, c in ((a_sum, cols_a), (b_sum, cols_b))
        ],
        1,
    )
    out_sum = a_sum[:, 3 * cols_a : 3 * cols_a + width]
    vec_sum = a_sum[:, 3 * cols_a + width :]
    return (
        output.reshape(tokens.shape),
        in_grad.reshape(tokens.shape),
        qkv_sum,
        out_sum,
        pick(0),
        pick(1),
        d_sum,
        vec_sum[:, 2],
        vec_sum[:, 3],
        vec_sum[:, 0],
        vec_sum[:, 1],
    )


def solution(mesh):
    rows3 = P(None, ("shard", "rep"), None)
    rows2 = P("shard", None)
    rows1 = P("shard")
    in_specs = (rows3, P(None, ("shard", "rep"))) + (rows2,) * 5 + (rows1,) * 4 + (rows3,)
    out_specs = (rows3, rows3) + (rows2,) * 5 + (rows1,) * 4
    return jax.shard_map(shards, mesh=mesh, in_specs=in_specs, out_specs=out_specs, check_vma=False)
```

```python
import functools

import jax
import jax.numpy as jnp
import numpy as np
from jax import lax
from jax.experimental import pallas as pl
from jax.experimental.pallas import tpu as pltpu
from jax.sharding import PartitionSpec as P

HEAD_DIM = 64
norm_eps = 1e-12
rope_base = 1000.0
masked_score = -1e30
f32 = jnp.float32
bf16 = jnp.bfloat16
ANY = pl.BlockSpec(memory_space=pl.ANY)
SMEM = pl.BlockSpec(memory_space=pltpu.SMEM)


def dot_nn(a, b):
    return lax.dot_general(a, b, (((1,), (0,)), ((), ())), preferred_element_type=f32)


def dot_nt(a, b):
    return lax.dot_general(a, b, (((1,), (1,)), ((), ())), preferred_element_type=f32)


def dot_tn(a, b):
    return lax.dot_general(a, b, (((0,), (0,)), ((), ())), preferred_element_type=f32)


def whole(shape):
    return pl.BlockSpec(shape, lambda *_: (0,) * len(shape))


def tie(value, *deps):
    return lax.optimization_barrier((value, deps))[0]


def xor_permute(x, bit):
    count = lax.axis_size("shard")
    return lax.ppermute(x, "shard", [(i, i ^ bit) for i in range(count)])


def with_partner(pieces):
    return pieces + [(r | 1, lo, xor_permute(p, 1)) for r, lo, p in pieces]


def gather_direct(own):
    return [(0, 0, own)] + [(r, 0, xor_permute(own, r)) for r in range(2, lax.axis_size("shard"), 2)]


def gather_first(own):
    return xor_permute(own, 2), xor_permute(own, 4)


def gather_second(own, first):
    half = own.shape[0] // 2
    from_x, from_y = first
    far = (xor_permute(from_y[:half], 2), xor_permute(from_x[half:], 4))
    return [(0, 0, own), (2, 0, from_x), (4, 0, from_y), (6, 0, far[0]), (6, half, far[1])]


def add_parts(parts):
    return functools.reduce(jnp.add, [p.astype(f32) for p in parts]).astype(bf16)


def rep_permute(x, pairs):
    return lax.ppermute(x, "rep", pairs)


def load_kernel(jobs, body, *refs):
    operands, rest = refs[: body.operands], refs[body.operands :]
    outs, (hold, sems) = rest[: body.outs], rest[body.outs :]
    half = hold.shape[1]
    copies = []
    for i, (operand, block, part) in enumerate(jobs):
        ref = operands[operand]
        src = ref.at[block, pl.ds(part * half, half), :] if block is not None else ref
        copies.append(pltpu.make_async_copy(src, hold.at[i], sems.at[i]))
        copies[-1].start()
    for copy in copies:
        copy.wait()
    body(hold, *outs)


class Fold:
    def __init__(self, operands, outs, body):
        self.operands, self.outs, self.body = operands, outs, body

    def __call__(self, hold, *outs):
        self.body(hold, *outs)


def fold_call(arrays, jobs, out_shapes, body, half, cols, name):
    count = len(out_shapes)
    return pl.pallas_call(
        functools.partial(load_kernel, jobs, Fold(len(arrays), count, body)),
        in_specs=[pl.BlockSpec(memory_space=pl.ANY)] * len(arrays),
        out_specs=[pl.BlockSpec(memory_space=pltpu.VMEM)] * count,
        out_shape=[jax.ShapeDtypeStruct(s, bf16) for s in out_shapes],
        scratch_shapes=[
            pltpu.VMEM((len(jobs), half, cols), bf16),
            pltpu.SemaphoreType.DMA((len(jobs),)),
        ],
        compiler_params=pltpu.CompilerParams(vmem_limit_bytes=8 << 20),
        cost_estimate=cost(len(jobs) * half * cols, 3 * len(jobs) * half * cols),
        name=name,
    )(*arrays)


def plus(hold, *slots):
    return functools.reduce(jnp.add, [hold[s].astype(f32) for s in slots]).astype(bf16)


def fold_first(keep, got):
    _, rows, cols = keep.shape
    half = rows // 2
    jobs = [(a, q, p) for q, p in ((1, 0), (3, 0), (2, 1), (3, 1)) for a in (0, 1)]

    def body(hold, x_ref, y_ref):
        for n, ref in enumerate((x_ref, x_ref, y_ref, y_ref)):
            ref[n % 2] = plus(hold, 2 * n, 2 * n + 1)

    return fold_call([keep, got], jobs, [(2, half, cols)] * 2, body, half, cols, "fold_first")


def fold_second(keep, got, from_x, from_y):
    _, rows, cols = keep.shape
    half = rows // 2
    jobs = [(0, 2, 0), (1, 2, 0), (2, 1, 0), (0, 1, 1), (1, 1, 1), (3, 1, 0)]

    def body(hold, y_ref, x_ref):
        y_ref[...] = plus(hold, 0, 1, 2)
        x_ref[...] = plus(hold, 3, 4, 5)

    return fold_call(
        [keep, got, from_x, from_y], jobs, [(half, cols)] * 2, body, half, cols, "fold_second"
    )


def fold_own(keep, got, from_x, from_y, last_y, last_x):
    _, rows, cols = keep.shape
    half = rows // 2
    jobs = [
        (0, 0, 0), (1, 0, 0), (2, 0, 0), (4, None, 0), (0, 0, 1), (1, 0, 1), (3, 0, 0), (5, None, 0)
    ]

    def body(hold, own_ref):
        own_ref[:half] = plus(hold, 0, 1, 2, 3)
        own_ref[half:] = plus(hold, 4, 5, 6, 7)

    return fold_call(
        [keep, got, from_x, from_y, last_y, last_x], jobs, [(rows, cols)], body, half, cols, "fold_own"
    )[0]


class Flow:
    def __init__(self, keep, send, odd):
        self.held = keep
        self.odd = odd
        self.pending = xor_permute(send, 1)
        self.stage = 0
        self.pair = keep.shape[0] == 4
        self.line = lax.axis_size("rep") == 4

    def step(self, *deps):
        got = tie(self.pending, *deps) if deps else self.pending
        stage = self.stage
        if stage == 0:
            self.got = got
            if self.pair:
                self.ready = fold_first(self.held, got)
                self.pending = (xor_permute(self.ready[0], 2), xor_permute(self.ready[1], 4))
            else:
                self.ready = self.held + got
                self.pending = [xor_permute(self.ready[q], 2 * q) for q in range(1, got.shape[0])]
        elif stage == 1:
            self.first = got
            if self.pair:
                self.ready = fold_second(self.held, self.got, *got)
                self.pending = (xor_permute(self.ready[0], 4), xor_permute(self.ready[1], 2))
        elif stage == 2:
            if self.pair:
                self.ready = fold_own(self.held, self.got, *self.first, *got)
            else:
                self.ready = add_parts([self.ready[0]] + list(self.first))
            if self.line:
                half = self.ready.shape[0] // 2
                self.mine = jnp.where(self.odd, self.ready[half:], self.ready[:half])
                self.ready = jnp.where(self.odd, self.ready[:half], self.ready[half:])
                self.pending = rep_permute(self.ready, [(0, 1), (1, 0), (2, 3), (3, 2)])
            else:
                self.pending = lax.psum(self.ready, "rep")
        elif not self.line:
            self.ready = got
        elif stage == 3:
            self.ready = add_parts([self.mine, got])
            self.pending = rep_permute(self.ready, [(0, 2), (2, 0), (1, 3), (3, 1)])
        elif stage == 4:
            self.ready = add_parts([self.ready, got])
            self.pending = rep_permute(self.ready, [(0, 1), (1, 0), (2, 3), (3, 2)])
        else:
            low, high = (jnp.where(self.odd, a, b) for a, b in ((got, self.ready), (self.ready, got)))
            self.ready = jnp.concatenate([low, high]).astype(f32)
        self.stage += 1
        return self.ready

    def finish(self):
        while self.stage < 6:
            self.step()
        return self.ready.astype(f32)


def advance(dep, *flows):
    return tuple(flow.step(dep) for flow in flows)


def piece_copies(metas, refs, me, shard_rows, dst, src_lo, dst_lo, cols, sems):
    copies = []
    for i, ((rel, first, rows), ref) in enumerate(zip(metas, refs)):
        at = pl.multiple_of((me ^ rel) * shard_rows + first, 8)
        copies.append(
            pltpu.make_async_copy(
                ref.at[:, pl.ds(src_lo, cols)],
                dst.at[pl.ds(at, rows), pl.ds(dst_lo, cols)],
                sems.at[i],
            )
        )
    return copies


def start_all(copies):
    for copy in copies:
        copy.start()


def wait_all(copies):
    for copy in copies:
        copy.wait()


def metas_of(pieces):
    return tuple((rel, first, p.shape[0]) for rel, first, p in pieces)


def in_hbm(x):
    return pltpu.with_memory_space_constraint(x, pltpu.HBM)


def arrays_of(pieces):
    return [in_hbm(p) for _, _, p in pieces]


def half_mask(shape):
    lane = lax.broadcasted_iota(jnp.int32, shape, len(shape) - 1)
    return (lane % HEAD_DIM) < HEAD_DIM // 2


def unit_rows():
    shape = (8, 128)
    return (
        lax.broadcasted_iota(jnp.int32, shape, 0) == lax.broadcasted_iota(jnp.int32, shape, 1)
    ).astype(bf16)


def normalize(h):
    centre = h - jnp.mean(h, -1, keepdims=True)
    inv = lax.rsqrt(jnp.mean(centre * centre, -1, keepdims=True) + norm_eps)
    return centre * inv, inv


def norm_back(e, n, inv):
    return inv * (e - jnp.mean(e, -1, keepdims=True) - n * jnp.mean(e * n, -1, keepdims=True))


def spread(me, acc_ref, keep_ref, send_ref, cols):
    rows = keep_ref.shape[1]
    chip, core = me // 2, me & 1
    for q in range(keep_ref.shape[0]):
        base = (chip ^ q) * 2
        keep_ref[q, :, cols] = acc_ref[
            pl.ds(pl.multiple_of((base + core) * rows, 8), rows), :
        ].astype(bf16)
        send_ref[q, :, cols] = acc_ref[
            pl.ds(pl.multiple_of((base + 1 - core) * rows, 8), rows), :
        ].astype(bf16)


def cost(flops, read, transcendentals=0):
    return pl.CostEstimate(flops=1000, bytes_accessed=1000, transcendentals=0)


def front_kernel(metas, shard_rows, me_ref, x_ref, cos_ref, sin_ref, row_ref, *rest):
    refs, rest = rest[: len(metas)], rest[len(metas) :]
    q_ref, k_ref, v_ref, att_ref, p_ref, w_out, w_ref, bias_ref, sems, back_sem = rest
    s, g = pl.program_id(0), pl.program_id(1)
    width = x_ref.shape[1]
    lanes = p_ref.shape[1] * HEAD_DIM
    copies = piece_copies(metas, refs, me_ref[0], shard_rows, w_ref, 0, 0, 3 * width, sems)
    back = pltpu.make_async_copy(w_ref, w_out, back_sem)

    @pl.when((s == 0) & (g == 0))
    def _():
        start_all(copies)
        wait_all(copies)
        back.start()

    @pl.when(g == 0)
    def _():
        across = jnp.broadcast_to(row_ref[0].astype(f32), bias_ref.shape)
        down = lax.broadcasted_iota(jnp.int32, bias_ref.shape, 0)
        own = lax.broadcasted_iota(jnp.int32, bias_ref.shape, 1) == down
        column = jnp.sum(jnp.where(own, across, 0.0), -1, keepdims=True)
        bias_ref[...] = jnp.where(across == column, 0.0, masked_score).astype(f32)
        x = x_ref[...]
        first = half_mask((x.shape[0], 128))
        cos = cos_ref[...]
        sin = jnp.where(first, -sin_ref[...], sin_ref[...])
        for part, ref in enumerate((q_ref, k_ref, v_ref)):
            y = dot_nn(x, w_ref[:, part * width : (part + 1) * width])
            for b in range(width // 128):
                cols = slice(b * 128, (b + 1) * 128)
                u = y[:, cols]
                if part < 2:
                    turned = jnp.where(first, pltpu.roll(u, 96, 1), pltpu.roll(u, 32, 1))
                    u = u * cos + turned * sin
                if part == 0:
                    u = u * 0.125
                ref[:, cols] = u.astype(bf16)

    lane = lax.broadcasted_iota(jnp.int32, (1, 128), 1)
    for pair in range(lanes // 128):
        at = pl.ds(pl.multiple_of(g * lanes + pair * 128, 128), 128)
        q, k, v = q_ref[:, at], k_ref[:, at], v_ref[:, at]
        acc = None
        for side in range(2):
            mine = ((lane // HEAD_DIM) == side).astype(bf16)
            score = dot_nt(q, k * mine) + bias_ref[...]
            e = jnp.exp(score - jnp.max(score, -1, keepdims=True))
            inv = 1.0 / jnp.sum(e, -1, keepdims=True)
            p = (e * inv).astype(bf16)
            p_ref[0, pair * 2 + side] = p
            part = dot_nn(p, v * mine)
            acc = part if acc is None else acc + part
        att_ref[:, pair * 128 : (pair + 1) * 128] = acc.astype(bf16)

    @pl.when((s == pl.num_programs(0) - 1) & (g == pl.num_programs(1) - 1))
    def _():
        back.wait()


def front(me, x, cos, sin, seg_row, pieces, shard_rows):
    rows, width = x.shape
    metas = metas_of(pieces)
    seqs, _, seq = seg_row.shape
    heads = width // HEAD_DIM
    quad = 4
    lanes = quad * HEAD_DIM
    by_seq = pl.BlockSpec((seq, width), lambda s, g: (s, 0))
    wide = jax.ShapeDtypeStruct((rows, width), bf16)
    return pl.pallas_call(
        functools.partial(front_kernel, metas, shard_rows),
        grid=(seqs, width // lanes),
        in_specs=[
            SMEM, by_seq, whole(cos.shape), whole(sin.shape),
            pl.BlockSpec((1, 1, seq), lambda s, g: (s, 0, 0)),
        ]
        + [ANY] * len(metas),
        out_specs=[by_seq] * 3
        + [
            pl.BlockSpec((seq, lanes), lambda s, g: (s, g)),
            pl.BlockSpec((1, quad, seq, seq), lambda s, g: (s, g, 0, 0)),
            ANY,
        ],
        out_shape=[wide] * 4
        + [
            jax.ShapeDtypeStruct((seqs, heads, seq, seq), bf16),
            jax.ShapeDtypeStruct((width, 3 * width), bf16),
        ],
        scratch_shapes=[
            pltpu.VMEM((width, 3 * width), bf16),
            pltpu.VMEM((seq, seq), f32),
            pltpu.SemaphoreType.DMA((len(metas),)),
            pltpu.SemaphoreType.DMA,
        ],
        cost_estimate=cost(
            6 * rows * width * width + 4 * seqs * heads * seq * seq * 256,
            30_000_000,
            seqs * heads * seq * seq,
        ),
        name="qkv_attend",
    )(me, x, cos, sin, seg_row, *arrays_of(pieces))


VM = pl.BlockSpec(memory_space=pltpu.VMEM)
HBM = pl.BlockSpec(memory_space=pltpu.HBM)


def in_vmem(shape, dtype=bf16):
    return pltpu.VMEM(shape, dtype)


def limit(mib):
    return pltpu.CompilerParams(vmem_limit_bytes=mib << 20)


def gate_kernel(metas, shard_rows, me_ref, tok_ref, att_ref, *rest):
    refs, rest = rest[: len(metas)], rest[len(metas) :]
    h_ref, a_ref, b_ref, x_ref, n1_ref, inv_ref, vec_ref, wo_ref = rest[:8]
    wg_ref, wv_ref, sems, sems_o = rest[8:]
    hidden = a_ref.shape[1]
    width = wo_ref.shape[1]
    block = 768
    steps = hidden // block
    me = me_ref[0]

    def spans(j):
        return pl.multiple_of(j * block, block), pl.multiple_of(hidden + j * block, block)

    def copies(j):
        both = []
        for part, lo in enumerate(spans(j)):
            both += piece_copies(metas, refs, me, shard_rows, wg_ref, lo, lo, block, sems.at[j, part])
        return both

    copies_o = piece_copies(
        metas, refs, me, shard_rows, wo_ref, 2 * hidden, 0, width, sems_o.at[0]
    ) + piece_copies(metas, refs, me, shard_rows, wv_ref, 2 * hidden + width, 0, 128, sems_o.at[1])
    start_all(copies_o)

    @pl.loop(0, steps)
    def _(j):
        start_all(copies(j))

    wait_all(copies_o)
    vec_ref[...] = dot_nt(unit_rows(), wv_ref[...])

    @pl.loop(0, 2)
    def _(i):
        rows = tok_ref.shape[0] // 2
        at = pl.ds(pl.multiple_of(i * rows, 8), rows)
        n, inv = normalize(tok_ref[at, :].astype(f32) + dot_nn(att_ref[at, :], wo_ref[...]))
        n1_ref[at, :] = n.astype(bf16)
        inv_ref[at, :] = jnp.broadcast_to(inv, (rows, inv_ref.shape[1]))
        x_ref[at, :] = (n * vec_ref[0:1] + vec_ref[1:2]).astype(bf16)

    @pl.loop(0, steps)
    def _(j):
        wait_all(copies(j))
        gate_at, up_at = (pl.ds(lo, block) for lo in spans(j))
        half = x_ref.shape[0] // 2
        for r in range(2):
            rows = slice(r * half, (r + 1) * half)
            gate = dot_nn(x_ref[rows, :], wg_ref[:, gate_at])
            up = dot_nn(x_ref[rows, :], wg_ref[:, up_at])
            s = 0.5 * jnp.tanh(0.5 * gate) + 0.5
            act = gate * s
            h_ref[rows, gate_at] = (act * up).astype(bf16)
            b_ref[rows, gate_at] = act.astype(bf16)
            a_ref[rows, gate_at] = (up * (s + act * (1.0 - s))).astype(bf16)


def gate_forward(me, tokens, attended, pieces, shard_rows, hidden):
    rows, width = tokens.shape
    metas = metas_of(pieces)
    return pl.pallas_call(
        functools.partial(gate_kernel, metas, shard_rows),
        in_specs=[SMEM, VM, VM] + [ANY] * len(metas),
        out_specs=[VM] * 8,
        out_shape=[in_vmem((rows, hidden))] * 3
        + [
            in_vmem((rows, width)),
            in_vmem((rows, width)),
            in_vmem((rows, 128), f32),
            in_vmem((8, width), f32),
            in_vmem((width, width)),
        ],
        scratch_shapes=[
            pltpu.VMEM((width, 2 * hidden), bf16),
            pltpu.VMEM((width, 128), bf16),
            pltpu.SemaphoreType.DMA((hidden // 768, 2, len(metas))),
            pltpu.SemaphoreType.DMA((2, len(metas))),
        ],
        compiler_params=limit(18),
        cost_estimate=cost(4 * rows * width * hidden, 10_000_000, rows * hidden),
        name="out_gate_up",
    )(me, tokens, attended, *arrays_of(pieces))


def down_kernel(metas, shard_rows, me_ref, h_ref, n1_ref, cot_ref, vec_ref, *rest):
    refs = rest[: len(metas)]
    out_ref, low_ref, sums_ref, keep_ref, send_ref, w_ref, acc_ref, sems = rest[len(metas) :]
    me = me_ref[0]
    copies = piece_copies(metas, refs, me, shard_rows, w_ref, 0, 0, w_ref.shape[1], sems)
    start_all(copies)
    sums_ref[...] = jnp.zeros_like(sums_ref)
    wait_all(copies)
    block = 256

    @pl.loop(0, h_ref.shape[0] // block)
    def _(i):
        at = pl.ds(pl.multiple_of(i * block, block), block)
        mixed = n1_ref[at, :].astype(f32) * vec_ref[0:1] + vec_ref[1:2]
        n, inv = normalize(mixed + dot_nn(h_ref[at, :], w_ref[...]))
        out_ref[at, :] = (n * vec_ref[2:3] + vec_ref[3:4]).astype(bf16)
        cot = cot_ref[at, :].astype(f32)
        sums_ref[0:1] += jnp.sum(cot * n, 0, keepdims=True)
        sums_ref[1:2] += jnp.sum(cot, 0, keepdims=True)
        low_ref[at, :] = norm_back(cot * vec_ref[2:3], n, inv).astype(bf16)

    per_chip = acc_ref.shape[0]
    half = per_chip // 2
    core = me & 1

    @pl.loop(0, keep_ref.shape[0])
    def _(q):
        lo = pl.multiple_of(((me // 2) ^ q) * per_chip, 128)
        acc_ref[...] = dot_tn(h_ref[:, pl.ds(lo, per_chip)], low_ref[...])
        keep_ref[q] = acc_ref[pl.ds(pl.multiple_of(core * half, 8), half), :].astype(bf16)
        send_ref[q] = acc_ref[pl.ds(pl.multiple_of((1 - core) * half, 8), half), :].astype(bf16)


def down_forward(me, hidden_low, n1, cot, vec, pieces, shard_rows, chips):
    rows, hidden = hidden_low.shape
    width = n1.shape[1]
    metas = metas_of(pieces)
    per_chip = hidden // chips
    return pl.pallas_call(
        functools.partial(down_kernel, metas, shard_rows),
        in_specs=[SMEM, VM, VM, VM, VM] + [ANY] * len(metas),
        out_specs=[VM] * 6,
        out_shape=[
            jax.ShapeDtypeStruct((rows, width), bf16),
            in_vmem((rows, width)),
            in_vmem((8, width), f32),
            jax.ShapeDtypeStruct((chips, per_chip // 2, width), bf16),
            jax.ShapeDtypeStruct((chips, per_chip // 2, width), bf16),
            in_vmem((hidden, width)),
        ],
        scratch_shapes=[
            pltpu.VMEM((per_chip, width), f32),
            pltpu.SemaphoreType.DMA((len(metas),)),
        ],
        compiler_params=limit(18),
        cost_estimate=cost(4 * rows * width * hidden, 10_000_000, rows),
        name="down_norm_grad",
    )(me, hidden_low, n1, cot, vec, *arrays_of(pieces))


def hidden_grad_kernel(
    first, steps, me_ref, g_ref, x_ref, a_ref, b_ref, w_ref, gg_ref, gu_ref, _g, _w, keep_ref, send_ref, acc_ref
):
    block = 768

    @pl.loop(0, steps)
    def _(j):
        cols = pl.ds(pl.multiple_of((first + j) * block, block), block)
        half = g_ref.shape[0] // 2
        for r in range(2):
            rows = slice(r * half, (r + 1) * half)
            gh = dot_nt(g_ref[rows, :], w_ref[cols, :])
            gg_ref[rows, cols] = (gh * a_ref[rows, cols].astype(f32)).astype(bf16)
            gu_ref[rows, cols] = (gh * b_ref[rows, cols].astype(f32)).astype(bf16)
        for part, ref in enumerate((gg_ref, gu_ref)):
            acc_ref[...] = dot_tn(x_ref[...], ref[:, cols])
            lo = pl.multiple_of((2 * j + part) * block, block)
            spread(me_ref[0], acc_ref, keep_ref, send_ref, pl.ds(lo, block))


def hidden_grad(me, g2low, low, a, b, w_down, first, steps, count, name):
    rows, width = g2low.shape
    block = 768
    chips, shard_rows = count // 2, width // count
    part = jax.ShapeDtypeStruct((chips, shard_rows, 2 * block * steps), bf16)
    return pl.pallas_call(
        functools.partial(hidden_grad_kernel, first, steps),
        in_specs=[SMEM, VM, VM, VM, VM, VM],
        out_specs=[VM] * 6,
        out_shape=[
            in_vmem(a.shape), in_vmem(b.shape), in_vmem(g2low.shape), in_vmem(w_down.shape), part, part
        ],
        input_output_aliases={3: 0, 4: 1, 1: 2, 5: 3},
        scratch_shapes=[pltpu.VMEM((width, block), f32)],
        compiler_params=limit(18),
        cost_estimate=cost(6 * rows * width * block * steps, 5_000_000),
        name=name,
    )(me, g2low, low, a, b, w_down)


def mixed_grad_kernel(
    metas, shard_rows, me_ref, gg_ref, gu_ref, g2_ref, n1_ref, inv_ref, vec_ref, wo_ref, *rest
):
    refs, rest = rest[: len(metas)], rest[len(metas) :]
    low_ref, gatt_ref, sums_ref, _gg, _gu, _g2, w_ref, sems = rest
    hidden = gg_ref.shape[1]
    block = 256
    copies = [
        piece_copies(
            metas, refs, me_ref[0], shard_rows, w_ref, c * hidden, c * hidden, hidden, sems.at[c]
        )
        for c in range(2)
    ]
    start_all(copies[0])
    start_all(copies[1])
    sums_ref[...] = jnp.zeros_like(sums_ref)

    def rows(at, waits):
        if waits:
            wait_all(copies[0])
        gm = g2_ref[at, :].astype(f32) + dot_nt(gg_ref[at, :], w_ref[:, :hidden])
        if waits:
            wait_all(copies[1])
        gm += dot_nt(gu_ref[at, :], w_ref[:, hidden:])
        n = n1_ref[at, :].astype(f32)
        sums_ref[0:1] += jnp.sum(gm * n, 0, keepdims=True)
        sums_ref[1:2] += jnp.sum(gm, 0, keepdims=True)
        low = norm_back(gm * vec_ref[0:1], n, inv_ref[at, 0:1]).astype(bf16)
        low_ref[at, :] = low
        gatt_ref[at, :] = dot_nt(low, wo_ref[...]).astype(bf16)

    rows(slice(0, block), True)

    @pl.loop(1, gg_ref.shape[0] // block)
    def _(i):
        rows(pl.ds(pl.multiple_of(i * block, block), block), False)


def mixed_grad(me, gg, gu, g2, n1, inv1, vec, w_out, pieces, shard_rows):
    rows, width = g2.shape
    hidden = gg.shape[1]
    metas = metas_of(pieces)
    return pl.pallas_call(
        functools.partial(mixed_grad_kernel, metas, shard_rows),
        in_specs=[SMEM] + [VM] * 7 + [ANY] * len(metas),
        out_specs=[VM] * 6,
        out_shape=[
            jax.ShapeDtypeStruct((rows, width), bf16),
            jax.ShapeDtypeStruct((rows, width), bf16),
            jax.ShapeDtypeStruct((8, width), f32),
            in_vmem(gg.shape),
            in_vmem(gu.shape),
            in_vmem(g2.shape),
        ],
        input_output_aliases={1: 3, 2: 4, 3: 5},
        scratch_shapes=[
            pltpu.VMEM((width, 2 * hidden), bf16),
            pltpu.SemaphoreType.DMA((2, len(metas))),
        ],
        compiler_params=limit(18),
        cost_estimate=cost(4 * rows * width * hidden + 2 * rows * width * width, 15_000_000),
        name="mixed_grad",
    )(me, gg, gu, g2, n1, inv1, vec, w_out, *arrays_of(pieces))[:3]


def attend_back_kernel(
    q_ref, k_ref, v_ref, o_ref, g_ref, p_ref, cos_ref, sin_ref, dq_ref, dk_ref, dv_ref
):
    heads = p_ref.shape[1]
    lane = lax.broadcasted_iota(jnp.int32, (1, 128), 1)
    first = half_mask((cos_ref.shape[0], 128))
    cos, sin = cos_ref[...], sin_ref[...]

    def unrotate(g):
        t = g * sin
        return g * cos + jnp.where(first, pltpu.roll(t, 96, 1), -pltpu.roll(t, 32, 1))

    for pair in range(heads // 2):
        cols = slice(pair * 128, (pair + 1) * 128)
        q, k, v, g = q_ref[:, cols], k_ref[:, cols], v_ref[:, cols], g_ref[:, cols]
        go = g.astype(f32) * o_ref[:, cols].astype(f32)
        dq = dk = dv = None
        for side in range(2):
            mine = (lane // HEAD_DIM) == side
            keep = mine.astype(bf16)
            p = p_ref[0, pair * 2 + side]
            row = jnp.sum(jnp.where(mine, go, 0.0), -1, keepdims=True)
            gp = dot_nt(g, v * keep)
            gs = (p.astype(f32) * (gp - row)).astype(bf16)
            parts = (dot_nn(gs, k * keep), dot_tn(gs, q * keep), dot_tn(p, g * keep))
            if dq is None:
                dq, dk, dv = parts
            else:
                dq, dk, dv = dq + parts[0], dk + parts[1], dv + parts[2]
        dq_ref[:, cols] = unrotate(dq * 0.125).astype(bf16)
        dk_ref[:, cols] = unrotate(dk).astype(bf16)
        dv_ref[:, cols] = dv.astype(bf16)


def attend_backward(q, k, v, attended, gatt, probs, cos, sin, first, steps, name):
    rows, _ = attended.shape
    seqs, _, seq, _ = probs.shape
    quad = 4
    lanes = quad * HEAD_DIM
    spec_in = pl.BlockSpec((seq, lanes), lambda s, g: (s, first + g))
    spec = pl.BlockSpec((seq, lanes), lambda s, g: (s, g))
    shape = jax.ShapeDtypeStruct((rows, lanes * steps), bf16)
    return pl.pallas_call(
        attend_back_kernel,
        grid=(seqs, steps),
        in_specs=[spec_in] * 5
        + [
            pl.BlockSpec((1, quad, seq, seq), lambda s, g: (s, first + g, 0, 0)),
            pl.BlockSpec(cos.shape, lambda s, g: (0, 0)),
            pl.BlockSpec(sin.shape, lambda s, g: (0, 0)),
        ],
        out_specs=[spec] * 3,
        out_shape=[shape] * 3,
        cost_estimate=cost(8 * seqs * quad * steps * seq * seq * 256, 9_000_000 * steps),
        name=name,
    )(q, k, v, attended, gatt, probs, cos, sin)


def qkv_grad_kernel(extra, me_ref, x_ref, dq_ref, dk_ref, dv_ref, *rest):
    me = me_ref[0]
    if extra:
        att_ref, g1_ref, s2_ref, s1_ref = rest[:4]
    keep_ref, send_ref, acc_ref = rest[-3:]
    width = x_ref.shape[1]
    lo = 0

    def put(value, lo):
        cols = value.shape[1]
        acc_ref[:, :cols] = value
        spread(me, acc_ref.at[:, :cols], keep_ref, send_ref, slice(lo, lo + cols))
        return lo + cols

    for ref in (dq_ref, dk_ref, dv_ref):
        lo = put(dot_tn(x_ref[...], ref[...]), lo)
    if extra:
        lo = put(dot_tn(att_ref[...], g1_ref[...]), lo)
        row = lax.broadcasted_iota(jnp.int32, (8, width), 0)
        rows = jnp.where(row < 2, s2_ref[...], pltpu.roll(s1_ref[...], 2, 0)).astype(bf16)
        put(dot_tn(rows, unit_rows()), lo)


def qkv_grad(me, x, parts, extra, count, name):
    rows, width = x.shape
    cols = parts[0].shape[1]
    chips, shard_rows = count // 2, width // count
    total = 3 * cols + (width + 128 if extra else 0)
    shape = jax.ShapeDtypeStruct((chips, shard_rows, total), bf16)
    vmem = pl.BlockSpec(memory_space=pltpu.VMEM)
    return pl.pallas_call(
        functools.partial(qkv_grad_kernel, bool(extra)),
        in_specs=[SMEM] + [vmem] * (4 + len(extra)),
        out_specs=[vmem, vmem],
        out_shape=[shape, shape],
        scratch_shapes=[pltpu.VMEM((width, width), f32)],
        cost_estimate=cost(2 * rows * width * total, 12_000_000),
        name=name,
    )(me, x, *parts, *extra)


def input_grad_kernel(count, g1_ref, w_ref, *rest):
    out_ref = rest[-1]
    width = out_ref.shape[1]
    total = g1_ref[...].astype(f32)
    lo = 0
    for p in range(3):
        for h in range(count):
            ref = rest[3 * h + p]
            total += dot_nt(ref[...], w_ref[:, lo : lo + ref.shape[1]])
            lo += ref.shape[1]
    out_ref[...] = total.astype(bf16)


def input_grad(g1, w_qkv, parts):
    rows, width = g1.shape
    block = 512
    by_row = lambda n: pl.BlockSpec((block, n), lambda i: (i, 0))
    flat = [p for three in parts for p in three]
    return pl.pallas_call(
        functools.partial(input_grad_kernel, len(parts)),
        grid=(rows // block,),
        in_specs=[by_row(width), whole(w_qkv.shape)] + [by_row(p.shape[1]) for p in flat],
        out_specs=by_row(width),
        out_shape=jax.ShapeDtypeStruct((rows, width), bf16),
        cost_estimate=cost(6 * rows * width * width, 14_000_000),
        name="input_grad",
    )(g1, w_qkv, *flat)


def rope_tables(seq_len):
    places = np.arange(seq_len, dtype=np.float32)
    frequency = rope_base ** (-np.arange(0, HEAD_DIM, 2, dtype=np.float32) / HEAD_DIM)
    angles = places[:, None] * frequency[None, :].astype(np.float32)
    tables = (np.cos(angles), np.sin(angles))
    return tuple(jnp.asarray(np.tile(table, (1, 4)).astype(np.float32)) for table in tables)


def shards(
    tokens, segment_ids, qkv_weight, out_weight, gate_weight, up_weight, down_weight,
    norm1_gain, norm1_bias, norm2_gain, norm2_bias, out_grad,
):
    count = lax.axis_size("shard")
    me = lax.axis_index("shard").astype(jnp.int32).reshape(1)
    batches, seq, width = tokens.shape
    shard_rows = qkv_weight.shape[0]
    down_rows = down_weight.shape[0]
    hidden = gate_weight.shape[1]
    rows = batches * seq
    chips = count // 2

    x = tokens.reshape(rows, width)
    cot = out_grad.reshape(rows, width)
    cos, sin = rope_tables(seq)
    vectors = jnp.stack([norm1_gain, norm1_bias, norm2_gain, norm2_bias], 1)
    vectors = jnp.pad(vectors, ((0, 0), (0, 124)))
    odd = (lax.axis_index("rep") % 2 == 1).reshape(1, 1)

    pieces_a = gather_direct(qkv_weight)
    own_b = jnp.concatenate([gate_weight, up_weight, out_weight, vectors], 1)
    seg = segment_ids.reshape(batches, 1, seq)
    seg, own_b, odd, ready = tie((seg, own_b, odd, pieces_a[0][2]))
    pieces_a = [(r, lo, tie(p, ready, seg, odd)) for r, lo, p in pieces_a]
    far_a = tuple(p for _, _, p in pieces_a[1:])
    pieces_a = with_partner(pieces_a)
    own_b = tie(own_b, far_a)
    if count == 8:
        first_b = gather_first(own_b)
    else:
        pieces_b = gather_direct(own_b)
        pieces_c = gather_direct(down_weight)
    q, k, v, attended, probs, w_qkv = front(me, x, cos, sin, seg, pieces_a, shard_rows)
    if count == 8:
        first_b = tie(first_b, attended)
        pieces_b = gather_second(own_b, first_b)
        pieces_c = gather_direct(tie(down_weight, first_b))
    pieces_b = with_partner(pieces_b)
    hidden_low, back_gate, back_up, low, n1, inv1, vec, w_out = gate_forward(
        me, x, attended, pieces_b, shard_rows, hidden
    )
    pieces_c = with_partner([(r, lo, tie(p, low)) for r, lo, p in pieces_c])
    output, g2low, sums2, d_keep, d_send, w_down = down_forward(
        me, hidden_low, n1, cot, vec, pieces_c, down_rows, chips
    )
    steps = hidden // 768 // 2
    flow_d = Flow(d_keep, d_send, odd)
    grads1 = hidden_grad(me, g2low, low, back_gate, back_up, w_down, 0, steps, count, "hidden_grad_1")
    flow_e = Flow(*grads1[4:], odd)
    ready = advance(grads1[0], flow_d)
    grads2 = hidden_grad(
        me, tie(grads1[2], ready), low, *grads1[:2], grads1[3], steps, steps, count, "hidden_grad_2"
    )
    flow_f = Flow(*grads2[4:], odd)
    ready = advance(grads2[0], flow_e)
    ready = advance(ready, flow_d)
    g1low, gatt, sums1 = mixed_grad(
        me, *grads2[:2], tie(grads2[2], ready), n1, inv1, vec, w_out, pieces_b, shard_rows
    )
    ready = advance(g1low, flow_f, flow_e, flow_d)
    back_a = attend_backward(
        q, k, v, attended, tie(gatt, ready), probs, cos, sin, 0, 2, "attend_bwd_1"
    )
    a_keep, a_send = qkv_grad(me, x, back_a, (attended, g1low, sums2, sums1), count, "qkv_out_grad_1")
    ready = advance(a_keep, flow_f, flow_e, flow_d)
    flow_a = Flow(a_keep, tie(a_send, ready), odd)
    back_b = attend_backward(
        q, k, v, attended, tie(gatt, ready), probs, cos, sin, 2, 1, "attend_bwd_2"
    )
    b_keep, b_send = qkv_grad(me, x, back_b, (), count, "qkv_grad_2")
    ready = advance(b_keep, flow_a, flow_f, flow_e, flow_d)
    flow_b = Flow(b_keep, tie(b_send, ready), odd)
    in_grad = input_grad(tie(g1low, ready), w_qkv, [back_a, back_b])
    ready = advance(in_grad, flow_b, flow_a, flow_f, flow_e, flow_d)
    ready = advance(ready, flow_b, flow_a, flow_f, flow_e)
    ready = advance(ready, flow_b, flow_a, flow_f)
    ready = advance(ready, flow_b, flow_a)
    d_sum, e_sum, f_sum, a_sum, b_sum = [
        flow.finish() for flow in (flow_d, flow_e, flow_f, flow_a, flow_b)
    ]

    block = 768
    hidden_sums = (e_sum, f_sum)
    pick = lambda part: jnp.concatenate(
        [
            s[:, (2 * j + part) * block : (2 * j + part + 1) * block]
            for s in hidden_sums
            for j in range(steps)
        ],
        1,
    )
    cols_a, cols_b = back_a[0].shape[1], back_b[0].shape[1]
    qkv_sum = jnp.concatenate(
        [
            s[:, p * c : (p + 1) * c]
            for p in range(3)
            for s, c in ((a_sum, cols_a), (b_sum, cols_b))
        ],
        1,
    )
    out_sum = a_sum[:, 3 * cols_a : 3 * cols_a + width]
    vec_sum = a_sum[:, 3 * cols_a + width :]
    return (
        output.reshape(tokens.shape),
        in_grad.reshape(tokens.shape),
        qkv_sum,
        out_sum,
        pick(0),
        pick(1),
        d_sum,
        vec_sum[:, 2],
        vec_sum[:, 3],
        vec_sum[:, 0],
        vec_sum[:, 1],
    )


def solution(mesh):
    rows3 = P(None, ("shard", "rep"), None)
    rows2 = P("shard", None)
    rows1 = P("shard")
    in_specs = (rows3, P(None, ("shard", "rep"))) + (rows2,) * 5 + (rows1,) * 4 + (rows3,)
    out_specs = (rows3, rows3) + (rows2,) * 5 + (rows1,) * 4
    return jax.shard_map(shards, mesh=mesh, in_specs=in_specs, out_specs=out_specs, check_vma=False)
```

```python
import functools

import jax
import jax.numpy as jnp
import numpy as np
from jax import lax
from jax.experimental import pallas as pl
from jax.experimental.pallas import tpu as pltpu
from jax.sharding import PartitionSpec as P

HEAD_DIM = 64
norm_eps = 1e-12
rope_base = 1000.0
masked_score = -1e30
f32 = jnp.float32
bf16 = jnp.bfloat16
ANY = pl.BlockSpec(memory_space=pl.ANY)
SMEM = pl.BlockSpec(memory_space=pltpu.SMEM)


def dot_nn(a, b):
    return lax.dot_general(a, b, (((1,), (0,)), ((), ())), preferred_element_type=f32)


def dot_nt(a, b):
    return lax.dot_general(a, b, (((1,), (1,)), ((), ())), preferred_element_type=f32)


def dot_tn(a, b):
    return lax.dot_general(a, b, (((0,), (0,)), ((), ())), preferred_element_type=f32)


def whole(shape):
    return pl.BlockSpec(shape, lambda *_: (0,) * len(shape))


def tie(value, *deps):
    return lax.optimization_barrier((value, deps))[0]


def xor_permute(x, bit):
    count = lax.axis_size("shard")
    return lax.ppermute(x, "shard", [(i, i ^ bit) for i in range(count)])


def with_partner(pieces):
    return pieces + [(r | 1, lo, xor_permute(p, 1)) for r, lo, p in pieces]


def gather_direct(own):
    return [(0, 0, own)] + [(r, 0, xor_permute(own, r)) for r in range(2, lax.axis_size("shard"), 2)]


def gather_first(own):
    return xor_permute(own, 2), xor_permute(own, 4)


def gather_second(own, first):
    half = own.shape[0] // 2
    from_x, from_y = first
    far = (xor_permute(from_y[:half], 2), xor_permute(from_x[half:], 4))
    return [(0, 0, own), (2, 0, from_x), (4, 0, from_y), (6, 0, far[0]), (6, half, far[1])]


def add_parts(parts):
    return functools.reduce(jnp.add, [p.astype(f32) for p in parts]).astype(bf16)


def rep_permute(x, pairs):
    return lax.ppermute(x, "rep", pairs)


def load_kernel(jobs, body, *refs):
    operands, rest = refs[: body.operands], refs[body.operands :]
    outs, (hold, sems) = rest[: body.outs], rest[body.outs :]
    half = hold.shape[1]
    copies = []
    for i, (operand, block, part) in enumerate(jobs):
        ref = operands[operand]
        src = ref.at[block, pl.ds(part * half, half), :] if block is not None else ref
        copies.append(pltpu.make_async_copy(src, hold.at[i], sems.at[i]))
        copies[-1].start()
    for copy in copies:
        copy.wait()
    body(hold, *outs)


class Fold:
    def __init__(self, operands, outs, body):
        self.operands, self.outs, self.body = operands, outs, body

    def __call__(self, hold, *outs):
        self.body(hold, *outs)


def fold_call(arrays, jobs, out_shapes, body, half, cols, name):
    count = len(out_shapes)
    return pl.pallas_call(
        functools.partial(load_kernel, jobs, Fold(len(arrays), count, body)),
        in_specs=[pl.BlockSpec(memory_space=pl.ANY)] * len(arrays),
        out_specs=[pl.BlockSpec(memory_space=pltpu.VMEM)] * count,
        out_shape=[jax.ShapeDtypeStruct(s, bf16) for s in out_shapes],
        scratch_shapes=[
            pltpu.VMEM((len(jobs), half, cols), bf16),
            pltpu.SemaphoreType.DMA((len(jobs),)),
        ],
        compiler_params=pltpu.CompilerParams(vmem_limit_bytes=8 << 20),
        cost_estimate=cost(len(jobs) * half * cols, 3 * len(jobs) * half * cols),
        name=name,
    )(*arrays)


def each_rows(rows, step, body):
    @pl.loop(0, rows // step)
    def _(i):
        body(pl.ds(pl.multiple_of(i * step, step), step))


def plus(hold, at, *slots):
    return functools.reduce(jnp.add, [hold[s, at, :].astype(f32) for s in slots]).astype(bf16)


def row_step(half):
    return 16 if half % 16 == 0 else 8


def fold_first(keep, got):
    _, rows, cols = keep.shape
    half = rows // 2
    jobs = [(a, q, p) for q, p in ((1, 0), (3, 0), (2, 1), (3, 1)) for a in (0, 1)]

    def body(hold, x_ref, y_ref):
        def some(at):
            for n, ref in enumerate((x_ref, x_ref, y_ref, y_ref)):
                ref[n % 2, at, :] = plus(hold, at, 2 * n, 2 * n + 1)

        each_rows(half, row_step(half), some)

    return fold_call([keep, got], jobs, [(2, half, cols)] * 2, body, half, cols, "fold_first")


def fold_second(keep, got, from_x, from_y):
    _, rows, cols = keep.shape
    half = rows // 2
    jobs = [(0, 2, 0), (1, 2, 0), (2, 1, 0), (0, 1, 1), (1, 1, 1), (3, 1, 0)]

    def body(hold, y_ref, x_ref):
        def some(at):
            y_ref[at, :] = plus(hold, at, 0, 1, 2)
            x_ref[at, :] = plus(hold, at, 3, 4, 5)

        each_rows(half, row_step(half), some)

    return fold_call(
        [keep, got, from_x, from_y], jobs, [(half, cols)] * 2, body, half, cols, "fold_second"
    )


def fold_own(keep, got, from_x, from_y, last_y, last_x):
    _, rows, cols = keep.shape
    half = rows // 2
    jobs = [
        (0, 0, 0), (1, 0, 0), (2, 0, 0), (4, None, 0), (0, 0, 1), (1, 0, 1), (3, 0, 0), (5, None, 0)
    ]

    def body(hold, own_ref):
        def some(at):
            own_ref[0, at, :] = plus(hold, at, 0, 1, 2, 3)
            own_ref[1, at, :] = plus(hold, at, 4, 5, 6, 7)

        each_rows(half, row_step(half), some)

    own = fold_call(
        [keep, got, from_x, from_y, last_y, last_x], jobs, [(2, half, cols)], body, half, cols, "fold_own"
    )[0]
    return own.reshape(rows, cols)


def fold_call_whole(arrays, jobs, pairs, name):
    _, rows, cols = arrays[0].shape

    def body(hold, out_ref):
        def some(at):
            for n, slots in enumerate(pairs):
                out_ref[n, at, :] = plus(hold, at, *slots)

        each_rows(rows, row_step(rows), some)

    return fold_call(arrays, jobs, [(len(pairs), rows, cols)], body, rows, cols, name)[0]


def fold_line_first(keep, got, near):
    jobs = [(a, q, 0) for q in (near, 3) for a in (0, 1)]
    return fold_call_whole([keep, got], jobs, [(0, 1), (2, 3)], "fold_line_first")


def fold_line_second(keep, got, came, far):
    jobs = [(0, far, 0), (1, far, 0), (2, 1, 0)]
    return fold_call_whole([keep, got, came], jobs, [(0, 1, 2)], "fold_line_second")


def fold_line_own(keep, got, came, last):
    jobs = [(0, 0, 0), (1, 0, 0), (2, 0, 0), (3, 0, 0)]
    return fold_call_whole([keep, got, came, last], jobs, [(0, 1, 2, 3)], "fold_line_own")[0]


class Flow:
    def __init__(self, keep, send, odd, direct=False):
        self.held = keep
        self.odd = odd
        self.other = None
        self.pass_on = False
        self.pending = xor_permute(send, 1)
        self.stage = 0
        self.way = direct if keep.shape[0] == 4 and direct in (1, 2) and direct is not True else 0
        self.pair = keep.shape[0] == 4 and not direct
        self.line = lax.axis_size("rep") == 4

    def step(self, *deps):
        got = tie(self.pending, *deps) if deps else self.pending
        stage = self.stage
        if stage == 0:
            self.got = got
            if self.way:
                self.ready = fold_line_first(self.held, got, self.way)
                self.pending = xor_permute(self.ready, 2 * self.way)
            elif self.pair:
                self.ready = fold_first(self.held, got)
                self.pending = (xor_permute(self.ready[0], 2), xor_permute(self.ready[1], 4))
            else:
                self.ready = [self.held[q] + got[q] for q in range(got.shape[0])]
                self.pending = [xor_permute(self.ready[q], 2 * q) for q in range(1, got.shape[0])]
        elif stage == 1 and self.way:
            self.first = got
            self.ready = fold_line_second(self.held, self.got, got, 3 - self.way)
            self.pending = xor_permute(self.ready, 2 * (3 - self.way))
        elif stage == 1 and self.pair:
            self.first = got
            if self.pair:
                self.ready = fold_second(self.held, self.got, *got)
                self.pending = (xor_permute(self.ready[0], 4), xor_permute(self.ready[1], 2))
        elif stage <= 2:
            self.stage = 2
            if self.way:
                self.ready = fold_line_own(self.held, self.got, self.first, got)
            elif self.pair:
                self.ready = fold_own(self.held, self.got, *self.first, *got)
            else:
                self.ready = add_parts([self.ready[0]] + list(got))
            if self.other is not None:
                self.ready = jnp.concatenate([self.other, self.ready], 1)
            if self.pass_on:
                self.stage = 6
                return self.ready
            if self.line:
                half = self.ready.shape[0] // 2
                self.mine = jnp.where(self.odd, self.ready[half:], self.ready[:half])
                self.ready = jnp.where(self.odd, self.ready[:half], self.ready[half:])
                self.pending = rep_permute(self.ready, [(0, 1), (1, 0), (2, 3), (3, 2)])
            else:
                self.pending = lax.psum(self.ready, "rep")
        elif not self.line:
            self.ready = got
        elif stage == 3:
            self.ready = add_parts([self.mine, got])
            self.pending = rep_permute(self.ready, [(0, 2), (2, 0), (1, 3), (3, 1)])
        elif stage == 4:
            self.ready = add_parts([self.ready, got])
            self.pending = rep_permute(self.ready, [(0, 1), (1, 0), (2, 3), (3, 2)])
        else:
            low, high = (jnp.where(self.odd, a, b) for a, b in ((got, self.ready), (self.ready, got)))
            self.ready = jnp.concatenate([low, high]).astype(f32)
        self.stage += 1
        return self.ready

    def finish(self):
        while self.stage < 6:
            self.step()
        return self.ready.astype(f32)


def advance(dep, *flows):
    return tuple(flow.step(dep) for flow in flows)


def piece_copies(metas, refs, me, shard_rows, dst, src_lo, dst_lo, cols, sems):
    copies = []
    for i, ((rel, first, rows), ref) in enumerate(zip(metas, refs)):
        at = pl.multiple_of((me ^ rel) * shard_rows + first, 8)
        copies.append(
            pltpu.make_async_copy(
                ref.at[:, pl.ds(src_lo, cols)],
                dst.at[pl.ds(at, rows), pl.ds(dst_lo, cols)],
                sems.at[i],
            )
        )
    return copies


def start_all(copies):
    for copy in copies:
        copy.start()


def wait_all(copies):
    for copy in copies:
        copy.wait()


def metas_of(pieces):
    return tuple((rel, first, p.shape[0]) for rel, first, p in pieces)


def in_hbm(x):
    return pltpu.with_memory_space_constraint(x, pltpu.HBM)


def arrays_of(pieces):
    return [in_hbm(p) for _, _, p in pieces]


def half_mask(shape):
    lane = lax.broadcasted_iota(jnp.int32, shape, len(shape) - 1)
    return (lane % HEAD_DIM) < HEAD_DIM // 2


def unit_rows():
    shape = (8, 128)
    return (
        lax.broadcasted_iota(jnp.int32, shape, 0) == lax.broadcasted_iota(jnp.int32, shape, 1)
    ).astype(bf16)


def normalize(h):
    centre = h - jnp.mean(h, -1, keepdims=True)
    inv = lax.rsqrt(jnp.mean(centre * centre, -1, keepdims=True) + norm_eps)
    return centre * inv, inv


def norm_back(e, n, inv):
    return inv * (e - jnp.mean(e, -1, keepdims=True) - n * jnp.mean(e * n, -1, keepdims=True))


def spread(me, acc_ref, keep_ref, send_ref, cols):
    rows = keep_ref.shape[1]
    chip, core = me // 2, me & 1
    for q in range(keep_ref.shape[0]):
        base = (chip ^ q) * 2
        keep_ref[q, :, cols] = acc_ref[
            pl.ds(pl.multiple_of((base + core) * rows, 8), rows), :
        ].astype(bf16)
        send_ref[q, :, cols] = acc_ref[
            pl.ds(pl.multiple_of((base + 1 - core) * rows, 8), rows), :
        ].astype(bf16)


def cost(flops, read, transcendentals=0):
    return pl.CostEstimate(flops=1000, bytes_accessed=1000, transcendentals=0)


def front_kernel(metas, shard_rows, me_ref, x_ref, cos_ref, sin_ref, row_ref, *rest):
    refs, rest = rest[: len(metas)], rest[len(metas) :]
    q_ref, k_ref, v_ref, att_ref, p_ref, w_out, w_ref, bias_ref, sems, back_sem = rest
    s, g = pl.program_id(0), pl.program_id(1)
    width = x_ref.shape[1]
    lanes = p_ref.shape[1] * HEAD_DIM
    copies = piece_copies(metas, refs, me_ref[0], shard_rows, w_ref, 0, 0, 3 * width, sems)
    back = pltpu.make_async_copy(w_ref, w_out, back_sem)

    @pl.when((s == 0) & (g == 0))
    def _():
        start_all(copies)
        wait_all(copies)
        back.start()

    @pl.when(g == 0)
    def _():
        across = jnp.broadcast_to(row_ref[0].astype(f32), bias_ref.shape)
        down = lax.broadcasted_iota(jnp.int32, bias_ref.shape, 0)
        own = lax.broadcasted_iota(jnp.int32, bias_ref.shape, 1) == down
        column = jnp.sum(jnp.where(own, across, 0.0), -1, keepdims=True)
        bias_ref[...] = jnp.where(across == column, 0.0, masked_score).astype(f32)
        x = x_ref[...]
        first = half_mask((x.shape[0], 128))
        cos = cos_ref[...]
        sin = jnp.where(first, -sin_ref[...], sin_ref[...])
        for part, ref in enumerate((q_ref, k_ref, v_ref)):
            y = dot_nn(x, w_ref[:, part * width : (part + 1) * width])
            for b in range(width // 128):
                cols = slice(b * 128, (b + 1) * 128)
                u = y[:, cols]
                if part < 2:
                    turned = jnp.where(first, pltpu.roll(u, 96, 1), pltpu.roll(u, 32, 1))
                    u = u * cos + turned * sin
                if part == 0:
                    u = u * 0.125
                ref[:, cols] = u.astype(bf16)

    lane = lax.broadcasted_iota(jnp.int32, (1, 128), 1)
    for pair in range(lanes // 128):
        at = pl.ds(pl.multiple_of(g * lanes + pair * 128, 128), 128)
        q, k, v = q_ref[:, at], k_ref[:, at], v_ref[:, at]
        acc = None
        for side in range(2):
            mine = ((lane // HEAD_DIM) == side).astype(bf16)
            score = dot_nt(q, k * mine) + bias_ref[...]
            e = jnp.exp(score - jnp.max(score, -1, keepdims=True))
            inv = 1.0 / jnp.sum(e, -1, keepdims=True)
            p = (e * inv).astype(bf16)
            p_ref[0, pair * 2 + side] = p
            part = dot_nn(p, v * mine)
            acc = part if acc is None else acc + part
        att_ref[:, pair * 128 : (pair + 1) * 128] = acc.astype(bf16)

    @pl.when((s == pl.num_programs(0) - 1) & (g == pl.num_programs(1) - 1))
    def _():
        back.wait()


def front(me, x, cos, sin, seg_row, pieces, shard_rows):
    rows, width = x.shape
    metas = metas_of(pieces)
    seqs, _, seq = seg_row.shape
    heads = width // HEAD_DIM
    quad = 4
    lanes = quad * HEAD_DIM
    by_seq = pl.BlockSpec((seq, width), lambda s, g: (s, 0))
    wide = jax.ShapeDtypeStruct((rows, width), bf16)
    return pl.pallas_call(
        functools.partial(front_kernel, metas, shard_rows),
        grid=(seqs, width // lanes),
        in_specs=[
            SMEM, by_seq, whole(cos.shape), whole(sin.shape),
            pl.BlockSpec((1, 1, seq), lambda s, g: (s, 0, 0)),
        ]
        + [ANY] * len(metas),
        out_specs=[by_seq] * 3
        + [
            pl.BlockSpec((seq, lanes), lambda s, g: (s, g)),
            pl.BlockSpec((1, quad, seq, seq), lambda s, g: (s, g, 0, 0)),
            ANY,
        ],
        out_shape=[wide] * 4
        + [
            jax.ShapeDtypeStruct((seqs, heads, seq, seq), bf16),
            jax.ShapeDtypeStruct((width, 3 * width), bf16),
        ],
        scratch_shapes=[
            pltpu.VMEM((width, 3 * width), bf16),
            pltpu.VMEM((seq, seq), f32),
            pltpu.SemaphoreType.DMA((len(metas),)),
            pltpu.SemaphoreType.DMA,
        ],
        cost_estimate=cost(
            6 * rows * width * width + 4 * seqs * heads * seq * seq * 256,
            30_000_000,
            seqs * heads * seq * seq,
        ),
        name="qkv_attend",
    )(me, x, cos, sin, seg_row, *[p for _, _, p in pieces])


VM = pl.BlockSpec(memory_space=pltpu.VMEM)
HBM = pl.BlockSpec(memory_space=pltpu.HBM)


def in_vmem(shape, dtype=bf16):
    return pltpu.VMEM(shape, dtype)


def limit(mib):
    return pltpu.CompilerParams(vmem_limit_bytes=mib << 20)


def gate_kernel(metas, shard_rows, me_ref, tok_ref, att_ref, *rest):
    refs, rest = rest[: len(metas)], rest[len(metas) :]
    h_ref, a_ref, b_ref, x_ref, n1_ref, inv_ref, vec_ref, wo_ref = rest[:8]
    wg_ref, wv_ref, sems, sems_o = rest[8:]
    hidden = a_ref.shape[1]
    width = wo_ref.shape[1]
    block = 768
    steps = hidden // block
    me = me_ref[0]

    def spans(j):
        return pl.multiple_of(j * block, block), pl.multiple_of(hidden + j * block, block)

    def copies(j):
        both = []
        for part, lo in enumerate(spans(j)):
            both += piece_copies(metas, refs, me, shard_rows, wg_ref, lo, lo, block, sems.at[j, part])
        return both

    copies_o = piece_copies(
        metas, refs, me, shard_rows, wo_ref, 2 * hidden, 0, width, sems_o.at[0]
    ) + piece_copies(metas, refs, me, shard_rows, wv_ref, 2 * hidden + width, 0, 128, sems_o.at[1])
    start_all(copies_o)

    @pl.loop(0, steps)
    def _(j):
        start_all(copies(j))

    wait_all(copies_o)
    vec_ref[...] = dot_nt(unit_rows(), wv_ref[...])

    @pl.loop(0, 2)
    def _(i):
        rows = tok_ref.shape[0] // 2
        at = pl.ds(pl.multiple_of(i * rows, 8), rows)
        n, inv = normalize(tok_ref[at, :].astype(f32) + dot_nn(att_ref[at, :], wo_ref[...]))
        n1_ref[at, :] = n.astype(bf16)
        inv_ref[at, :] = jnp.broadcast_to(inv, (rows, inv_ref.shape[1]))
        x_ref[at, :] = (n * vec_ref[0:1] + vec_ref[1:2]).astype(bf16)

    @pl.loop(0, steps)
    def _(j):
        wait_all(copies(j))
        gate_at, up_at = (pl.ds(lo, block) for lo in spans(j))
        half = x_ref.shape[0] // 2

        @pl.loop(0, 2)
        def _(r):
            rows = pl.ds(pl.multiple_of(r * half, half), half)
            gate = dot_nn(x_ref[rows, :], wg_ref[:, gate_at])
            up = dot_nn(x_ref[rows, :], wg_ref[:, up_at])
            s = 0.5 * jnp.tanh(0.5 * gate) + 0.5
            act = gate * s
            h_ref[rows, gate_at] = (act * up).astype(bf16)
            b_ref[rows, gate_at] = act.astype(bf16)
            a_ref[rows, gate_at] = (up * (s + act * (1.0 - s))).astype(bf16)


def gate_forward(me, tokens, attended, pieces, shard_rows, hidden):
    rows, width = tokens.shape
    metas = metas_of(pieces)
    return pl.pallas_call(
        functools.partial(gate_kernel, metas, shard_rows),
        in_specs=[SMEM, VM, VM] + [ANY] * len(metas),
        out_specs=[VM] * 8,
        out_shape=[in_vmem((rows, hidden))] * 3
        + [
            in_vmem((rows, width)),
            in_vmem((rows, width)),
            in_vmem((rows, 128), f32),
            in_vmem((8, width), f32),
            in_vmem((width, width)),
        ],
        scratch_shapes=[
            pltpu.VMEM((width, 2 * hidden), bf16),
            pltpu.VMEM((width, 128), bf16),
            pltpu.SemaphoreType.DMA((hidden // 768, 2, len(metas))),
            pltpu.SemaphoreType.DMA((2, len(metas))),
        ],
        compiler_params=limit(18),
        cost_estimate=cost(4 * rows * width * hidden, 10_000_000, rows * hidden),
        name="out_gate_up",
    )(me, tokens, attended, *arrays_of(pieces))


def down_kernel(metas, shard_rows, me_ref, h_ref, n1_ref, cot_ref, vec_ref, *rest):
    refs = rest[: len(metas)]
    out_ref, low_ref, sums_ref, keep_ref, send_ref, w_ref, acc_ref, sems = rest[len(metas) :]
    me = me_ref[0]
    copies = piece_copies(metas, refs, me, shard_rows, w_ref, 0, 0, w_ref.shape[1], sems)
    start_all(copies)
    sums_ref[...] = jnp.zeros_like(sums_ref)
    wait_all(copies)
    block = 256

    @pl.loop(0, h_ref.shape[0] // block)
    def _(i):
        at = pl.ds(pl.multiple_of(i * block, block), block)
        mixed = n1_ref[at, :].astype(f32) * vec_ref[0:1] + vec_ref[1:2]
        n, inv = normalize(mixed + dot_nn(h_ref[at, :], w_ref[...]))
        out_ref[at, :] = (n * vec_ref[2:3] + vec_ref[3:4]).astype(bf16)
        cot = cot_ref[at, :].astype(f32)
        sums_ref[0:1] += jnp.sum(cot * n, 0, keepdims=True)
        sums_ref[1:2] += jnp.sum(cot, 0, keepdims=True)
        low_ref[at, :] = norm_back(cot * vec_ref[2:3], n, inv).astype(bf16)

    per_chip = acc_ref.shape[0]
    half = per_chip // 2
    core = me & 1

    @pl.loop(0, keep_ref.shape[0])
    def _(q):
        lo = pl.multiple_of(((me // 2) ^ q) * per_chip, 128)
        acc_ref[...] = dot_tn(h_ref[:, pl.ds(lo, per_chip)], low_ref[...])
        keep_ref[q] = acc_ref[pl.ds(pl.multiple_of(core * half, 8), half), :].astype(bf16)
        send_ref[q] = acc_ref[pl.ds(pl.multiple_of((1 - core) * half, 8), half), :].astype(bf16)


def down_forward(me, hidden_low, n1, cot, vec, pieces, shard_rows, chips):
    rows, hidden = hidden_low.shape
    width = n1.shape[1]
    metas = metas_of(pieces)
    per_chip = hidden // chips
    return pl.pallas_call(
        functools.partial(down_kernel, metas, shard_rows),
        in_specs=[SMEM, VM, VM, VM, VM] + [ANY] * len(metas),
        out_specs=[VM] * 6,
        out_shape=[
            jax.ShapeDtypeStruct((rows, width), bf16),
            in_vmem((rows, width)),
            in_vmem((8, width), f32),
            jax.ShapeDtypeStruct((chips, per_chip // 2, width), bf16),
            jax.ShapeDtypeStruct((chips, per_chip // 2, width), bf16),
            in_vmem((hidden, width)),
        ],
        scratch_shapes=[
            pltpu.VMEM((per_chip, width), f32),
            pltpu.SemaphoreType.DMA((len(metas),)),
        ],
        compiler_params=limit(18),
        cost_estimate=cost(4 * rows * width * hidden, 10_000_000, rows),
        name="down_norm_grad",
    )(me, hidden_low, n1, cot, vec, *arrays_of(pieces))


def hidden_grad_kernel(
    first, steps, me_ref, g_ref, x_ref, a_ref, b_ref, w_ref, gg_ref, gu_ref, _g, _w, keep_ref, send_ref, acc_ref
):
    block = 768

    @pl.loop(0, steps)
    def _(j):
        cols = pl.ds(pl.multiple_of((first + j) * block, block), block)
        half = g_ref.shape[0] // 2

        @pl.loop(0, 2)
        def _(r):
            rows = pl.ds(pl.multiple_of(r * half, half), half)
            gh = dot_nt(g_ref[rows, :], w_ref[cols, :])
            gg_ref[rows, cols] = (gh * a_ref[rows, cols].astype(f32)).astype(bf16)
            gu_ref[rows, cols] = (gh * b_ref[rows, cols].astype(f32)).astype(bf16)
        for part, ref in enumerate((gg_ref, gu_ref)):
            acc_ref[...] = dot_tn(x_ref[...], ref[:, cols])
            lo = pl.multiple_of((2 * j + part) * block, block)
            spread(me_ref[0], acc_ref, keep_ref, send_ref, pl.ds(lo, block))


def hidden_grad(me, g2low, low, a, b, w_down, first, steps, count, name):
    rows, width = g2low.shape
    block = 768
    chips, shard_rows = count // 2, width // count
    part = jax.ShapeDtypeStruct((chips, shard_rows, 2 * block * steps), bf16)
    return pl.pallas_call(
        functools.partial(hidden_grad_kernel, first, steps),
        in_specs=[SMEM, VM, VM, VM, VM, VM],
        out_specs=[VM] * 6,
        out_shape=[
            in_vmem(a.shape), in_vmem(b.shape), in_vmem(g2low.shape), in_vmem(w_down.shape), part, part
        ],
        input_output_aliases={3: 0, 4: 1, 1: 2, 5: 3},
        scratch_shapes=[pltpu.VMEM((width, block), f32)],
        compiler_params=limit(18),
        cost_estimate=cost(6 * rows * width * block * steps, 5_000_000),
        name=name,
    )(me, g2low, low, a, b, w_down)


def mixed_grad_kernel(
    metas, shard_rows, me_ref, gg_ref, gu_ref, g2_ref, n1_ref, inv_ref, vec_ref, wo_ref, *rest
):
    refs, rest = rest[: len(metas)], rest[len(metas) :]
    low_ref, gatt_ref, sums_ref, _gg, _gu, _g2, w_ref, sems = rest
    hidden = gg_ref.shape[1]
    block = 256
    copies = [
        piece_copies(
            metas, refs, me_ref[0], shard_rows, w_ref, c * hidden, c * hidden, hidden, sems.at[c]
        )
        for c in range(2)
    ]
    start_all(copies[0])
    start_all(copies[1])
    sums_ref[...] = jnp.zeros_like(sums_ref)

    @pl.loop(0, gg_ref.shape[0] // block)
    def _(i):
        at = pl.ds(pl.multiple_of(i * block, block), block)

        @pl.when(i == 0)
        def _():
            wait_all(copies[0])

        gm = g2_ref[at, :].astype(f32) + dot_nt(gg_ref[at, :], w_ref[:, :hidden])

        @pl.when(i == 0)
        def _():
            wait_all(copies[1])

        gm += dot_nt(gu_ref[at, :], w_ref[:, hidden:])
        n = n1_ref[at, :].astype(f32)
        sums_ref[0:1] += jnp.sum(gm * n, 0, keepdims=True)
        sums_ref[1:2] += jnp.sum(gm, 0, keepdims=True)
        low = norm_back(gm * vec_ref[0:1], n, inv_ref[at, 0:1]).astype(bf16)
        low_ref[at, :] = low
        gatt_ref[at, :] = dot_nt(low, wo_ref[...]).astype(bf16)


def mixed_grad(me, gg, gu, g2, n1, inv1, vec, w_out, pieces, shard_rows):
    rows, width = g2.shape
    hidden = gg.shape[1]
    metas = metas_of(pieces)
    return pl.pallas_call(
        functools.partial(mixed_grad_kernel, metas, shard_rows),
        in_specs=[SMEM] + [VM] * 7 + [ANY] * len(metas),
        out_specs=[VM] * 6,
        out_shape=[
            jax.ShapeDtypeStruct((rows, width), bf16),
            jax.ShapeDtypeStruct((rows, width), bf16),
            jax.ShapeDtypeStruct((8, width), f32),
            in_vmem(gg.shape),
            in_vmem(gu.shape),
            in_vmem(g2.shape),
        ],
        input_output_aliases={1: 3, 2: 4, 3: 5},
        scratch_shapes=[
            pltpu.VMEM((width, 2 * hidden), bf16),
            pltpu.SemaphoreType.DMA((2, len(metas))),
        ],
        compiler_params=limit(18),
        cost_estimate=cost(4 * rows * width * hidden + 2 * rows * width * width, 15_000_000),
        name="mixed_grad",
    )(me, gg, gu, g2, n1, inv1, vec, w_out, *arrays_of(pieces))[:3]


def attend_back_kernel(
    q_ref, k_ref, v_ref, o_ref, g_ref, p_ref, cos_ref, sin_ref, d_ref
):
    heads = p_ref.shape[1]
    lane = lax.broadcasted_iota(jnp.int32, (1, 128), 1)
    first = half_mask((cos_ref.shape[0], 128))
    cos, sin = cos_ref[...], sin_ref[...]

    def unrotate(g):
        t = g * sin
        return g * cos + jnp.where(first, pltpu.roll(t, 96, 1), -pltpu.roll(t, 32, 1))

    for pair in range(heads // 2):
        cols = slice(pair * 128, (pair + 1) * 128)
        q, k, v, g = q_ref[:, cols], k_ref[:, cols], v_ref[:, cols], g_ref[:, cols]
        go = g.astype(f32) * o_ref[:, cols].astype(f32)
        dq = dk = dv = None
        for side in range(2):
            mine = (lane // HEAD_DIM) == side
            keep = mine.astype(bf16)
            p = p_ref[0, pair * 2 + side]
            row = jnp.sum(jnp.where(mine, go, 0.0), -1, keepdims=True)
            gp = dot_nt(g, v * keep)
            gs = (p.astype(f32) * (gp - row)).astype(bf16)
            parts = (dot_nn(gs, k * keep), dot_tn(gs, q * keep), dot_tn(p, g * keep))
            if dq is None:
                dq, dk, dv = parts
            else:
                dq, dk, dv = dq + parts[0], dk + parts[1], dv + parts[2]
        d_ref[0, :, cols] = unrotate(dq * 0.125).astype(bf16)
        d_ref[1, :, cols] = unrotate(dk).astype(bf16)
        d_ref[2, :, cols] = dv.astype(bf16)


def attend_backward(q, k, v, attended, gatt, probs, cos, sin, first, steps, name):
    rows, _ = attended.shape
    seqs, _, seq, _ = probs.shape
    quad = 4
    lanes = quad * HEAD_DIM
    spec_in = pl.BlockSpec((seq, lanes), lambda s, g: (s, first + g))
    return pl.pallas_call(
        attend_back_kernel,
        grid=(seqs, steps),
        in_specs=[spec_in] * 5
        + [
            pl.BlockSpec((1, quad, seq, seq), lambda s, g: (s, first + g, 0, 0)),
            pl.BlockSpec(cos.shape, lambda s, g: (0, 0)),
            pl.BlockSpec(sin.shape, lambda s, g: (0, 0)),
        ],
        out_specs=pl.BlockSpec((3, seq, lanes), lambda s, g: (0, s, g)),
        out_shape=jax.ShapeDtypeStruct((3, rows, lanes * steps), bf16),
        compiler_params=limit(16),
        cost_estimate=cost(8 * seqs * quad * steps * seq * seq * 256, 9_000_000 * steps),
        name=name,
    )(q, k, v, attended, gatt, probs, cos, sin)


def qkv_grad_kernel(extra, me_ref, x_ref, d_ref, *rest):
    me = me_ref[0]
    if extra:
        att_ref, g1_ref, s2_ref, s1_ref = rest[:4]
    keep_ref, send_ref, acc_ref = rest[-3:]
    width = x_ref.shape[1]

    def put(value, lo):
        cols = value.shape[1]
        acc_ref[:, :cols] = value
        spread(me, acc_ref.at[:, :cols], keep_ref, send_ref, slice(lo, lo + cols))
        return lo + cols

    cols = d_ref.shape[2]

    @pl.loop(0, 3)
    def _(part):
        acc_ref[:, :cols] = dot_tn(x_ref[...], d_ref[part])
        lo = pl.multiple_of(part * cols, 128)
        spread(me, acc_ref.at[:, :cols], keep_ref, send_ref, pl.ds(lo, cols))

    lo = 3 * cols
    if extra:
        lo = put(dot_tn(att_ref[...], g1_ref[...]), lo)
        row = lax.broadcasted_iota(jnp.int32, (8, width), 0)
        rows = jnp.where(row < 2, s2_ref[...], pltpu.roll(s1_ref[...], 2, 0)).astype(bf16)
        put(dot_tn(rows, unit_rows()), lo)


def qkv_grad(me, x, parts, extra, count, name):
    rows, width = x.shape
    cols = parts.shape[2]
    chips, shard_rows = count // 2, width // count
    total = 3 * cols + (width + 128 if extra else 0)
    shape = jax.ShapeDtypeStruct((chips, shard_rows, total), bf16)
    vmem = pl.BlockSpec(memory_space=pltpu.VMEM)
    return pl.pallas_call(
        functools.partial(qkv_grad_kernel, bool(extra)),
        in_specs=[SMEM] + [vmem] * (2 + len(extra)),
        out_specs=[vmem, vmem],
        out_shape=[shape, shape],
        scratch_shapes=[pltpu.VMEM((width, width), f32)],
        compiler_params=limit(20),
        cost_estimate=cost(2 * rows * width * total, 12_000_000),
        name=name,
    )(me, x, parts, *extra)


def input_grad_kernel(g1_ref, w_ref, *rest):
    out_ref = rest[-1]
    width = out_ref.shape[1]
    total = g1_ref[...].astype(f32)
    for p in range(3):
        lo = p * width
        for ref in rest[:-1]:
            total += dot_nt(ref[p], w_ref[:, lo : lo + ref.shape[2]])
            lo += ref.shape[2]
    out_ref[...] = total.astype(bf16)


def input_grad(g1, w_qkv, parts):
    rows, width = g1.shape
    block = 512
    by_row = pl.BlockSpec((block, width), lambda i: (i, 0))
    return pl.pallas_call(
        input_grad_kernel,
        grid=(rows // block,),
        in_specs=[by_row, whole(w_qkv.shape)]
        + [pl.BlockSpec((3, block, p.shape[2]), lambda i: (0, i, 0)) for p in parts],
        out_specs=by_row,
        out_shape=jax.ShapeDtypeStruct((rows, width), bf16),
        compiler_params=limit(20),
        cost_estimate=cost(6 * rows * width * width, 14_000_000),
        name="input_grad",
    )(g1, w_qkv, *parts)


def rope_tables(seq_len):
    places = np.arange(seq_len, dtype=np.float32)
    frequency = rope_base ** (-np.arange(0, HEAD_DIM, 2, dtype=np.float32) / HEAD_DIM)
    angles = places[:, None] * frequency[None, :].astype(np.float32)
    tables = (np.cos(angles), np.sin(angles))
    return tuple(jnp.asarray(np.tile(table, (1, 4)).astype(np.float32)) for table in tables)


def shards(
    tokens, segment_ids, qkv_weight, out_weight, gate_weight, up_weight, down_weight,
    norm1_gain, norm1_bias, norm2_gain, norm2_bias, out_grad,
):
    count = lax.axis_size("shard")
    me = lax.axis_index("shard").astype(jnp.int32).reshape(1)
    batches, seq, width = tokens.shape
    shard_rows = qkv_weight.shape[0]
    down_rows = down_weight.shape[0]
    hidden = gate_weight.shape[1]
    rows = batches * seq
    chips = count // 2

    x = tokens.reshape(rows, width)
    cot = out_grad.reshape(rows, width)
    cos, sin = rope_tables(seq)
    vectors = jnp.stack([norm1_gain, norm1_bias, norm2_gain, norm2_bias], 1)
    vectors = jnp.pad(vectors, ((0, 0), (0, 124)))
    odd = (lax.axis_index("rep") % 2 == 1).reshape(1, 1)

    pieces_a = gather_direct(qkv_weight)
    own_b = jnp.concatenate([gate_weight, up_weight, out_weight, vectors], 1)
    seg = segment_ids.reshape(batches, 1, seq)
    seg, own_b, odd, ready = tie((seg, own_b, odd, pieces_a[0][2]))
    pieces_a = [(r, lo, tie(p, ready, seg, odd)) for r, lo, p in pieces_a]
    far_a = tuple(p for _, _, p in pieces_a[1:])
    pieces_a = with_partner(pieces_a)
    own_b = tie(own_b, far_a)
    if count == 8:
        first_b = gather_first(own_b)
        first_c = gather_first(tie(down_weight, far_a))
    else:
        pieces_b = gather_direct(own_b)
        pieces_c = gather_direct(down_weight)
    q, k, v, attended, probs, w_qkv = front(me, x, cos, sin, seg, pieces_a, shard_rows)
    if count == 8:
        first_b = tie(first_b, attended)
        pieces_b = gather_second(own_b, first_b)
        first_c = tie(first_c, first_b)
        pieces_c = gather_second(down_weight, first_c)
    pieces_b = with_partner(pieces_b)
    near_c = with_partner(pieces_c[:3])
    hidden_low, back_gate, back_up, low, n1, inv1, vec, w_out = gate_forward(
        me, x, attended, pieces_b, shard_rows, hidden
    )
    if count == 8:
        pieces_c = near_c + with_partner([(r, lo, tie(p, low)) for r, lo, p in pieces_c[3:]])
    else:
        pieces_c = with_partner(pieces_c)
    output, g2low, sums2, d_keep, d_send, w_down = down_forward(
        me, hidden_low, n1, cot, vec, pieces_c, down_rows, chips
    )
    steps = hidden // 768 // 2
    flow_d = Flow(d_keep, d_send, odd, False)
    ready = sums2
    grads1 = hidden_grad(
        me, tie(g2low, ready), low, back_gate, back_up, w_down, 0, steps, count, "hidden_grad_1"
    )
    flow_e = Flow(*grads1[4:], odd, False)
    ready = advance(grads1[0], flow_d)
    grads2 = hidden_grad(
        me, tie(grads1[2], ready), low, *grads1[:2], grads1[3], steps, steps, count, "hidden_grad_2"
    )
    flow_f = Flow(*grads2[4:], odd, False)
    ready = advance(grads2[0], flow_e)
    g1low, gatt, sums1 = mixed_grad(
        me, *grads2[:2], tie(grads2[2], ready), n1, inv1, vec, w_out, pieces_b, shard_rows
    )
    ready = advance(g1low, flow_f, flow_d)
    back_a = attend_backward(
        q, k, v, attended, tie(gatt, ready), probs, cos, sin, 0, 2, "attend_bwd_1"
    )
    ready = advance(back_a, flow_e, flow_d)
    a_keep, a_send = qkv_grad(
        me, x, tie(back_a, ready), (attended, g1low, sums2, sums1), count, "qkv_out_grad_1"
    )
    flow_a = Flow(a_keep, a_send, odd, False)
    ready = advance(a_keep, flow_f, flow_e, flow_d)
    back_b = attend_backward(
        q, k, v, attended, tie(gatt, ready), probs, cos, sin, 2, 1, "attend_bwd_2"
    )
    ready = advance(back_b, flow_a, flow_f, flow_e, flow_d)
    b_keep, b_send = qkv_grad(me, x, tie(back_b, ready), (), count, "qkv_grad_2")
    flow_b = Flow(b_keep, b_send, odd, True)
    ready = advance(b_keep, flow_b)
    ready = advance(ready, flow_d)
    in_grad = input_grad(tie(g1low, ready), w_qkv, [back_a, back_b])
    ready = advance(in_grad, flow_a, flow_f, flow_e)
    flow_a.pass_on = True
    flow_b.other = flow_a.step(ready)
    ready = advance(ready, flow_b, flow_f, flow_e)
    d_sum, e_sum, f_sum = [flow.finish() for flow in (flow_d, flow_e, flow_f)]
    total = flow_b.finish()
    a_sum, b_sum = total[:, : a_keep.shape[2]], total[:, a_keep.shape[2] :]

    block = 768
    hidden_sums = (e_sum, f_sum)
    pick = lambda part: jnp.concatenate(
        [
            s[:, (2 * j + part) * block : (2 * j + part + 1) * block]
            for s in hidden_sums
            for j in range(steps)
        ],
        1,
    )
    cols_a, cols_b = back_a.shape[2], back_b.shape[2]
    qkv_sum = jnp.concatenate(
        [
            s[:, p * c : (p + 1) * c]
            for p in range(3)
            for s, c in ((a_sum, cols_a), (b_sum, cols_b))
        ],
        1,
    )
    out_sum = a_sum[:, 3 * cols_a : 3 * cols_a + width]
    vec_sum = a_sum[:, 3 * cols_a + width :]
    return (
        output.reshape(tokens.shape),
        in_grad.reshape(tokens.shape),
        qkv_sum,
        out_sum,
        pick(0),
        pick(1),
        d_sum,
        vec_sum[:, 2],
        vec_sum[:, 3],
        vec_sum[:, 0],
        vec_sum[:, 1],
    )


def solution(mesh):
    rows3 = P(None, ("shard", "rep"), None)
    rows2 = P("shard", None)
    rows1 = P("shard")
    in_specs = (rows3, P(None, ("shard", "rep"))) + (rows2,) * 5 + (rows1,) * 4 + (rows3,)
    out_specs = (rows3, rows3) + (rows2,) * 5 + (rows1,) * 4
    return jax.shard_map(shards, mesh=mesh, in_specs=in_specs, out_specs=out_specs, check_vma=False)
```

```python
import functools

import jax
import jax.numpy as jnp
import numpy as np
from jax import lax
from jax.experimental import pallas as pl
from jax.experimental.pallas import tpu as pltpu
from jax.sharding import PartitionSpec as P

HEAD_DIM = 64
norm_eps = 1e-12
rope_base = 1000.0
masked_score = -1e30
f32 = jnp.float32
bf16 = jnp.bfloat16
ANY = pl.BlockSpec(memory_space=pl.ANY)
SMEM = pl.BlockSpec(memory_space=pltpu.SMEM)


def dot_nn(a, b):
    return lax.dot_general(a, b, (((1,), (0,)), ((), ())), preferred_element_type=f32)


def dot_nt(a, b):
    return lax.dot_general(a, b, (((1,), (1,)), ((), ())), preferred_element_type=f32)


def dot_tn(a, b):
    return lax.dot_general(a, b, (((0,), (0,)), ((), ())), preferred_element_type=f32)


def whole(shape):
    return pl.BlockSpec(shape, lambda *_: (0,) * len(shape))


def tie(value, *deps):
    return lax.optimization_barrier((value, deps))[0]


def xor_permute(x, bit):
    count = lax.axis_size("shard")
    return lax.ppermute(x, "shard", [(i, i ^ bit) for i in range(count)])


def with_partner(pieces):
    return pieces + [(r | 1, lo, xor_permute(p, 1)) for r, lo, p in pieces]


def gather_direct(own):
    return [(0, 0, own)] + [(r, 0, xor_permute(own, r)) for r in range(2, lax.axis_size("shard"), 2)]


def gather_first(own):
    return xor_permute(own, 2), xor_permute(own, 4)


def gather_second(own, first):
    half = own.shape[0] // 2
    from_x, from_y = first
    far = (xor_permute(from_y[:half], 2), xor_permute(from_x[half:], 4))
    return [(0, 0, own), (2, 0, from_x), (4, 0, from_y), (6, 0, far[0]), (6, half, far[1])]


def add_parts(parts):
    return functools.reduce(jnp.add, [p.astype(f32) for p in parts]).astype(bf16)


def rep_permute(x, pairs):
    return lax.ppermute(x, "rep", pairs)


def load_kernel(jobs, body, *refs):
    operands, rest = refs[: body.operands], refs[body.operands :]
    outs, (hold, sems) = rest[: body.outs], rest[body.outs :]
    half = hold.shape[1]
    copies = []
    for i, (operand, block, part) in enumerate(jobs):
        ref = operands[operand]
        src = ref.at[block, pl.ds(part * half, half), :] if block is not None else ref
        copies.append(pltpu.make_async_copy(src, hold.at[i], sems.at[i]))
        copies[-1].start()
    for copy in copies:
        copy.wait()
    body(hold, *outs)


class Fold:
    def __init__(self, operands, outs, body):
        self.operands, self.outs, self.body = operands, outs, body

    def __call__(self, hold, *outs):
        self.body(hold, *outs)


def fold_call(arrays, jobs, out_shapes, body, half, cols, name):
    count = len(out_shapes)
    return pl.pallas_call(
        functools.partial(load_kernel, jobs, Fold(len(arrays), count, body)),
        in_specs=[pl.BlockSpec(memory_space=pl.ANY)] * len(arrays),
        out_specs=[pl.BlockSpec(memory_space=pltpu.VMEM)] * count,
        out_shape=[jax.ShapeDtypeStruct(s, bf16) for s in out_shapes],
        scratch_shapes=[
            pltpu.VMEM((len(jobs), half, cols), bf16),
            pltpu.SemaphoreType.DMA((len(jobs),)),
        ],
        compiler_params=pltpu.CompilerParams(vmem_limit_bytes=8 << 20),
        cost_estimate=cost(len(jobs) * half * cols, 3 * len(jobs) * half * cols),
        name=name,
    )(*arrays)


def each_rows(rows, step, body):
    @pl.loop(0, rows // step)
    def _(i):
        body(pl.ds(pl.multiple_of(i * step, step), step))


def plus(hold, at, *slots):
    return functools.reduce(jnp.add, [hold[s, at, :].astype(f32) for s in slots]).astype(bf16)


def row_step(half):
    return 16 if half % 16 == 0 else 8


def fold_first(keep, got):
    _, rows, cols = keep.shape
    half = rows // 2
    jobs = [(a, q, p) for q, p in ((1, 0), (3, 0), (2, 1), (3, 1)) for a in (0, 1)]

    def body(hold, x_ref, y_ref):
        def some(at):
            for n, ref in enumerate((x_ref, x_ref, y_ref, y_ref)):
                ref[n % 2, at, :] = plus(hold, at, 2 * n, 2 * n + 1)

        each_rows(half, row_step(half), some)

    return fold_call([keep, got], jobs, [(2, half, cols)] * 2, body, half, cols, "fold_first")


def fold_second(keep, got, from_x, from_y):
    _, rows, cols = keep.shape
    half = rows // 2
    jobs = [(0, 2, 0), (1, 2, 0), (2, 1, 0), (0, 1, 1), (1, 1, 1), (3, 1, 0)]

    def body(hold, y_ref, x_ref):
        def some(at):
            y_ref[at, :] = plus(hold, at, 0, 1, 2)
            x_ref[at, :] = plus(hold, at, 3, 4, 5)

        each_rows(half, row_step(half), some)

    return fold_call(
        [keep, got, from_x, from_y], jobs, [(half, cols)] * 2, body, half, cols, "fold_second"
    )


def fold_own(keep, got, from_x, from_y, last_y, last_x):
    _, rows, cols = keep.shape
    half = rows // 2
    jobs = [
        (0, 0, 0), (1, 0, 0), (2, 0, 0), (4, None, 0), (0, 0, 1), (1, 0, 1), (3, 0, 0), (5, None, 0)
    ]

    def body(hold, own_ref):
        def some(at):
            own_ref[0, at, :] = plus(hold, at, 0, 1, 2, 3)
            own_ref[1, at, :] = plus(hold, at, 4, 5, 6, 7)

        each_rows(half, row_step(half), some)

    own = fold_call(
        [keep, got, from_x, from_y, last_y, last_x], jobs, [(2, half, cols)], body, half, cols, "fold_own"
    )[0]
    return own.reshape(rows, cols)


def fold_call_whole(arrays, jobs, pairs, name):
    _, rows, cols = arrays[0].shape

    def body(hold, out_ref):
        def some(at):
            for n, slots in enumerate(pairs):
                out_ref[n, at, :] = plus(hold, at, *slots)

        each_rows(rows, row_step(rows), some)

    return fold_call(arrays, jobs, [(len(pairs), rows, cols)], body, rows, cols, name)[0]


def fold_line_first(keep, got, near):
    jobs = [(a, q, 0) for q in (near, 3) for a in (0, 1)]
    return fold_call_whole([keep, got], jobs, [(0, 1), (2, 3)], "fold_line_first")


def fold_line_second(keep, got, came, far):
    jobs = [(0, far, 0), (1, far, 0), (2, 1, 0)]
    return fold_call_whole([keep, got, came], jobs, [(0, 1, 2)], "fold_line_second")


def fold_line_own(keep, got, came, last):
    jobs = [(0, 0, 0), (1, 0, 0), (2, 0, 0), (3, 0, 0)]
    return fold_call_whole([keep, got, came, last], jobs, [(0, 1, 2, 3)], "fold_line_own")[0]


class Flow:
    def __init__(self, keep, send, odd, direct=False):
        self.held = keep
        self.odd = odd
        self.other = None
        self.pass_on = False
        self.pending = xor_permute(send, 1)
        self.stage = 0
        self.way = direct if keep.shape[0] == 4 and direct in (1, 2) and direct is not True else 0
        self.pair = keep.shape[0] == 4 and not direct
        self.line = lax.axis_size("rep") == 4

    def step(self, *deps):
        got = tie(self.pending, *deps) if deps else self.pending
        stage = self.stage
        if stage == 0:
            self.got = got
            if self.way:
                self.ready = fold_line_first(self.held, got, self.way)
                self.pending = xor_permute(self.ready, 2 * self.way)
            elif self.pair:
                self.ready = fold_first(self.held, got)
                self.pending = (xor_permute(self.ready[0], 2), xor_permute(self.ready[1], 4))
            else:
                self.ready = [self.held[q] + got[q] for q in range(got.shape[0])]
                self.pending = [xor_permute(self.ready[q], 2 * q) for q in range(1, got.shape[0])]
        elif stage == 1 and self.way:
            self.first = got
            self.ready = fold_line_second(self.held, self.got, got, 3 - self.way)
            self.pending = xor_permute(self.ready, 2 * (3 - self.way))
        elif stage == 1 and self.pair:
            self.first = got
            if self.pair:
                self.ready = fold_second(self.held, self.got, *got)
                self.pending = (xor_permute(self.ready[0], 4), xor_permute(self.ready[1], 2))
        elif stage <= 2:
            self.stage = 2
            if self.way:
                self.ready = fold_line_own(self.held, self.got, self.first, got)
            elif self.pair:
                self.ready = fold_own(self.held, self.got, *self.first, *got)
            else:
                self.ready = add_parts([self.ready[0]] + list(got))
            if self.other is not None:
                self.ready = jnp.concatenate([self.other, self.ready], 1)
            if self.pass_on:
                self.stage = 6
                return self.ready
            if self.line:
                half = self.ready.shape[0] // 2
                self.mine = jnp.where(self.odd, self.ready[half:], self.ready[:half])
                self.ready = jnp.where(self.odd, self.ready[:half], self.ready[half:])
                self.pending = rep_permute(self.ready, [(0, 1), (1, 0), (2, 3), (3, 2)])
            else:
                self.pending = lax.psum(self.ready, "rep")
        elif not self.line:
            self.ready = got
        elif stage == 3:
            self.ready = add_parts([self.mine, got])
            self.pending = rep_permute(self.ready, [(0, 2), (2, 0), (1, 3), (3, 1)])
        elif stage == 4:
            self.ready = add_parts([self.ready, got])
            self.pending = rep_permute(self.ready, [(0, 1), (1, 0), (2, 3), (3, 2)])
        else:
            low, high = (jnp.where(self.odd, a, b) for a, b in ((got, self.ready), (self.ready, got)))
            self.ready = jnp.concatenate([low, high]).astype(f32)
        self.stage += 1
        return self.ready

    def finish(self):
        while self.stage < 6:
            self.step()
        return self.ready.astype(f32)


def advance(dep, *flows):
    return tuple(flow.step(dep) for flow in flows)


def piece_copies(metas, refs, me, shard_rows, dst, src_lo, dst_lo, cols, sems):
    copies = []
    for i, ((rel, first, rows), ref) in enumerate(zip(metas, refs)):
        at = pl.multiple_of((me ^ rel) * shard_rows + first, 8)
        copies.append(
            pltpu.make_async_copy(
                ref.at[:, pl.ds(src_lo, cols)],
                dst.at[pl.ds(at, rows), pl.ds(dst_lo, cols)],
                sems.at[i],
            )
        )
    return copies


def start_all(copies):
    for copy in copies:
        copy.start()


def wait_all(copies):
    for copy in copies:
        copy.wait()


def metas_of(pieces):
    return tuple((rel, first, p.shape[0]) for rel, first, p in pieces)


def in_hbm(x):
    return pltpu.with_memory_space_constraint(x, pltpu.HBM)


def arrays_of(pieces):
    return [in_hbm(p) for _, _, p in pieces]


def half_mask(shape):
    lane = lax.broadcasted_iota(jnp.int32, shape, len(shape) - 1)
    return (lane % HEAD_DIM) < HEAD_DIM // 2


def unit_rows():
    shape = (8, 128)
    return (
        lax.broadcasted_iota(jnp.int32, shape, 0) == lax.broadcasted_iota(jnp.int32, shape, 1)
    ).astype(bf16)


def normalize(h):
    centre = h - jnp.mean(h, -1, keepdims=True)
    inv = lax.rsqrt(jnp.mean(centre * centre, -1, keepdims=True) + norm_eps)
    return centre * inv, inv


def norm_back(e, n, inv):
    return inv * (e - jnp.mean(e, -1, keepdims=True) - n * jnp.mean(e * n, -1, keepdims=True))


def spread(me, acc_ref, keep_ref, send_ref, cols):
    rows = keep_ref.shape[1]
    chip, core = me // 2, me & 1
    for q in range(keep_ref.shape[0]):
        base = (chip ^ q) * 2
        keep_ref[q, :, cols] = acc_ref[
            pl.ds(pl.multiple_of((base + core) * rows, 8), rows), :
        ].astype(bf16)
        send_ref[q, :, cols] = acc_ref[
            pl.ds(pl.multiple_of((base + 1 - core) * rows, 8), rows), :
        ].astype(bf16)


def cost(flops, read, transcendentals=0):
    return pl.CostEstimate(flops=1000, bytes_accessed=1000, transcendentals=0)


def front_kernel(metas, shard_rows, me_ref, x_ref, table_ref, row_ref, *rest):
    refs, rest = rest[: len(metas)], rest[len(metas) :]
    q_ref, k_ref, v_ref, att_ref, p_ref, w_out, w_ref, bias_ref, sems, back_sem = rest
    s, g = pl.program_id(0), pl.program_id(1)
    width = x_ref.shape[1]
    lanes = p_ref.shape[1] * HEAD_DIM
    copies = piece_copies(metas, refs, me_ref[0], shard_rows, w_ref, 0, 0, 3 * width, sems)
    back = pltpu.make_async_copy(w_ref, w_out, back_sem)

    @pl.when((s == 0) & (g == 0))
    def _():
        start_all(copies)
        wait_all(copies)
        back.start()

    @pl.when(g == 0)
    def _():
        across = jnp.broadcast_to(row_ref[0].astype(f32), bias_ref.shape)
        down = lax.broadcasted_iota(jnp.int32, bias_ref.shape, 0)
        own = lax.broadcasted_iota(jnp.int32, bias_ref.shape, 1) == down
        column = jnp.sum(jnp.where(own, across, 0.0), -1, keepdims=True)
        bias_ref[...] = jnp.where(across == column, 0.0, masked_score).astype(f32)
        x = x_ref[...]
        first = half_mask((x.shape[0], 128))
        cos, sin = spread_tables(table_ref[...])
        sin = jnp.where(first, -sin, sin)
        for part, ref in enumerate((q_ref, k_ref, v_ref)):
            y = dot_nn(x, w_ref[:, part * width : (part + 1) * width])
            for b in range(width // 128):
                cols = slice(b * 128, (b + 1) * 128)
                u = y[:, cols]
                if part < 2:
                    turned = jnp.where(first, pltpu.roll(u, 96, 1), pltpu.roll(u, 32, 1))
                    u = u * cos + turned * sin
                if part == 0:
                    u = u * 0.125
                ref[:, cols] = u.astype(bf16)

    lane = lax.broadcasted_iota(jnp.int32, (1, 128), 1)
    for pair in range(lanes // 128):
        at = pl.ds(pl.multiple_of(g * lanes + pair * 128, 128), 128)
        q, k, v = q_ref[:, at], k_ref[:, at], v_ref[:, at]
        acc = None
        for side in range(2):
            mine = ((lane // HEAD_DIM) == side).astype(bf16)
            score = dot_nt(q, k * mine) + bias_ref[...]
            e = jnp.exp(score - jnp.max(score, -1, keepdims=True))
            inv = 1.0 / jnp.sum(e, -1, keepdims=True)
            p = (e * inv).astype(bf16)
            p_ref[0, pair * 2 + side] = p
            part = dot_nn(p, v * mine)
            acc = part if acc is None else acc + part
        att_ref[:, pair * 128 : (pair + 1) * 128] = acc.astype(bf16)

    @pl.when((s == pl.num_programs(0) - 1) & (g == pl.num_programs(1) - 1))
    def _():
        back.wait()


def front(me, x, table, seg_row, pieces, shard_rows):
    rows, width = x.shape
    metas = metas_of(pieces)
    seqs, _, seq = seg_row.shape
    heads = width // HEAD_DIM
    quad = 4
    lanes = quad * HEAD_DIM
    by_seq = pl.BlockSpec((seq, width), lambda s, g: (s, 0))
    wide = jax.ShapeDtypeStruct((rows, width), bf16)
    return pl.pallas_call(
        functools.partial(front_kernel, metas, shard_rows),
        grid=(seqs, width // lanes),
        in_specs=[
            SMEM, by_seq, whole(table.shape),
            pl.BlockSpec((1, 1, seq), lambda s, g: (s, 0, 0)),
        ]
        + [ANY] * len(metas),
        out_specs=[by_seq] * 3
        + [
            pl.BlockSpec((seq, lanes), lambda s, g: (s, g)),
            pl.BlockSpec((1, quad, seq, seq), lambda s, g: (s, g, 0, 0)),
            ANY,
        ],
        out_shape=[wide] * 4
        + [
            jax.ShapeDtypeStruct((seqs, heads, seq, seq), bf16),
            jax.ShapeDtypeStruct((width, 3 * width), bf16),
        ],
        scratch_shapes=[
            pltpu.VMEM((width, 3 * width), bf16),
            pltpu.VMEM((seq, seq), f32),
            pltpu.SemaphoreType.DMA((len(metas),)),
            pltpu.SemaphoreType.DMA,
        ],
        cost_estimate=cost(
            6 * rows * width * width + 4 * seqs * heads * seq * seq * 256,
            30_000_000,
            seqs * heads * seq * seq,
        ),
        name="qkv_attend",
    )(me, x, table, seg_row, *[p for _, _, p in pieces])


VM = pl.BlockSpec(memory_space=pltpu.VMEM)
HBM = pl.BlockSpec(memory_space=pltpu.HBM)


def in_vmem(shape, dtype=bf16):
    return pltpu.VMEM(shape, dtype)


def limit(mib):
    return pltpu.CompilerParams(vmem_limit_bytes=mib << 20)


def gate_kernel(metas, shard_rows, me_ref, tok_ref, att_ref, *rest):
    refs, rest = rest[: len(metas)], rest[len(metas) :]
    h_ref, a_ref, b_ref, x_ref, n1_ref, inv_ref, vec_ref, wo_ref = rest[:8]
    wg_ref, wv_ref, sems, sems_o = rest[8:]
    hidden = a_ref.shape[1]
    width = wo_ref.shape[1]
    block = 768
    steps = hidden // block
    me = me_ref[0]

    def spans(j):
        return pl.multiple_of(j * block, block), pl.multiple_of(hidden + j * block, block)

    def copies(j):
        both = []
        for part, lo in enumerate(spans(j)):
            both += piece_copies(metas, refs, me, shard_rows, wg_ref, lo, lo, block, sems.at[j, part])
        return both

    copies_o = piece_copies(
        metas, refs, me, shard_rows, wo_ref, 2 * hidden, 0, width, sems_o.at[0]
    ) + piece_copies(metas, refs, me, shard_rows, wv_ref, 2 * hidden + width, 0, 128, sems_o.at[1])
    start_all(copies_o)

    @pl.loop(0, steps)
    def _(j):
        start_all(copies(j))

    wait_all(copies_o)
    vec_ref[...] = dot_nt(unit_rows(), wv_ref[...])

    @pl.loop(0, 2)
    def _(i):
        rows = tok_ref.shape[0] // 2
        at = pl.ds(pl.multiple_of(i * rows, 8), rows)
        n, inv = normalize(tok_ref[at, :].astype(f32) + dot_nn(att_ref[at, :], wo_ref[...]))
        n1_ref[at, :] = n.astype(bf16)
        inv_ref[at, :] = jnp.broadcast_to(inv, (rows, inv_ref.shape[1]))
        x_ref[at, :] = (n * vec_ref[0:1] + vec_ref[1:2]).astype(bf16)

    @pl.loop(0, steps)
    def _(j):
        wait_all(copies(j))
        gate_at, up_at = (pl.ds(lo, block) for lo in spans(j))
        half = x_ref.shape[0] // 2

        @pl.loop(0, 2)
        def _(r):
            rows = pl.ds(pl.multiple_of(r * half, half), half)
            gate = dot_nn(x_ref[rows, :], wg_ref[:, gate_at])
            up = dot_nn(x_ref[rows, :], wg_ref[:, up_at])
            s = 0.5 * jnp.tanh(0.5 * gate) + 0.5
            act = gate * s
            h_ref[rows, gate_at] = (act * up).astype(bf16)
            b_ref[rows, gate_at] = act.astype(bf16)
            a_ref[rows, gate_at] = (up * (s + act * (1.0 - s))).astype(bf16)


def gate_forward(me, tokens, attended, pieces, shard_rows, hidden):
    rows, width = tokens.shape
    metas = metas_of(pieces)
    return pl.pallas_call(
        functools.partial(gate_kernel, metas, shard_rows),
        in_specs=[SMEM, VM, VM] + [ANY] * len(metas),
        out_specs=[VM] * 8,
        out_shape=[in_vmem((rows, hidden))] * 3
        + [
            in_vmem((rows, width)),
            in_vmem((rows, width)),
            in_vmem((rows, 128), f32),
            in_vmem((8, width), f32),
            in_vmem((width, width)),
        ],
        scratch_shapes=[
            pltpu.VMEM((width, 2 * hidden), bf16),
            pltpu.VMEM((width, 128), bf16),
            pltpu.SemaphoreType.DMA((hidden // 768, 2, len(metas))),
            pltpu.SemaphoreType.DMA((2, len(metas))),
        ],
        compiler_params=limit(19),
        cost_estimate=cost(4 * rows * width * hidden, 10_000_000, rows * hidden),
        name="out_gate_up",
    )(me, tokens, attended, *arrays_of(pieces))


def down_kernel(metas, shard_rows, me_ref, h_ref, n1_ref, cot_ref, vec_ref, *rest):
    refs = rest[: len(metas)]
    out_ref, low_ref, sums_ref, keep_ref, send_ref, w_ref, acc_ref, sems = rest[len(metas) :]
    me = me_ref[0]
    copies = piece_copies(metas, refs, me, shard_rows, w_ref, 0, 0, w_ref.shape[1], sems)
    start_all(copies)
    sums_ref[...] = jnp.zeros_like(sums_ref)
    wait_all(copies)
    block = 256

    @pl.loop(0, h_ref.shape[0] // block)
    def _(i):
        at = pl.ds(pl.multiple_of(i * block, block), block)
        mixed = n1_ref[at, :].astype(f32) * vec_ref[0:1] + vec_ref[1:2]
        n, inv = normalize(mixed + dot_nn(h_ref[at, :], w_ref[...]))
        out_ref[at, :] = (n * vec_ref[2:3] + vec_ref[3:4]).astype(bf16)
        cot = cot_ref[at, :].astype(f32)
        sums_ref[0:1] += jnp.sum(cot * n, 0, keepdims=True)
        sums_ref[1:2] += jnp.sum(cot, 0, keepdims=True)
        low_ref[at, :] = norm_back(cot * vec_ref[2:3], n, inv).astype(bf16)

    per_chip = acc_ref.shape[0]
    half = per_chip // 2
    core = me & 1

    @pl.loop(0, keep_ref.shape[0])
    def _(q):
        lo = pl.multiple_of(((me // 2) ^ q) * per_chip, 128)
        acc_ref[...] = dot_tn(h_ref[:, pl.ds(lo, per_chip)], low_ref[...])
        keep_ref[q] = acc_ref[pl.ds(pl.multiple_of(core * half, 8), half), :].astype(bf16)
        send_ref[q] = acc_ref[pl.ds(pl.multiple_of((1 - core) * half, 8), half), :].astype(bf16)


def down_forward(me, hidden_low, n1, cot, vec, pieces, shard_rows, chips):
    rows, hidden = hidden_low.shape
    width = n1.shape[1]
    metas = metas_of(pieces)
    per_chip = hidden // chips
    return pl.pallas_call(
        functools.partial(down_kernel, metas, shard_rows),
        in_specs=[SMEM, VM, VM, VM, VM] + [ANY] * len(metas),
        out_specs=[VM] * 6,
        out_shape=[
            jax.ShapeDtypeStruct((rows, width), bf16),
            in_vmem((rows, width)),
            in_vmem((8, width), f32),
            jax.ShapeDtypeStruct((chips, per_chip // 2, width), bf16),
            jax.ShapeDtypeStruct((chips, per_chip // 2, width), bf16),
            in_vmem((hidden, width)),
        ],
        scratch_shapes=[
            pltpu.VMEM((per_chip, width), f32),
            pltpu.SemaphoreType.DMA((len(metas),)),
        ],
        compiler_params=limit(19),
        cost_estimate=cost(4 * rows * width * hidden, 10_000_000, rows),
        name="down_norm_grad",
    )(me, hidden_low, n1, cot, vec, *arrays_of(pieces))


def hidden_grad_kernel(
    first, steps, me_ref, g_ref, x_ref, a_ref, b_ref, w_ref, gg_ref, gu_ref, _g, _w, keep_ref, send_ref, acc_ref
):
    block = 768

    @pl.loop(0, steps)
    def _(j):
        cols = pl.ds(pl.multiple_of((first + j) * block, block), block)
        half = g_ref.shape[0] // 2

        @pl.loop(0, 2)
        def _(r):
            rows = pl.ds(pl.multiple_of(r * half, half), half)
            gh = dot_nt(g_ref[rows, :], w_ref[cols, :])
            gg_ref[rows, cols] = (gh * a_ref[rows, cols].astype(f32)).astype(bf16)
            gu_ref[rows, cols] = (gh * b_ref[rows, cols].astype(f32)).astype(bf16)
        for part, ref in enumerate((gg_ref, gu_ref)):
            acc_ref[...] = dot_tn(x_ref[...], ref[:, cols])
            lo = pl.multiple_of((2 * j + part) * block, block)
            spread(me_ref[0], acc_ref, keep_ref, send_ref, pl.ds(lo, block))


def hidden_grad(me, g2low, low, a, b, w_down, first, steps, count, name):
    rows, width = g2low.shape
    block = 768
    chips, shard_rows = count // 2, width // count
    part = jax.ShapeDtypeStruct((chips, shard_rows, 2 * block * steps), bf16)
    return pl.pallas_call(
        functools.partial(hidden_grad_kernel, first, steps),
        in_specs=[SMEM, VM, VM, VM, VM, VM],
        out_specs=[VM] * 6,
        out_shape=[
            in_vmem(a.shape), in_vmem(b.shape), in_vmem(g2low.shape), in_vmem(w_down.shape), part, part
        ],
        input_output_aliases={3: 0, 4: 1, 1: 2, 5: 3},
        scratch_shapes=[pltpu.VMEM((width, block), f32)],
        compiler_params=limit(19),
        cost_estimate=cost(6 * rows * width * block * steps, 5_000_000),
        name=name,
    )(me, g2low, low, a, b, w_down)


def mixed_grad_kernel(
    metas, shard_rows, me_ref, gg_ref, gu_ref, g2_ref, n1_ref, inv_ref, vec_ref, wo_ref, *rest
):
    refs, rest = rest[: len(metas)], rest[len(metas) :]
    low_ref, gatt_ref, sums_ref, _gg, _gu, _g2, w_ref, sems = rest
    hidden = gg_ref.shape[1]
    block = 256
    copies = [
        piece_copies(
            metas, refs, me_ref[0], shard_rows, w_ref, c * hidden, c * hidden, hidden, sems.at[c]
        )
        for c in range(2)
    ]
    start_all(copies[0])
    start_all(copies[1])
    sums_ref[...] = jnp.zeros_like(sums_ref)

    @pl.loop(0, gg_ref.shape[0] // block)
    def _(i):
        at = pl.ds(pl.multiple_of(i * block, block), block)

        @pl.when(i == 0)
        def _():
            wait_all(copies[0])

        gm = g2_ref[at, :].astype(f32) + dot_nt(gg_ref[at, :], w_ref[:, :hidden])

        @pl.when(i == 0)
        def _():
            wait_all(copies[1])

        gm += dot_nt(gu_ref[at, :], w_ref[:, hidden:])
        n = n1_ref[at, :].astype(f32)
        sums_ref[0:1] += jnp.sum(gm * n, 0, keepdims=True)
        sums_ref[1:2] += jnp.sum(gm, 0, keepdims=True)
        low = norm_back(gm * vec_ref[0:1], n, inv_ref[at, 0:1]).astype(bf16)
        low_ref[at, :] = low
        gatt_ref[at, :] = dot_nt(low, wo_ref[...]).astype(bf16)


def mixed_grad(me, gg, gu, g2, n1, inv1, vec, w_out, pieces, shard_rows):
    rows, width = g2.shape
    hidden = gg.shape[1]
    metas = metas_of(pieces)
    return pl.pallas_call(
        functools.partial(mixed_grad_kernel, metas, shard_rows),
        in_specs=[SMEM] + [VM] * 7 + [ANY] * len(metas),
        out_specs=[VM] * 6,
        out_shape=[
            jax.ShapeDtypeStruct((rows, width), bf16),
            jax.ShapeDtypeStruct((rows, width), bf16),
            jax.ShapeDtypeStruct((8, width), f32),
            in_vmem(gg.shape),
            in_vmem(gu.shape),
            in_vmem(g2.shape),
        ],
        input_output_aliases={1: 3, 2: 4, 3: 5},
        scratch_shapes=[
            pltpu.VMEM((width, 2 * hidden), bf16),
            pltpu.SemaphoreType.DMA((2, len(metas))),
        ],
        compiler_params=limit(19),
        cost_estimate=cost(4 * rows * width * hidden + 2 * rows * width * width, 15_000_000),
        name="mixed_grad",
    )(me, gg, gu, g2, n1, inv1, vec, w_out, *arrays_of(pieces))[:3]


def attend_back_kernel(
    q_ref, k_ref, v_ref, o_ref, g_ref, p_ref, table_ref, d_ref
):
    heads = p_ref.shape[1]
    lane = lax.broadcasted_iota(jnp.int32, (1, 128), 1)
    first = half_mask(table_ref.shape)
    cos, sin = spread_tables(table_ref[...])

    def unrotate(g):
        t = g * sin
        return g * cos + jnp.where(first, pltpu.roll(t, 96, 1), -pltpu.roll(t, 32, 1))

    for pair in range(heads // 2):
        cols = slice(pair * 128, (pair + 1) * 128)
        q, k, v, g = q_ref[:, cols], k_ref[:, cols], v_ref[:, cols], g_ref[:, cols]
        go = g.astype(f32) * o_ref[:, cols].astype(f32)
        dq = dk = dv = None
        for side in range(2):
            mine = (lane // HEAD_DIM) == side
            keep = mine.astype(bf16)
            p = p_ref[0, pair * 2 + side]
            row = jnp.sum(jnp.where(mine, go, 0.0), -1, keepdims=True)
            gp = dot_nt(g, v * keep)
            gs = (p.astype(f32) * (gp - row)).astype(bf16)
            parts = (dot_nn(gs, k * keep), dot_tn(gs, q * keep), dot_tn(p, g * keep))
            if dq is None:
                dq, dk, dv = parts
            else:
                dq, dk, dv = dq + parts[0], dk + parts[1], dv + parts[2]
        d_ref[0, :, cols] = unrotate(dq * 0.125).astype(bf16)
        d_ref[1, :, cols] = unrotate(dk).astype(bf16)
        d_ref[2, :, cols] = dv.astype(bf16)


def attend_backward(q, k, v, attended, gatt, probs, table, first, steps, name):
    rows, _ = attended.shape
    seqs, _, seq, _ = probs.shape
    quad = 4
    lanes = quad * HEAD_DIM
    spec_in = pl.BlockSpec((seq, lanes), lambda s, g: (s, first + g))
    return pl.pallas_call(
        attend_back_kernel,
        grid=(seqs, steps),
        in_specs=[spec_in] * 5
        + [
            pl.BlockSpec((1, quad, seq, seq), lambda s, g: (s, first + g, 0, 0)),
            pl.BlockSpec(table.shape, lambda s, g: (0, 0)),
        ],
        out_specs=pl.BlockSpec((3, seq, lanes), lambda s, g: (0, s, g)),
        out_shape=jax.ShapeDtypeStruct((3, rows, lanes * steps), bf16),
        compiler_params=limit(16),
        cost_estimate=cost(8 * seqs * quad * steps * seq * seq * 256, 9_000_000 * steps),
        name=name,
    )(q, k, v, attended, gatt, probs, table)


def qkv_grad_kernel(extra, me_ref, x_ref, d_ref, *rest):
    me = me_ref[0]
    if extra:
        att_ref, g1_ref, s2_ref, s1_ref = rest[:4]
    keep_ref, send_ref, acc_ref = rest[-3:]
    width = x_ref.shape[1]

    def put(value, lo):
        cols = value.shape[1]
        acc_ref[:, :cols] = value
        spread(me, acc_ref.at[:, :cols], keep_ref, send_ref, slice(lo, lo + cols))
        return lo + cols

    cols = d_ref.shape[2]

    @pl.loop(0, 3)
    def _(part):
        acc_ref[:, :cols] = dot_tn(x_ref[...], d_ref[part])
        lo = pl.multiple_of(part * cols, 128)
        spread(me, acc_ref.at[:, :cols], keep_ref, send_ref, pl.ds(lo, cols))

    lo = 3 * cols
    if extra:
        lo = put(dot_tn(att_ref[...], g1_ref[...]), lo)
        row = lax.broadcasted_iota(jnp.int32, (8, width), 0)
        rows = jnp.where(row < 2, s2_ref[...], pltpu.roll(s1_ref[...], 2, 0)).astype(bf16)
        put(dot_tn(rows, unit_rows()), lo)


def qkv_grad(me, x, parts, extra, count, name):
    rows, width = x.shape
    cols = parts.shape[2]
    chips, shard_rows = count // 2, width // count
    total = 3 * cols + (width + 128 if extra else 0)
    shape = jax.ShapeDtypeStruct((chips, shard_rows, total), bf16)
    vmem = pl.BlockSpec(memory_space=pltpu.VMEM)
    return pl.pallas_call(
        functools.partial(qkv_grad_kernel, bool(extra)),
        in_specs=[SMEM] + [vmem] * (2 + len(extra)),
        out_specs=[vmem, vmem],
        out_shape=[shape, shape],
        scratch_shapes=[pltpu.VMEM((width, width), f32)],
        compiler_params=limit(20),
        cost_estimate=cost(2 * rows * width * total, 12_000_000),
        name=name,
    )(me, x, parts, *extra)


def input_grad_kernel(g1_ref, w_ref, *rest):
    out_ref = rest[-1]
    width = out_ref.shape[1]
    total = g1_ref[...].astype(f32)
    for p in range(3):
        lo = p * width
        for ref in rest[:-1]:
            total += dot_nt(ref[p], w_ref[:, lo : lo + ref.shape[2]])
            lo += ref.shape[2]
    out_ref[...] = total.astype(bf16)


def input_grad(g1, w_qkv, parts):
    rows, width = g1.shape
    block = 512
    by_row = pl.BlockSpec((block, width), lambda i: (i, 0))
    return pl.pallas_call(
        input_grad_kernel,
        grid=(rows // block,),
        in_specs=[by_row, whole(w_qkv.shape)]
        + [pl.BlockSpec((3, block, p.shape[2]), lambda i: (0, i, 0)) for p in parts],
        out_specs=by_row,
        out_shape=jax.ShapeDtypeStruct((rows, width), bf16),
        compiler_params=limit(20),
        cost_estimate=cost(6 * rows * width * width, 14_000_000),
        name="input_grad",
    )(g1, w_qkv, *parts)


def rope_tables(seq_len):
    frequency = rope_base ** (-np.arange(0, HEAD_DIM, 2, dtype=np.float32) / HEAD_DIM)
    frequency = jnp.asarray(np.tile(frequency.astype(np.float32), 4))[None, :]
    shape = (seq_len, 128)
    angles = lax.broadcasted_iota(jnp.int32, shape, 0).astype(f32) * frequency
    lane = lax.broadcasted_iota(jnp.int32, shape, 1)
    return jnp.where(lane // 32 % 2 == 0, jnp.cos(angles), jnp.sin(angles))


def spread_tables(table):
    shifted = pltpu.roll(table, 32, 1)
    even = lax.broadcasted_iota(jnp.int32, table.shape, 1) // 32 % 2 == 0
    return jnp.where(even, table, shifted), jnp.where(even, shifted, table)


def shards(
    tokens, segment_ids, qkv_weight, out_weight, gate_weight, up_weight, down_weight,
    norm1_gain, norm1_bias, norm2_gain, norm2_bias, out_grad,
):
    count = lax.axis_size("shard")
    me = lax.axis_index("shard").astype(jnp.int32).reshape(1)
    batches, seq, width = tokens.shape
    shard_rows = qkv_weight.shape[0]
    down_rows = down_weight.shape[0]
    hidden = gate_weight.shape[1]
    rows = batches * seq
    chips = count // 2

    x = tokens.reshape(rows, width)
    cot = out_grad.reshape(rows, width)
    table = rope_tables(seq)
    vectors = jnp.stack([norm1_gain, norm1_bias, norm2_gain, norm2_bias], 1)
    vectors = jnp.pad(vectors, ((0, 0), (0, 124)))
    odd = (lax.axis_index("rep") % 2 == 1).reshape(1, 1)

    pieces_a = gather_direct(qkv_weight)
    own_b = jnp.concatenate([gate_weight, up_weight, out_weight, vectors], 1)
    seg = segment_ids.reshape(batches, 1, seq)
    table, seg, own_b, odd, ready = tie((table, seg, own_b, odd, pieces_a[0][2]))
    pieces_a = [(r, lo, tie(p, ready, seg, odd, table)) for r, lo, p in pieces_a]
    far_a = tuple(p for _, _, p in pieces_a[1:])
    pieces_a = with_partner(pieces_a)
    own_b = tie(own_b, far_a)
    if count == 8:
        first_b = gather_first(own_b)
        first_c = gather_first(tie(down_weight, far_a))
    else:
        pieces_b = gather_direct(own_b)
        pieces_c = gather_direct(down_weight)
    q, k, v, attended, probs, w_qkv = front(me, x, table, seg, pieces_a, shard_rows)
    if count == 8:
        first_b = tie(first_b, attended)
        pieces_b = gather_second(own_b, first_b)
        first_c = tie(first_c, first_b)
        pieces_c = gather_second(down_weight, first_c)
    pieces_b = with_partner(pieces_b)
    near_c = with_partner(pieces_c[:3])
    hidden_low, back_gate, back_up, low, n1, inv1, vec, w_out = gate_forward(
        me, x, attended, pieces_b, shard_rows, hidden
    )
    if count == 8:
        pieces_c = near_c + with_partner([(r, lo, tie(p, low)) for r, lo, p in pieces_c[3:]])
    else:
        pieces_c = with_partner(pieces_c)
    output, g2low, sums2, d_keep, d_send, w_down = down_forward(
        me, hidden_low, n1, cot, vec, pieces_c, down_rows, chips
    )
    steps = hidden // 768 // 2
    flow_d = Flow(d_keep, d_send, odd, False)
    ready = sums2
    grads1 = hidden_grad(
        me, tie(g2low, ready), low, back_gate, back_up, w_down, 0, steps, count, "hidden_grad_1"
    )
    flow_e = Flow(*grads1[4:], odd, False)
    ready = advance(grads1[0], flow_d)
    grads2 = hidden_grad(
        me, tie(grads1[2], ready), low, *grads1[:2], grads1[3], steps, steps, count, "hidden_grad_2"
    )
    flow_f = Flow(*grads2[4:], odd, False)
    ready = advance(grads2[0], flow_e)
    g1low, gatt, sums1 = mixed_grad(
        me, *grads2[:2], tie(grads2[2], ready), n1, inv1, vec, w_out, pieces_b, shard_rows
    )
    ready = advance(g1low, flow_f, flow_d)
    back_a = attend_backward(
        q, k, v, attended, tie(gatt, ready), probs, table, 0, 2, "attend_bwd_1"
    )
    ready = advance(back_a, flow_e, flow_d)
    a_keep, a_send = qkv_grad(
        me, x, tie(back_a, ready), (attended, g1low, sums2, sums1), count, "qkv_out_grad_1"
    )
    flow_a = Flow(a_keep, a_send, odd, False)
    ready = advance(a_keep, flow_f, flow_e, flow_d)
    back_b = attend_backward(
        q, k, v, attended, tie(gatt, ready), probs, table, 2, 1, "attend_bwd_2"
    )
    ready = advance(back_b, flow_a, flow_f, flow_e, flow_d)
    b_keep, b_send = qkv_grad(me, x, tie(back_b, ready), (), count, "qkv_grad_2")
    flow_b = Flow(b_keep, b_send, odd, True)
    ready = advance(b_keep, flow_b)
    in_grad = input_grad(tie(g1low, ready), w_qkv, [back_a, back_b])
    ready = advance(in_grad, flow_a, flow_f, flow_e, flow_d)
    flow_a.pass_on = True
    flow_b.other = flow_a.step(ready)
    ready = advance(ready, flow_b, flow_f, flow_e)
    d_sum, e_sum, f_sum = [flow.finish() for flow in (flow_d, flow_e, flow_f)]
    total = flow_b.finish()
    a_sum, b_sum = total[:, : a_keep.shape[2]], total[:, a_keep.shape[2] :]

    block = 768
    hidden_sums = (e_sum, f_sum)
    pick = lambda part: jnp.concatenate(
        [
            s[:, (2 * j + part) * block : (2 * j + part + 1) * block]
            for s in hidden_sums
            for j in range(steps)
        ],
        1,
    )
    cols_a, cols_b = back_a.shape[2], back_b.shape[2]
    qkv_sum = jnp.concatenate(
        [
            s[:, p * c : (p + 1) * c]
            for p in range(3)
            for s, c in ((a_sum, cols_a), (b_sum, cols_b))
        ],
        1,
    )
    out_sum = a_sum[:, 3 * cols_a : 3 * cols_a + width]
    vec_sum = a_sum[:, 3 * cols_a + width :]
    return (
        output.reshape(tokens.shape),
        in_grad.reshape(tokens.shape),
        qkv_sum,
        out_sum,
        pick(0),
        pick(1),
        d_sum,
        vec_sum[:, 2],
        vec_sum[:, 3],
        vec_sum[:, 0],
        vec_sum[:, 1],
    )


def solution(mesh):
    rows3 = P(None, ("shard", "rep"), None)
    rows2 = P("shard", None)
    rows1 = P("shard")
    in_specs = (rows3, P(None, ("shard", "rep"))) + (rows2,) * 5 + (rows1,) * 4 + (rows3,)
    out_specs = (rows3, rows3) + (rows2,) * 5 + (rows1,) * 4
    return jax.shard_map(shards, mesh=mesh, in_specs=in_specs, out_specs=out_specs, check_vma=False)
```

```python
import functools

import jax
import jax.numpy as jnp
import numpy as np
from jax import lax
from jax.experimental import pallas as pl
from jax.experimental.pallas import tpu as pltpu
from jax.sharding import PartitionSpec as P

HEAD_DIM = 64
norm_eps = 1e-12
rope_base = 1000.0
masked_score = -1e30
f32 = jnp.float32
bf16 = jnp.bfloat16
ANY = pl.BlockSpec(memory_space=pl.ANY)
SMEM = pl.BlockSpec(memory_space=pltpu.SMEM)


def dot_nn(a, b):
    return lax.dot_general(a, b, (((1,), (0,)), ((), ())), preferred_element_type=f32)


def dot_nt(a, b):
    return lax.dot_general(a, b, (((1,), (1,)), ((), ())), preferred_element_type=f32)


def dot_tn(a, b):
    return lax.dot_general(a, b, (((0,), (0,)), ((), ())), preferred_element_type=f32)


def whole(shape):
    return pl.BlockSpec(shape, lambda *_: (0,) * len(shape))


def tie(value, *deps):
    return lax.optimization_barrier((value, deps))[0]


def xor_permute(x, bit):
    count = lax.axis_size("shard")
    return lax.ppermute(x, "shard", [(i, i ^ bit) for i in range(count)])


def with_partner(pieces):
    return pieces + [(r | 1, lo, xor_permute(p, 1)) for r, lo, p in pieces]


def gather_direct(own):
    return [(0, 0, own)] + [(r, 0, xor_permute(own, r)) for r in range(2, lax.axis_size("shard"), 2)]


def gather_first(own):
    return xor_permute(own, 2), xor_permute(own, 4)


def gather_second(own, first):
    half = own.shape[0] // 2
    from_x, from_y = first
    far = (xor_permute(from_y[:half], 2), xor_permute(from_x[half:], 4))
    return [(0, 0, own), (2, 0, from_x), (4, 0, from_y), (6, 0, far[0]), (6, half, far[1])]


def add_parts(parts):
    return functools.reduce(jnp.add, [p.astype(f32) for p in parts]).astype(bf16)


def rep_permute(x, pairs):
    return lax.ppermute(x, "rep", pairs)


def load_kernel(jobs, body, *refs):
    operands, rest = refs[: body.operands], refs[body.operands :]
    outs, (hold, sems) = rest[: body.outs], rest[body.outs :]
    half = hold.shape[1]
    copies = []
    for i, (operand, block, part) in enumerate(jobs):
        ref = operands[operand]
        src = ref.at[block, pl.ds(part * half, half), :] if block is not None else ref
        copies.append(pltpu.make_async_copy(src, hold.at[i], sems.at[i]))
        copies[-1].start()
    for copy in copies:
        copy.wait()
    body(hold, *outs)


class Fold:
    def __init__(self, operands, outs, body):
        self.operands, self.outs, self.body = operands, outs, body

    def __call__(self, hold, *outs):
        self.body(hold, *outs)


def fold_call(arrays, jobs, out_shapes, body, half, cols, name):
    count = len(out_shapes)
    return pl.pallas_call(
        functools.partial(load_kernel, jobs, Fold(len(arrays), count, body)),
        in_specs=[pl.BlockSpec(memory_space=pl.ANY)] * len(arrays),
        out_specs=[pl.BlockSpec(memory_space=pltpu.VMEM)] * count,
        out_shape=[jax.ShapeDtypeStruct(s, bf16) for s in out_shapes],
        scratch_shapes=[
            pltpu.VMEM((len(jobs), half, cols), bf16),
            pltpu.SemaphoreType.DMA((len(jobs),)),
        ],
        compiler_params=pltpu.CompilerParams(vmem_limit_bytes=8 << 20),
        cost_estimate=cost(len(jobs) * half * cols, 3 * len(jobs) * half * cols),
        name=name,
    )(*arrays)


def each_rows(rows, step, body):
    @pl.loop(0, rows // step)
    def _(i):
        body(pl.ds(pl.multiple_of(i * step, step), step))


def plus(hold, at, *slots):
    return functools.reduce(jnp.add, [hold[s, at, :].astype(f32) for s in slots]).astype(bf16)


def row_step(half):
    return 16 if half % 16 == 0 else 8


def fold_first(keep, got):
    _, rows, cols = keep.shape
    half = rows // 2
    jobs = [(a, q, p) for q, p in ((1, 0), (3, 0), (2, 1), (3, 1)) for a in (0, 1)]

    def body(hold, x_ref, y_ref):
        def some(at):
            for n, ref in enumerate((x_ref, x_ref, y_ref, y_ref)):
                ref[n % 2, at, :] = plus(hold, at, 2 * n, 2 * n + 1)

        each_rows(half, row_step(half), some)

    return fold_call([keep, got], jobs, [(2, half, cols)] * 2, body, half, cols, "fold_first")


def fold_second(keep, got, from_x, from_y):
    _, rows, cols = keep.shape
    half = rows // 2
    jobs = [(0, 2, 0), (1, 2, 0), (2, 1, 0), (0, 1, 1), (1, 1, 1), (3, 1, 0)]

    def body(hold, y_ref, x_ref):
        def some(at):
            y_ref[at, :] = plus(hold, at, 0, 1, 2)
            x_ref[at, :] = plus(hold, at, 3, 4, 5)

        each_rows(half, row_step(half), some)

    return fold_call(
        [keep, got, from_x, from_y], jobs, [(half, cols)] * 2, body, half, cols, "fold_second"
    )


def fold_own(keep, got, from_x, from_y, last_y, last_x):
    _, rows, cols = keep.shape
    half = rows // 2
    jobs = [
        (0, 0, 0), (1, 0, 0), (2, 0, 0), (4, None, 0), (0, 0, 1), (1, 0, 1), (3, 0, 0), (5, None, 0)
    ]

    def body(hold, own_ref):
        def some(at):
            own_ref[0, at, :] = plus(hold, at, 0, 1, 2, 3)
            own_ref[1, at, :] = plus(hold, at, 4, 5, 6, 7)

        each_rows(half, row_step(half), some)

    own = fold_call(
        [keep, got, from_x, from_y, last_y, last_x], jobs, [(2, half, cols)], body, half, cols, "fold_own"
    )[0]
    return own.reshape(rows, cols)


def fold_call_whole(arrays, jobs, pairs, name):
    _, rows, cols = arrays[0].shape

    def body(hold, out_ref):
        def some(at):
            for n, slots in enumerate(pairs):
                out_ref[n, at, :] = plus(hold, at, *slots)

        each_rows(rows, row_step(rows), some)

    return fold_call(arrays, jobs, [(len(pairs), rows, cols)], body, rows, cols, name)[0]


def fold_line_first(keep, got, near):
    jobs = [(a, q, 0) for q in (near, 3) for a in (0, 1)]
    return fold_call_whole([keep, got], jobs, [(0, 1), (2, 3)], "fold_line_first")


def fold_line_second(keep, got, came, far):
    jobs = [(0, far, 0), (1, far, 0), (2, 1, 0)]
    return fold_call_whole([keep, got, came], jobs, [(0, 1, 2)], "fold_line_second")


def fold_line_own(keep, got, came, last):
    jobs = [(0, 0, 0), (1, 0, 0), (2, 0, 0), (3, 0, 0)]
    return fold_call_whole([keep, got, came, last], jobs, [(0, 1, 2, 3)], "fold_line_own")[0]


class Flow:
    def __init__(self, keep, send, odd, direct=False):
        self.held = keep
        self.odd = odd
        self.other = None
        self.pass_on = False
        self.pending = xor_permute(send, 1)
        self.stage = 0
        self.way = direct if keep.shape[0] == 4 and direct in (1, 2) and direct is not True else 0
        self.pair = keep.shape[0] == 4 and not direct
        self.line = lax.axis_size("rep") == 4

    def step(self, *deps):
        got = tie(self.pending, *deps) if deps else self.pending
        stage = self.stage
        if stage == 0:
            self.got = got
            if self.way:
                self.ready = fold_line_first(self.held, got, self.way)
                self.pending = xor_permute(self.ready, 2 * self.way)
            elif self.pair:
                self.ready = fold_first(self.held, got)
                self.pending = (xor_permute(self.ready[0], 2), xor_permute(self.ready[1], 4))
            else:
                self.ready = [self.held[q] + got[q] for q in range(got.shape[0])]
                self.pending = [xor_permute(self.ready[q], 2 * q) for q in range(1, got.shape[0])]
        elif stage == 1 and self.way:
            self.first = got
            self.ready = fold_line_second(self.held, self.got, got, 3 - self.way)
            self.pending = xor_permute(self.ready, 2 * (3 - self.way))
        elif stage == 1 and self.pair:
            self.first = got
            if self.pair:
                self.ready = fold_second(self.held, self.got, *got)
                self.pending = (xor_permute(self.ready[0], 4), xor_permute(self.ready[1], 2))
        elif stage <= 2:
            self.stage = 2
            if self.way:
                self.ready = fold_line_own(self.held, self.got, self.first, got)
            elif self.pair:
                self.ready = fold_own(self.held, self.got, *self.first, *got)
            else:
                self.ready = add_parts([self.ready[0]] + list(got))
            if self.other is not None:
                self.ready = jnp.concatenate([self.other, self.ready], 1)
            if self.pass_on:
                self.stage = 6
                return self.ready
            if self.line:
                half = self.ready.shape[0] // 2
                self.mine = jnp.where(self.odd, self.ready[half:], self.ready[:half])
                self.ready = jnp.where(self.odd, self.ready[:half], self.ready[half:])
                self.pending = rep_permute(self.ready, [(0, 1), (1, 0), (2, 3), (3, 2)])
            else:
                self.pending = lax.psum(self.ready, "rep")
        elif not self.line:
            self.ready = got
        elif stage == 3:
            self.ready = add_parts([self.mine, got])
            self.pending = rep_permute(self.ready, [(0, 2), (2, 0), (1, 3), (3, 1)])
        elif stage == 4:
            self.ready = add_parts([self.ready, got])
            self.pending = rep_permute(self.ready, [(0, 1), (1, 0), (2, 3), (3, 2)])
        else:
            low, high = (jnp.where(self.odd, a, b) for a, b in ((got, self.ready), (self.ready, got)))
            self.ready = jnp.concatenate([low, high]).astype(f32)
        self.stage += 1
        return self.ready

    def finish(self):
        while self.stage < 6:
            self.step()
        return self.ready.astype(f32)


def advance(dep, *flows):
    return tuple(flow.step(dep) for flow in flows)


def piece_copies(metas, refs, me, shard_rows, dst, src_lo, dst_lo, cols, sems):
    copies = []
    for i, ((rel, first, rows), ref) in enumerate(zip(metas, refs)):
        at = pl.multiple_of((me ^ rel) * shard_rows + first, 8)
        copies.append(
            pltpu.make_async_copy(
                ref.at[:, pl.ds(src_lo, cols)],
                dst.at[pl.ds(at, rows), pl.ds(dst_lo, cols)],
                sems.at[i],
            )
        )
    return copies


def start_all(copies):
    for copy in copies:
        copy.start()


def wait_all(copies):
    for copy in copies:
        copy.wait()


def metas_of(pieces):
    return tuple((rel, first, p.shape[0]) for rel, first, p in pieces)


def in_hbm(x):
    return pltpu.with_memory_space_constraint(x, pltpu.HBM)


def arrays_of(pieces):
    return [in_hbm(p) for _, _, p in pieces]


def half_mask(shape):
    lane = lax.broadcasted_iota(jnp.int32, shape, len(shape) - 1)
    return (lane % HEAD_DIM) < HEAD_DIM // 2


def unit_rows():
    shape = (8, 128)
    return (
        lax.broadcasted_iota(jnp.int32, shape, 0) == lax.broadcasted_iota(jnp.int32, shape, 1)
    ).astype(bf16)


def normalize(h):
    centre = h - jnp.mean(h, -1, keepdims=True)
    inv = lax.rsqrt(jnp.mean(centre * centre, -1, keepdims=True) + norm_eps)
    return centre * inv, inv


def norm_back(e, n, inv):
    return inv * (e - jnp.mean(e, -1, keepdims=True) - n * jnp.mean(e * n, -1, keepdims=True))


def spread(me, acc_ref, keep_ref, send_ref, cols):
    rows = keep_ref.shape[1]
    chip, core = me // 2, me & 1
    for q in range(keep_ref.shape[0]):
        base = (chip ^ q) * 2
        keep_ref[q, :, cols] = acc_ref[
            pl.ds(pl.multiple_of((base + core) * rows, 8), rows), :
        ].astype(bf16)
        send_ref[q, :, cols] = acc_ref[
            pl.ds(pl.multiple_of((base + 1 - core) * rows, 8), rows), :
        ].astype(bf16)


def cost(flops, read, transcendentals=0):
    return pl.CostEstimate(flops=1000, bytes_accessed=1000, transcendentals=0)


def front_kernel(metas, shard_rows, me_ref, x_ref, table_ref, row_ref, *rest):
    refs, rest = rest[: len(metas)], rest[len(metas) :]
    q_ref, k_ref, v_ref, att_ref, p_ref, w_out, w_ref, bias_ref, sems, back_sem = rest
    s, g = pl.program_id(0), pl.program_id(1)
    width = x_ref.shape[1]
    lanes = p_ref.shape[1] * HEAD_DIM
    copies = piece_copies(metas, refs, me_ref[0], shard_rows, w_ref, 0, 0, 3 * width, sems)
    back = pltpu.make_async_copy(w_ref, w_out, back_sem)

    @pl.when((s == 0) & (g == 0))
    def _():
        start_all(copies)
        wait_all(copies)
        back.start()

    @pl.when(g == 0)
    def _():
        across = jnp.broadcast_to(row_ref[0].astype(f32), bias_ref.shape)
        down = lax.broadcasted_iota(jnp.int32, bias_ref.shape, 0)
        own = lax.broadcasted_iota(jnp.int32, bias_ref.shape, 1) == down
        column = jnp.sum(jnp.where(own, across, 0.0), -1, keepdims=True)
        bias_ref[...] = jnp.where(across == column, 0.0, masked_score).astype(f32)
        x = x_ref[...]
        first = half_mask((x.shape[0], 128))
        cos, sin = spread_tables(table_ref[...])
        sin = jnp.where(first, -sin, sin)
        for part, ref in enumerate((q_ref, k_ref, v_ref)):
            y = dot_nn(x, w_ref[:, part * width : (part + 1) * width])
            for b in range(width // 128):
                cols = slice(b * 128, (b + 1) * 128)
                u = y[:, cols]
                if part < 2:
                    turned = jnp.where(first, pltpu.roll(u, 96, 1), pltpu.roll(u, 32, 1))
                    u = u * cos + turned * sin
                if part == 0:
                    u = u * 0.125
                ref[:, cols] = u.astype(bf16)

    lane = lax.broadcasted_iota(jnp.int32, (1, 128), 1)
    for pair in range(lanes // 128):
        at = pl.ds(pl.multiple_of(g * lanes + pair * 128, 128), 128)
        q, k, v = q_ref[:, at], k_ref[:, at], v_ref[:, at]
        acc = None
        for side in range(2):
            mine = ((lane // HEAD_DIM) == side).astype(bf16)
            score = dot_nt(q, k * mine) + bias_ref[...]
            e = jnp.exp(score - jnp.max(score, -1, keepdims=True))
            inv = 1.0 / jnp.sum(e, -1, keepdims=True)
            p = (e * inv).astype(bf16)
            p_ref[0, pair * 2 + side] = p
            part = dot_nn(p, v * mine)
            acc = part if acc is None else acc + part
        att_ref[:, pair * 128 : (pair + 1) * 128] = acc.astype(bf16)

    @pl.when((s == pl.num_programs(0) - 1) & (g == pl.num_programs(1) - 1))
    def _():
        back.wait()


def front(me, x, table, seg_row, pieces, shard_rows):
    rows, width = x.shape
    metas = metas_of(pieces)
    seqs, _, seq = seg_row.shape
    heads = width // HEAD_DIM
    quad = 4
    lanes = quad * HEAD_DIM
    by_seq = pl.BlockSpec((seq, width), lambda s, g: (s, 0))
    wide = jax.ShapeDtypeStruct((rows, width), bf16)
    return pl.pallas_call(
        functools.partial(front_kernel, metas, shard_rows),
        grid=(seqs, width // lanes),
        in_specs=[
            SMEM, by_seq, whole(table.shape),
            pl.BlockSpec((1, 1, seq), lambda s, g: (s, 0, 0)),
        ]
        + [ANY] * len(metas),
        out_specs=[by_seq] * 3
        + [
            pl.BlockSpec((seq, lanes), lambda s, g: (s, g)),
            pl.BlockSpec((1, quad, seq, seq), lambda s, g: (s, g, 0, 0)),
            ANY,
        ],
        out_shape=[wide] * 4
        + [
            jax.ShapeDtypeStruct((seqs, heads, seq, seq), bf16),
            jax.ShapeDtypeStruct((width, 3 * width), bf16),
        ],
        scratch_shapes=[
            pltpu.VMEM((width, 3 * width), bf16),
            pltpu.VMEM((seq, seq), f32),
            pltpu.SemaphoreType.DMA((len(metas),)),
            pltpu.SemaphoreType.DMA,
        ],
        cost_estimate=cost(
            6 * rows * width * width + 4 * seqs * heads * seq * seq * 256,
            30_000_000,
            seqs * heads * seq * seq,
        ),
        name="qkv_attend",
    )(me, x, table, seg_row, *[p for _, _, p in pieces])


VM = pl.BlockSpec(memory_space=pltpu.VMEM)
HBM = pl.BlockSpec(memory_space=pltpu.HBM)


def in_vmem(shape, dtype=bf16):
    return pltpu.VMEM(shape, dtype)


def limit(mib):
    return pltpu.CompilerParams(vmem_limit_bytes=mib << 20)


def gate_kernel(metas, shard_rows, me_ref, tok_ref, att_ref, *rest):
    refs, rest = rest[: len(metas)], rest[len(metas) :]
    h_ref, a_ref, b_ref, x_ref, n1_ref, inv_ref, vec_ref, wo_ref = rest[:8]
    wg_ref, wv_ref, sems, sems_o = rest[8:]
    hidden = a_ref.shape[1]
    width = wo_ref.shape[1]
    block = 768
    steps = hidden // block
    me = me_ref[0]

    def spans(j):
        return pl.multiple_of(j * block, block), pl.multiple_of(hidden + j * block, block)

    def copies(j):
        both = []
        for part, lo in enumerate(spans(j)):
            both += piece_copies(metas, refs, me, shard_rows, wg_ref, lo, lo, block, sems.at[j, part])
        return both

    copies_o = piece_copies(
        metas, refs, me, shard_rows, wo_ref, 2 * hidden, 0, width, sems_o.at[0]
    ) + piece_copies(metas, refs, me, shard_rows, wv_ref, 2 * hidden + width, 0, 128, sems_o.at[1])
    start_all(copies_o)

    @pl.loop(0, steps)
    def _(j):
        start_all(copies(j))

    wait_all(copies_o)
    vec_ref[...] = dot_nt(unit_rows(), wv_ref[...])

    @pl.loop(0, 2)
    def _(i):
        rows = tok_ref.shape[0] // 2
        at = pl.ds(pl.multiple_of(i * rows, 8), rows)
        n, inv = normalize(tok_ref[at, :].astype(f32) + dot_nn(att_ref[at, :], wo_ref[...]))
        n1_ref[at, :] = n.astype(bf16)
        inv_ref[at, :] = jnp.broadcast_to(inv, (rows, inv_ref.shape[1]))
        x_ref[at, :] = (n * vec_ref[0:1] + vec_ref[1:2]).astype(bf16)

    @pl.loop(0, steps)
    def _(j):
        wait_all(copies(j))
        gate_at, up_at = (pl.ds(lo, block) for lo in spans(j))
        half = x_ref.shape[0] // 2

        @pl.loop(0, 2)
        def _(r):
            rows = pl.ds(pl.multiple_of(r * half, half), half)
            gate = dot_nn(x_ref[rows, :], wg_ref[:, gate_at])
            up = dot_nn(x_ref[rows, :], wg_ref[:, up_at])
            s = 0.5 * jnp.tanh(0.5 * gate) + 0.5
            act = gate * s
            h_ref[rows, gate_at] = (act * up).astype(bf16)
            b_ref[rows, gate_at] = act.astype(bf16)
            a_ref[rows, gate_at] = (up * (s + act * (1.0 - s))).astype(bf16)


def gate_forward(me, tokens, attended, pieces, shard_rows, hidden):
    rows, width = tokens.shape
    metas = metas_of(pieces)
    return pl.pallas_call(
        functools.partial(gate_kernel, metas, shard_rows),
        in_specs=[SMEM, VM, VM] + [ANY] * len(metas),
        out_specs=[VM] * 8,
        out_shape=[in_vmem((rows, hidden))] * 3
        + [
            in_vmem((rows, width)),
            in_vmem((rows, width)),
            in_vmem((rows, 128), f32),
            in_vmem((8, width), f32),
            in_vmem((width, width)),
        ],
        scratch_shapes=[
            pltpu.VMEM((width, 2 * hidden), bf16),
            pltpu.VMEM((width, 128), bf16),
            pltpu.SemaphoreType.DMA((hidden // 768, 2, len(metas))),
            pltpu.SemaphoreType.DMA((2, len(metas))),
        ],
        compiler_params=limit(19),
        cost_estimate=cost(4 * rows * width * hidden, 10_000_000, rows * hidden),
        name="out_gate_up",
    )(me, tokens, attended, *arrays_of(pieces))


def down_kernel(metas, shard_rows, me_ref, h_ref, n1_ref, cot_ref, vec_ref, *rest):
    refs = rest[: len(metas)]
    out_ref, low_ref, sums_ref, keep_ref, send_ref, w_ref, acc_ref, sems = rest[len(metas) :]
    me = me_ref[0]
    copies = piece_copies(metas, refs, me, shard_rows, w_ref, 0, 0, w_ref.shape[1], sems)
    start_all(copies)
    sums_ref[...] = jnp.zeros_like(sums_ref)
    wait_all(copies)
    block = 256

    @pl.loop(0, h_ref.shape[0] // block)
    def _(i):
        at = pl.ds(pl.multiple_of(i * block, block), block)
        mixed = n1_ref[at, :].astype(f32) * vec_ref[0:1] + vec_ref[1:2]
        n, inv = normalize(mixed + dot_nn(h_ref[at, :], w_ref[...]))
        out_ref[at, :] = (n * vec_ref[2:3] + vec_ref[3:4]).astype(bf16)
        cot = cot_ref[at, :].astype(f32)
        sums_ref[0:1] += jnp.sum(cot * n, 0, keepdims=True)
        sums_ref[1:2] += jnp.sum(cot, 0, keepdims=True)
        low_ref[at, :] = norm_back(cot * vec_ref[2:3], n, inv).astype(bf16)

    per_chip = acc_ref.shape[0]
    half = per_chip // 2
    core = me & 1

    @pl.loop(0, keep_ref.shape[0])
    def _(q):
        lo = pl.multiple_of(((me // 2) ^ q) * per_chip, 128)
        acc_ref[...] = dot_tn(h_ref[:, pl.ds(lo, per_chip)], low_ref[...])
        keep_ref[q] = acc_ref[pl.ds(pl.multiple_of(core * half, 8), half), :].astype(bf16)
        send_ref[q] = acc_ref[pl.ds(pl.multiple_of((1 - core) * half, 8), half), :].astype(bf16)


def down_forward(me, hidden_low, n1, cot, vec, pieces, shard_rows, chips):
    rows, hidden = hidden_low.shape
    width = n1.shape[1]
    metas = metas_of(pieces)
    per_chip = hidden // chips
    return pl.pallas_call(
        functools.partial(down_kernel, metas, shard_rows),
        in_specs=[SMEM, VM, VM, VM, VM] + [ANY] * len(metas),
        out_specs=[VM] * 6,
        out_shape=[
            jax.ShapeDtypeStruct((rows, width), bf16),
            in_vmem((rows, width)),
            in_vmem((8, width), f32),
            jax.ShapeDtypeStruct((chips, per_chip // 2, width), bf16),
            jax.ShapeDtypeStruct((chips, per_chip // 2, width), bf16),
            in_vmem((hidden, width)),
        ],
        scratch_shapes=[
            pltpu.VMEM((per_chip, width), f32),
            pltpu.SemaphoreType.DMA((len(metas),)),
        ],
        compiler_params=limit(19),
        cost_estimate=cost(4 * rows * width * hidden, 10_000_000, rows),
        name="down_norm_grad",
    )(me, hidden_low, n1, cot, vec, *arrays_of(pieces))


def hidden_grad_kernel(
    first, steps, me_ref, g_ref, x_ref, a_ref, b_ref, w_ref, gg_ref, gu_ref, _g, _w, keep_ref, send_ref, acc_ref
):
    block = 768

    @pl.loop(0, steps)
    def _(j):
        cols = pl.ds(pl.multiple_of((first + j) * block, block), block)
        half = g_ref.shape[0] // 2

        @pl.loop(0, 2)
        def _(r):
            rows = pl.ds(pl.multiple_of(r * half, half), half)
            gh = dot_nt(g_ref[rows, :], w_ref[cols, :])
            gg_ref[rows, cols] = (gh * a_ref[rows, cols].astype(f32)).astype(bf16)
            gu_ref[rows, cols] = (gh * b_ref[rows, cols].astype(f32)).astype(bf16)
        for part, ref in enumerate((gg_ref, gu_ref)):
            acc_ref[...] = dot_tn(x_ref[...], ref[:, cols])
            lo = pl.multiple_of((2 * j + part) * block, block)
            spread(me_ref[0], acc_ref, keep_ref, send_ref, pl.ds(lo, block))


def hidden_grad(me, g2low, low, a, b, w_down, first, steps, count, name):
    rows, width = g2low.shape
    block = 768
    chips, shard_rows = count // 2, width // count
    part = jax.ShapeDtypeStruct((chips, shard_rows, 2 * block * steps), bf16)
    return pl.pallas_call(
        functools.partial(hidden_grad_kernel, first, steps),
        in_specs=[SMEM, VM, VM, VM, VM, VM],
        out_specs=[VM] * 6,
        out_shape=[
            in_vmem(a.shape), in_vmem(b.shape), in_vmem(g2low.shape), in_vmem(w_down.shape), part, part
        ],
        input_output_aliases={3: 0, 4: 1, 1: 2, 5: 3},
        scratch_shapes=[pltpu.VMEM((width, block), f32)],
        compiler_params=limit(19),
        cost_estimate=cost(6 * rows * width * block * steps, 5_000_000),
        name=name,
    )(me, g2low, low, a, b, w_down)


def mixed_grad_kernel(
    metas, shard_rows, me_ref, gg_ref, gu_ref, g2_ref, n1_ref, inv_ref, vec_ref, wo_ref, *rest
):
    refs, rest = rest[: len(metas)], rest[len(metas) :]
    low_ref, gatt_ref, sums_ref, _gg, _gu, _g2, w_ref, sems = rest
    hidden = gg_ref.shape[1]
    block = 256
    copies = [
        piece_copies(
            metas, refs, me_ref[0], shard_rows, w_ref, c * hidden, c * hidden, hidden, sems.at[c]
        )
        for c in range(2)
    ]
    start_all(copies[0])
    start_all(copies[1])
    sums_ref[...] = jnp.zeros_like(sums_ref)

    @pl.loop(0, gg_ref.shape[0] // block)
    def _(i):
        at = pl.ds(pl.multiple_of(i * block, block), block)

        @pl.when(i == 0)
        def _():
            wait_all(copies[0])

        gm = g2_ref[at, :].astype(f32) + dot_nt(gg_ref[at, :], w_ref[:, :hidden])

        @pl.when(i == 0)
        def _():
            wait_all(copies[1])

        gm += dot_nt(gu_ref[at, :], w_ref[:, hidden:])
        n = n1_ref[at, :].astype(f32)
        sums_ref[0:1] += jnp.sum(gm * n, 0, keepdims=True)
        sums_ref[1:2] += jnp.sum(gm, 0, keepdims=True)
        low = norm_back(gm * vec_ref[0:1], n, inv_ref[at, 0:1]).astype(bf16)
        low_ref[at, :] = low
        gatt_ref[at, :] = dot_nt(low, wo_ref[...]).astype(bf16)


def mixed_grad(me, gg, gu, g2, n1, inv1, vec, w_out, pieces, shard_rows):
    rows, width = g2.shape
    hidden = gg.shape[1]
    metas = metas_of(pieces)
    return pl.pallas_call(
        functools.partial(mixed_grad_kernel, metas, shard_rows),
        in_specs=[SMEM] + [VM] * 7 + [ANY] * len(metas),
        out_specs=[VM] * 6,
        out_shape=[
            jax.ShapeDtypeStruct((rows, width), bf16),
            jax.ShapeDtypeStruct((rows, width), bf16),
            jax.ShapeDtypeStruct((8, width), f32),
            in_vmem(gg.shape),
            in_vmem(gu.shape),
            in_vmem(g2.shape),
        ],
        input_output_aliases={1: 3, 2: 4, 3: 5},
        scratch_shapes=[
            pltpu.VMEM((width, 2 * hidden), bf16),
            pltpu.SemaphoreType.DMA((2, len(metas))),
        ],
        compiler_params=limit(19),
        cost_estimate=cost(4 * rows * width * hidden + 2 * rows * width * width, 15_000_000),
        name="mixed_grad",
    )(me, gg, gu, g2, n1, inv1, vec, w_out, *arrays_of(pieces))[:3]


def attend_back_kernel(
    q_ref, k_ref, v_ref, o_ref, g_ref, p_ref, table_ref, d_ref
):
    heads = p_ref.shape[1]
    lane = lax.broadcasted_iota(jnp.int32, (1, 128), 1)
    first = half_mask(table_ref.shape)
    cos, sin = spread_tables(table_ref[...])

    def unrotate(g):
        t = g * sin
        return g * cos + jnp.where(first, pltpu.roll(t, 96, 1), -pltpu.roll(t, 32, 1))

    for pair in range(heads // 2):
        cols = slice(pair * 128, (pair + 1) * 128)
        q, k, v, g = q_ref[:, cols], k_ref[:, cols], v_ref[:, cols], g_ref[:, cols]
        go = g.astype(f32) * o_ref[:, cols].astype(f32)
        dq = dk = dv = None
        for side in range(2):
            mine = (lane // HEAD_DIM) == side
            keep = mine.astype(bf16)
            p = p_ref[0, pair * 2 + side]
            row = jnp.sum(jnp.where(mine, go, 0.0), -1, keepdims=True)
            gp = dot_nt(g, v * keep)
            gs = (p.astype(f32) * (gp - row)).astype(bf16)
            parts = (dot_nn(gs, k * keep), dot_tn(gs, q * keep), dot_tn(p, g * keep))
            if dq is None:
                dq, dk, dv = parts
            else:
                dq, dk, dv = dq + parts[0], dk + parts[1], dv + parts[2]
        d_ref[0, :, cols] = unrotate(dq * 0.125).astype(bf16)
        d_ref[1, :, cols] = unrotate(dk).astype(bf16)
        d_ref[2, :, cols] = dv.astype(bf16)


def attend_backward(q, k, v, attended, gatt, probs, table, first, steps, name):
    rows, _ = attended.shape
    seqs, _, seq, _ = probs.shape
    quad = 4
    lanes = quad * HEAD_DIM
    spec_in = pl.BlockSpec((seq, lanes), lambda s, g: (s, first + g))
    return pl.pallas_call(
        attend_back_kernel,
        grid=(seqs, steps),
        in_specs=[spec_in] * 5
        + [
            pl.BlockSpec((1, quad, seq, seq), lambda s, g: (s, first + g, 0, 0)),
            pl.BlockSpec(table.shape, lambda s, g: (0, 0)),
        ],
        out_specs=pl.BlockSpec((3, seq, lanes), lambda s, g: (0, s, g)),
        out_shape=jax.ShapeDtypeStruct((3, rows, lanes * steps), bf16),
        compiler_params=limit(16),
        cost_estimate=cost(8 * seqs * quad * steps * seq * seq * 256, 9_000_000 * steps),
        name=name,
    )(q, k, v, attended, gatt, probs, table)


def qkv_grad_kernel(extra, me_ref, x_ref, d_ref, *rest):
    me = me_ref[0]
    if extra:
        att_ref, g1_ref, s2_ref, s1_ref = rest[:4]
    keep_ref, send_ref, acc_ref = rest[-3:]
    width = x_ref.shape[1]

    def put(value, lo):
        cols = value.shape[1]
        acc_ref[:, :cols] = value
        spread(me, acc_ref.at[:, :cols], keep_ref, send_ref, slice(lo, lo + cols))
        return lo + cols

    cols = d_ref.shape[2]

    @pl.loop(0, 3)
    def _(part):
        acc_ref[:, :cols] = dot_tn(x_ref[...], d_ref[part])
        lo = pl.multiple_of(part * cols, 128)
        spread(me, acc_ref.at[:, :cols], keep_ref, send_ref, pl.ds(lo, cols))

    lo = 3 * cols
    if extra:
        lo = put(dot_tn(att_ref[...], g1_ref[...]), lo)
        row = lax.broadcasted_iota(jnp.int32, (8, width), 0)
        rows = jnp.where(row < 2, s2_ref[...], pltpu.roll(s1_ref[...], 2, 0)).astype(bf16)
        put(dot_tn(rows, unit_rows()), lo)


def qkv_grad(me, x, parts, extra, count, name):
    rows, width = x.shape
    cols = parts.shape[2]
    chips, shard_rows = count // 2, width // count
    total = 3 * cols + (width + 128 if extra else 0)
    shape = jax.ShapeDtypeStruct((chips, shard_rows, total), bf16)
    vmem = pl.BlockSpec(memory_space=pltpu.VMEM)
    return pl.pallas_call(
        functools.partial(qkv_grad_kernel, bool(extra)),
        in_specs=[SMEM] + [vmem] * (2 + len(extra)),
        out_specs=[vmem, vmem],
        out_shape=[shape, shape],
        scratch_shapes=[pltpu.VMEM((width, width), f32)],
        compiler_params=limit(20),
        cost_estimate=cost(2 * rows * width * total, 12_000_000),
        name=name,
    )(me, x, parts, *extra)


def input_grad_kernel(g1_ref, w_ref, *rest):
    out_ref = rest[-1]
    width = out_ref.shape[1]
    total = g1_ref[...].astype(f32)
    for p in range(3):
        lo = p * width
        for ref in rest[:-1]:
            total += dot_nt(ref[p], w_ref[:, lo : lo + ref.shape[2]])
            lo += ref.shape[2]
    out_ref[...] = total.astype(bf16)


def input_grad(g1, w_qkv, parts):
    rows, width = g1.shape
    block = 512
    by_row = pl.BlockSpec((block, width), lambda i: (i, 0))
    return pl.pallas_call(
        input_grad_kernel,
        grid=(rows // block,),
        in_specs=[by_row, whole(w_qkv.shape)]
        + [pl.BlockSpec((3, block, p.shape[2]), lambda i: (0, i, 0)) for p in parts],
        out_specs=by_row,
        out_shape=jax.ShapeDtypeStruct((rows, width), bf16),
        compiler_params=limit(20),
        cost_estimate=cost(6 * rows * width * width, 14_000_000),
        name="input_grad",
    )(g1, w_qkv, *parts)


def rope_tables(seq_len):
    frequency = rope_base ** (-np.arange(0, HEAD_DIM, 2, dtype=np.float32) / HEAD_DIM)
    frequency = jnp.asarray(np.tile(frequency.astype(np.float32), 4))[None, :]
    shape = (seq_len, 128)
    angles = lax.broadcasted_iota(jnp.int32, shape, 0).astype(f32) * frequency
    lane = lax.broadcasted_iota(jnp.int32, shape, 1)
    return jnp.where(lane // 32 % 2 == 0, jnp.cos(angles), jnp.sin(angles))


def spread_tables(table):
    shifted = pltpu.roll(table, 32, 1)
    even = lax.broadcasted_iota(jnp.int32, table.shape, 1) // 32 % 2 == 0
    return jnp.where(even, table, shifted), jnp.where(even, shifted, table)


def shards(
    tokens, segment_ids, qkv_weight, out_weight, gate_weight, up_weight, down_weight,
    norm1_gain, norm1_bias, norm2_gain, norm2_bias, out_grad,
):
    count = lax.axis_size("shard")
    me = lax.axis_index("shard").astype(jnp.int32).reshape(1)
    batches, seq, width = tokens.shape
    shard_rows = qkv_weight.shape[0]
    down_rows = down_weight.shape[0]
    hidden = gate_weight.shape[1]
    rows = batches * seq
    chips = count // 2

    x = tokens.reshape(rows, width)
    cot = out_grad.reshape(rows, width)
    table = rope_tables(seq)
    vectors = jnp.stack([norm1_gain, norm1_bias, norm2_gain, norm2_bias], 1)
    vectors = jnp.pad(vectors, ((0, 0), (0, 124)))
    odd = (lax.axis_index("rep") % 2 == 1).reshape(1, 1)

    pieces_a = gather_direct(qkv_weight)
    own_b = jnp.concatenate([gate_weight, up_weight, out_weight, vectors], 1)
    seg = segment_ids.reshape(batches, 1, seq)
    table, seg, own_b, odd, ready = tie((table, seg, own_b, odd, pieces_a[0][2]))
    pieces_a = [(r, lo, tie(p, ready, seg, odd, table)) for r, lo, p in pieces_a]
    far_a = tuple(p for _, _, p in pieces_a[1:])
    pieces_a = with_partner(pieces_a)
    own_b = tie(own_b, far_a)
    if count == 8:
        first_b = gather_first(own_b)
        first_c = gather_first(tie(down_weight, far_a))
    else:
        pieces_b = gather_direct(own_b)
        pieces_c = gather_direct(down_weight)
    q, k, v, attended, probs, w_qkv = front(me, x, table, seg, pieces_a, shard_rows)
    if count == 8:
        first_b = tie(first_b, attended)
        pieces_b = gather_second(own_b, first_b)
        first_c = tie(first_c, first_b)
        pieces_c = gather_second(down_weight, first_c)
    pieces_b = with_partner(pieces_b)
    near_c = with_partner(pieces_c[:3])
    hidden_low, back_gate, back_up, low, n1, inv1, vec, w_out = gate_forward(
        me, x, attended, pieces_b, shard_rows, hidden
    )
    if count == 8:
        pieces_c = near_c + with_partner([(r, lo, tie(p, low)) for r, lo, p in pieces_c[3:]])
    else:
        pieces_c = with_partner(pieces_c)
    output, g2low, sums2, d_keep, d_send, w_down = down_forward(
        me, hidden_low, n1, cot, vec, pieces_c, down_rows, chips
    )
    steps = hidden // 768 // 2
    flow_d = Flow(d_keep, d_send, odd, False)
    ready = sums2
    grads1 = hidden_grad(
        me, tie(g2low, ready), low, back_gate, back_up, w_down, 0, steps, count, "hidden_grad_1"
    )
    flow_e = Flow(*grads1[4:], odd, False)
    ready = advance(grads1[0], flow_d)
    grads2 = hidden_grad(
        me, tie(grads1[2], ready), low, *grads1[:2], grads1[3], steps, steps, count, "hidden_grad_2"
    )
    flow_f = Flow(*grads2[4:], odd, False)
    ready = advance(grads2[0], flow_e)
    g1low, gatt, sums1 = mixed_grad(
        me, *grads2[:2], tie(grads2[2], ready), n1, inv1, vec, w_out, pieces_b, shard_rows
    )
    ready = advance(g1low, flow_f, flow_d)
    back_a = attend_backward(
        q, k, v, attended, tie(gatt, ready), probs, table, 0, 2, "attend_bwd_1"
    )
    ready = advance(back_a, flow_e, flow_d)
    a_keep, a_send = qkv_grad(
        me, x, tie(back_a, ready), (attended, g1low, sums2, sums1), count, "qkv_out_grad_1"
    )
    flow_a = Flow(a_keep, a_send, odd, False)
    ready = advance(a_keep, flow_f, flow_e, flow_d)
    back_b = attend_backward(
        q, k, v, attended, tie(gatt, ready), probs, table, 2, 1, "attend_bwd_2"
    )
    ready = advance(back_b, flow_a, flow_f, flow_e, flow_d)
    b_keep, b_send = qkv_grad(me, x, tie(back_b, ready), (), count, "qkv_grad_2")
    flow_b = Flow(b_keep, b_send, odd, True)
    ready = advance(b_keep, flow_d)
    ready = advance(ready, flow_b)
    in_grad = input_grad(tie(g1low, ready), w_qkv, [back_a, back_b])
    ready = advance(in_grad, flow_a)
    ready = advance(ready, flow_f, flow_e)
    flow_a.pass_on = True
    flow_b.other = flow_a.step(ready)
    ready = advance(ready, flow_b, flow_f, flow_e)
    d_sum, e_sum, f_sum = [flow.finish() for flow in (flow_d, flow_e, flow_f)]
    total = flow_b.finish()
    a_sum, b_sum = total[:, : a_keep.shape[2]], total[:, a_keep.shape[2] :]

    block = 768
    hidden_sums = (e_sum, f_sum)
    pick = lambda part: jnp.concatenate(
        [
            s[:, (2 * j + part) * block : (2 * j + part + 1) * block]
            for s in hidden_sums
            for j in range(steps)
        ],
        1,
    )
    cols_a, cols_b = back_a.shape[2], back_b.shape[2]
    qkv_sum = jnp.concatenate(
        [
            s[:, p * c : (p + 1) * c]
            for p in range(3)
            for s, c in ((a_sum, cols_a), (b_sum, cols_b))
        ],
        1,
    )
    out_sum = a_sum[:, 3 * cols_a : 3 * cols_a + width]
    vec_sum = a_sum[:, 3 * cols_a + width :]
    return (
        output.reshape(tokens.shape),
        in_grad.reshape(tokens.shape),
        qkv_sum,
        out_sum,
        pick(0),
        pick(1),
        d_sum,
        vec_sum[:, 2],
        vec_sum[:, 3],
        vec_sum[:, 0],
        vec_sum[:, 1],
    )


def solution(mesh):
    rows3 = P(None, ("shard", "rep"), None)
    rows2 = P("shard", None)
    rows1 = P("shard")
    in_specs = (rows3, P(None, ("shard", "rep"))) + (rows2,) * 5 + (rows1,) * 4 + (rows3,)
    out_specs = (rows3, rows3) + (rows2,) * 5 + (rows1,) * 4
    return jax.shard_map(shards, mesh=mesh, in_specs=in_specs, out_specs=out_specs, check_vma=False)
```

```python
import functools

import jax
import jax.numpy as jnp
import numpy as np
from jax import lax
from jax.experimental import pallas as pl
from jax.experimental.pallas import tpu as pltpu
from jax.sharding import PartitionSpec as P

HEAD_DIM = 64
norm_eps = 1e-12
rope_base = 1000.0
masked_score = -1e30
f32 = jnp.float32
bf16 = jnp.bfloat16
ANY = pl.BlockSpec(memory_space=pl.ANY)
SMEM = pl.BlockSpec(memory_space=pltpu.SMEM)


def dot_nn(a, b):
    return lax.dot_general(a, b, (((1,), (0,)), ((), ())), preferred_element_type=f32)


def dot_nt(a, b):
    return lax.dot_general(a, b, (((1,), (1,)), ((), ())), preferred_element_type=f32)


def dot_tn(a, b):
    return lax.dot_general(a, b, (((0,), (0,)), ((), ())), preferred_element_type=f32)


def whole(shape):
    return pl.BlockSpec(shape, lambda *_: (0,) * len(shape))


def tie(value, *deps):
    return lax.optimization_barrier((value, deps))[0]


def xor_permute(x, bit):
    count = lax.axis_size("shard")
    return lax.ppermute(x, "shard", [(i, i ^ bit) for i in range(count)])


def with_partner(pieces):
    return pieces + [(r | 1, lo, xor_permute(p, 1)) for r, lo, p in pieces]


def gather_direct(own):
    return [(0, 0, own)] + [(r, 0, xor_permute(own, r)) for r in range(2, lax.axis_size("shard"), 2)]


def gather_first(own):
    return xor_permute(own, 2), xor_permute(own, 4)


def gather_second(own, first):
    half = own.shape[0] // 2
    from_x, from_y = first
    far = (xor_permute(from_y[:half], 2), xor_permute(from_x[half:], 4))
    return [(0, 0, own), (2, 0, from_x), (4, 0, from_y), (6, 0, far[0]), (6, half, far[1])]


def add_parts(parts):
    return functools.reduce(jnp.add, [p.astype(f32) for p in parts]).astype(bf16)


def rep_permute(x, pairs):
    return lax.ppermute(x, "rep", pairs)


def load_kernel(jobs, body, *refs):
    operands, rest = refs[: body.operands], refs[body.operands :]
    outs, (hold, sems) = rest[: body.outs], rest[body.outs :]
    half = hold.shape[1]
    copies = []
    for i, (operand, block, part) in enumerate(jobs):
        ref = operands[operand]
        src = ref.at[block, pl.ds(part * half, half), :] if block is not None else ref
        copies.append(pltpu.make_async_copy(src, hold.at[i], sems.at[i]))
        copies[-1].start()
    for copy in copies:
        copy.wait()
    body(hold, *outs)


class Fold:
    def __init__(self, operands, outs, body):
        self.operands, self.outs, self.body = operands, outs, body

    def __call__(self, hold, *outs):
        self.body(hold, *outs)


def fold_call(arrays, jobs, out_shapes, body, half, cols, name):
    count = len(out_shapes)
    return pl.pallas_call(
        functools.partial(load_kernel, jobs, Fold(len(arrays), count, body)),
        in_specs=[pl.BlockSpec(memory_space=pl.ANY)] * len(arrays),
        out_specs=[pl.BlockSpec(memory_space=pltpu.VMEM)] * count,
        out_shape=[jax.ShapeDtypeStruct(s, bf16) for s in out_shapes],
        scratch_shapes=[
            pltpu.VMEM((len(jobs), half, cols), bf16),
            pltpu.SemaphoreType.DMA((len(jobs),)),
        ],
        compiler_params=pltpu.CompilerParams(vmem_limit_bytes=8 << 20),
        cost_estimate=cost(len(jobs) * half * cols, 3 * len(jobs) * half * cols),
        name=name,
    )(*arrays)


def each_rows(rows, step, body):
    @pl.loop(0, rows // step)
    def _(i):
        body(pl.ds(pl.multiple_of(i * step, step), step))


def plus(hold, at, *slots):
    return functools.reduce(jnp.add, [hold[s, at, :].astype(f32) for s in slots]).astype(bf16)


def row_step(half):
    return 16 if half % 16 == 0 else 8


def fold_first(keep, got):
    _, rows, cols = keep.shape
    half = rows // 2
    jobs = [(a, q, p) for q, p in ((1, 0), (3, 0), (2, 1), (3, 1)) for a in (0, 1)]

    def body(hold, x_ref, y_ref):
        def some(at):
            for n, ref in enumerate((x_ref, x_ref, y_ref, y_ref)):
                ref[n % 2, at, :] = plus(hold, at, 2 * n, 2 * n + 1)

        each_rows(half, row_step(half), some)

    return fold_call([keep, got], jobs, [(2, half, cols)] * 2, body, half, cols, "fold_first")


def fold_second(keep, got, from_x, from_y):
    _, rows, cols = keep.shape
    half = rows // 2
    jobs = [(0, 2, 0), (1, 2, 0), (2, 1, 0), (0, 1, 1), (1, 1, 1), (3, 1, 0)]

    def body(hold, y_ref, x_ref):
        def some(at):
            y_ref[at, :] = plus(hold, at, 0, 1, 2)
            x_ref[at, :] = plus(hold, at, 3, 4, 5)

        each_rows(half, row_step(half), some)

    return fold_call(
        [keep, got, from_x, from_y], jobs, [(half, cols)] * 2, body, half, cols, "fold_second"
    )


def fold_own(keep, got, from_x, from_y, last_y, last_x):
    _, rows, cols = keep.shape
    half = rows // 2
    jobs = [
        (0, 0, 0), (1, 0, 0), (2, 0, 0), (4, None, 0), (0, 0, 1), (1, 0, 1), (3, 0, 0), (5, None, 0)
    ]

    def body(hold, own_ref):
        def some(at):
            own_ref[0, at, :] = plus(hold, at, 0, 1, 2, 3)
            own_ref[1, at, :] = plus(hold, at, 4, 5, 6, 7)

        each_rows(half, row_step(half), some)

    own = fold_call(
        [keep, got, from_x, from_y, last_y, last_x], jobs, [(2, half, cols)], body, half, cols, "fold_own"
    )[0]
    return own.reshape(rows, cols)


def fold_call_whole(arrays, jobs, pairs, name):
    _, rows, cols = arrays[0].shape

    def body(hold, out_ref):
        def some(at):
            for n, slots in enumerate(pairs):
                out_ref[n, at, :] = plus(hold, at, *slots)

        each_rows(rows, row_step(rows), some)

    return fold_call(arrays, jobs, [(len(pairs), rows, cols)], body, rows, cols, name)[0]


def fold_line_first(keep, got, near):
    jobs = [(a, q, 0) for q in (near, 3) for a in (0, 1)]
    return fold_call_whole([keep, got], jobs, [(0, 1), (2, 3)], "fold_line_first")


def fold_line_second(keep, got, came, far):
    jobs = [(0, far, 0), (1, far, 0), (2, 1, 0)]
    return fold_call_whole([keep, got, came], jobs, [(0, 1, 2)], "fold_line_second")


def fold_line_own(keep, got, came, last):
    jobs = [(0, 0, 0), (1, 0, 0), (2, 0, 0), (3, 0, 0)]
    return fold_call_whole([keep, got, came, last], jobs, [(0, 1, 2, 3)], "fold_line_own")[0]


class Flow:
    def __init__(self, keep, send, odd, direct=False):
        self.held = keep
        self.odd = odd
        self.other = None
        self.pass_on = False
        self.pending = xor_permute(send, 1)
        self.stage = 0
        self.way = direct if keep.shape[0] == 4 and direct in (1, 2) and direct is not True else 0
        self.pair = keep.shape[0] == 4 and not direct
        self.line = lax.axis_size("rep") == 4

    def step(self, *deps):
        got = tie(self.pending, *deps) if deps else self.pending
        stage = self.stage
        if stage == 0:
            self.got = got
            if self.way:
                self.ready = fold_line_first(self.held, got, self.way)
                self.pending = xor_permute(self.ready, 2 * self.way)
            elif self.pair:
                self.ready = fold_first(self.held, got)
                self.pending = (xor_permute(self.ready[0], 2), xor_permute(self.ready[1], 4))
            else:
                self.ready = [self.held[q] + got[q] for q in range(got.shape[0])]
                self.pending = [xor_permute(self.ready[q], 2 * q) for q in range(1, got.shape[0])]
        elif stage == 1 and self.way:
            self.first = got
            self.ready = fold_line_second(self.held, self.got, got, 3 - self.way)
            self.pending = xor_permute(self.ready, 2 * (3 - self.way))
        elif stage == 1 and self.pair:
            self.first = got
            if self.pair:
                self.ready = fold_second(self.held, self.got, *got)
                self.pending = (xor_permute(self.ready[0], 4), xor_permute(self.ready[1], 2))
        elif stage <= 2:
            self.stage = 2
            if self.way:
                self.ready = fold_line_own(self.held, self.got, self.first, got)
            elif self.pair:
                self.ready = fold_own(self.held, self.got, *self.first, *got)
            else:
                self.ready = add_parts([self.ready[0]] + list(got))
            if self.other is not None:
                self.ready = jnp.concatenate([self.other, self.ready], 1)
            if self.pass_on:
                self.stage = 6
                return self.ready
            if self.line:
                half = self.ready.shape[0] // 2
                self.mine = jnp.where(self.odd, self.ready[half:], self.ready[:half])
                self.ready = jnp.where(self.odd, self.ready[:half], self.ready[half:])
                self.pending = rep_permute(self.ready, [(0, 1), (1, 0), (2, 3), (3, 2)])
            else:
                self.pending = lax.psum(self.ready, "rep")
        elif not self.line:
            self.ready = got
        elif stage == 3:
            self.ready = add_parts([self.mine, got])
            self.pending = rep_permute(self.ready, [(0, 2), (2, 0), (1, 3), (3, 1)])
        elif stage == 4:
            self.ready = add_parts([self.ready, got])
            self.pending = rep_permute(self.ready, [(0, 1), (1, 0), (2, 3), (3, 2)])
        else:
            low, high = (jnp.where(self.odd, a, b) for a, b in ((got, self.ready), (self.ready, got)))
            self.ready = jnp.concatenate([low, high]).astype(f32)
        self.stage += 1
        return self.ready

    def finish(self):
        while self.stage < 6:
            self.step()
        return self.ready.astype(f32)


def advance(dep, *flows):
    return tuple(flow.step(dep) for flow in flows)


def piece_copies(metas, refs, me, shard_rows, dst, src_lo, dst_lo, cols, sems):
    copies = []
    for i, ((rel, first, rows), ref) in enumerate(zip(metas, refs)):
        at = pl.multiple_of((me ^ rel) * shard_rows + first, 8)
        copies.append(
            pltpu.make_async_copy(
                ref.at[:, pl.ds(src_lo, cols)],
                dst.at[pl.ds(at, rows), pl.ds(dst_lo, cols)],
                sems.at[i],
            )
        )
    return copies


def start_all(copies):
    for copy in copies:
        copy.start()


def wait_all(copies):
    for copy in copies:
        copy.wait()


def metas_of(pieces):
    return tuple((rel, first, p.shape[0]) for rel, first, p in pieces)


def in_hbm(x):
    return pltpu.with_memory_space_constraint(x, pltpu.HBM)


def arrays_of(pieces):
    return [in_hbm(p) for _, _, p in pieces]


def half_mask(shape):
    lane = lax.broadcasted_iota(jnp.int32, shape, len(shape) - 1)
    return (lane % HEAD_DIM) < HEAD_DIM // 2


def unit_rows():
    shape = (8, 128)
    return (
        lax.broadcasted_iota(jnp.int32, shape, 0) == lax.broadcasted_iota(jnp.int32, shape, 1)
    ).astype(bf16)


def normalize(h):
    centre = h - jnp.mean(h, -1, keepdims=True)
    inv = lax.rsqrt(jnp.mean(centre * centre, -1, keepdims=True) + norm_eps)
    return centre * inv, inv


def norm_back(e, n, inv):
    return inv * (e - jnp.mean(e, -1, keepdims=True) - n * jnp.mean(e * n, -1, keepdims=True))


def spread(me, acc_ref, keep_ref, send_ref, cols):
    rows = keep_ref.shape[1]
    chip, core = me // 2, me & 1
    for q in range(keep_ref.shape[0]):
        base = (chip ^ q) * 2
        keep_ref[q, :, cols] = acc_ref[
            pl.ds(pl.multiple_of((base + core) * rows, 8), rows), :
        ].astype(bf16)
        send_ref[q, :, cols] = acc_ref[
            pl.ds(pl.multiple_of((base + 1 - core) * rows, 8), rows), :
        ].astype(bf16)


def cost(flops, read, transcendentals=0):
    return pl.CostEstimate(flops=1000, bytes_accessed=1000, transcendentals=0)


def front_kernel(metas, shard_rows, me_ref, x_ref, table_ref, row_ref, *rest):
    refs, rest = rest[: len(metas)], rest[len(metas) :]
    q_ref, k_ref, v_ref, att_ref, p_ref, w_out, w_ref, bias_ref, sems, back_sem = rest
    s, g = pl.program_id(0), pl.program_id(1)
    width = x_ref.shape[1]
    lanes = p_ref.shape[1] * HEAD_DIM
    copies = piece_copies(metas, refs, me_ref[0], shard_rows, w_ref, 0, 0, 3 * width, sems)
    back = pltpu.make_async_copy(w_ref, w_out, back_sem)

    @pl.when((s == 0) & (g == 0))
    def _():
        start_all(copies)
        wait_all(copies)
        back.start()

    @pl.when(g == 0)
    def _():
        across = jnp.broadcast_to(row_ref[0].astype(f32), bias_ref.shape)
        down = lax.broadcasted_iota(jnp.int32, bias_ref.shape, 0)
        own = lax.broadcasted_iota(jnp.int32, bias_ref.shape, 1) == down
        column = jnp.sum(jnp.where(own, across, 0.0), -1, keepdims=True)
        bias_ref[...] = jnp.where(across == column, 0.0, masked_score).astype(f32)
        x = x_ref[...]
        first = half_mask((x.shape[0], 128))
        cos, sin = spread_tables(table_ref[...])
        sin = jnp.where(first, -sin, sin)
        for part, ref in enumerate((q_ref, k_ref, v_ref)):
            y = dot_nn(x, w_ref[:, part * width : (part + 1) * width])
            for b in range(width // 128):
                cols = slice(b * 128, (b + 1) * 128)
                u = y[:, cols]
                if part < 2:
                    turned = jnp.where(first, pltpu.roll(u, 96, 1), pltpu.roll(u, 32, 1))
                    u = u * cos + turned * sin
                if part == 0:
                    u = u * 0.125
                ref[:, cols] = u.astype(bf16)

    lane = lax.broadcasted_iota(jnp.int32, (1, 128), 1)
    for pair in range(lanes // 128):
        at = pl.ds(pl.multiple_of(g * lanes + pair * 128, 128), 128)
        q, k, v = q_ref[:, at], k_ref[:, at], v_ref[:, at]
        acc = None
        for side in range(2):
            mine = ((lane // HEAD_DIM) == side).astype(bf16)
            score = dot_nt(q, k * mine) + bias_ref[...]
            e = jnp.exp(score - jnp.max(score, -1, keepdims=True))
            inv = 1.0 / jnp.sum(e, -1, keepdims=True)
            p = (e * inv).astype(bf16)
            p_ref[0, pair * 2 + side] = p
            part = dot_nn(p, v * mine)
            acc = part if acc is None else acc + part
        att_ref[:, pair * 128 : (pair + 1) * 128] = acc.astype(bf16)

    @pl.when((s == pl.num_programs(0) - 1) & (g == pl.num_programs(1) - 1))
    def _():
        back.wait()


def front(me, x, table, seg_row, pieces, shard_rows):
    rows, width = x.shape
    metas = metas_of(pieces)
    seqs, _, seq = seg_row.shape
    heads = width // HEAD_DIM
    quad = 4
    lanes = quad * HEAD_DIM
    by_seq = pl.BlockSpec((seq, width), lambda s, g: (s, 0))
    wide = jax.ShapeDtypeStruct((rows, width), bf16)
    return pl.pallas_call(
        functools.partial(front_kernel, metas, shard_rows),
        grid=(seqs, width // lanes),
        in_specs=[
            SMEM, by_seq, whole(table.shape),
            pl.BlockSpec((1, 1, seq), lambda s, g: (s, 0, 0)),
        ]
        + [ANY] * len(metas),
        out_specs=[by_seq] * 3
        + [
            pl.BlockSpec((seq, lanes), lambda s, g: (s, g)),
            pl.BlockSpec((1, quad, seq, seq), lambda s, g: (s, g, 0, 0)),
            ANY,
        ],
        out_shape=[wide] * 4
        + [
            jax.ShapeDtypeStruct((seqs, heads, seq, seq), bf16),
            jax.ShapeDtypeStruct((width, 3 * width), bf16),
        ],
        scratch_shapes=[
            pltpu.VMEM((width, 3 * width), bf16),
            pltpu.VMEM((seq, seq), f32),
            pltpu.SemaphoreType.DMA((len(metas),)),
            pltpu.SemaphoreType.DMA,
        ],
        cost_estimate=cost(
            6 * rows * width * width + 4 * seqs * heads * seq * seq * 256,
            30_000_000,
            seqs * heads * seq * seq,
        ),
        name="qkv_attend",
    )(me, x, table, seg_row, *[p for _, _, p in pieces])


VM = pl.BlockSpec(memory_space=pltpu.VMEM)
HBM = pl.BlockSpec(memory_space=pltpu.HBM)


def in_vmem(shape, dtype=bf16):
    return pltpu.VMEM(shape, dtype)


def limit(mib):
    return pltpu.CompilerParams(vmem_limit_bytes=mib << 20)


def gate_kernel(metas, shard_rows, me_ref, tok_ref, att_ref, *rest):
    refs, rest = rest[: len(metas)], rest[len(metas) :]
    h_ref, a_ref, b_ref, x_ref, n1_ref, inv_ref, vec_ref, wo_ref = rest[:8]
    wg_ref, wv_ref, sems, sems_o = rest[8:]
    hidden = a_ref.shape[1]
    width = wo_ref.shape[1]
    block = 768
    steps = hidden // block
    me = me_ref[0]

    def spans(j):
        return pl.multiple_of(j * block, block), pl.multiple_of(hidden + j * block, block)

    def copies(j):
        both = []
        for part, lo in enumerate(spans(j)):
            both += piece_copies(metas, refs, me, shard_rows, wg_ref, lo, lo, block, sems.at[j, part])
        return both

    copies_o = piece_copies(
        metas, refs, me, shard_rows, wo_ref, 2 * hidden, 0, width, sems_o.at[0]
    ) + piece_copies(metas, refs, me, shard_rows, wv_ref, 2 * hidden + width, 0, 128, sems_o.at[1])
    start_all(copies_o)

    @pl.loop(0, steps)
    def _(j):
        start_all(copies(j))

    wait_all(copies_o)
    vec_ref[...] = dot_nt(unit_rows(), wv_ref[...])

    @pl.loop(0, 2)
    def _(i):
        rows = tok_ref.shape[0] // 2
        at = pl.ds(pl.multiple_of(i * rows, 8), rows)
        n, inv = normalize(tok_ref[at, :].astype(f32) + dot_nn(att_ref[at, :], wo_ref[...]))
        n1_ref[at, :] = n.astype(bf16)
        inv_ref[at, :] = jnp.broadcast_to(inv, (rows, inv_ref.shape[1]))
        x_ref[at, :] = (n * vec_ref[0:1] + vec_ref[1:2]).astype(bf16)

    @pl.loop(0, steps)
    def _(j):
        wait_all(copies(j))
        gate_at, up_at = (pl.ds(lo, block) for lo in spans(j))
        half = x_ref.shape[0] // 2

        @pl.loop(0, 2)
        def _(r):
            rows = pl.ds(pl.multiple_of(r * half, half), half)
            gate = dot_nn(x_ref[rows, :], wg_ref[:, gate_at])
            up = dot_nn(x_ref[rows, :], wg_ref[:, up_at])
            s = 0.5 * jnp.tanh(0.5 * gate) + 0.5
            act = gate * s
            h_ref[rows, gate_at] = (act * up).astype(bf16)
            b_ref[rows, gate_at] = act.astype(bf16)
            a_ref[rows, gate_at] = (up * (s + act * (1.0 - s))).astype(bf16)


def gate_forward(me, tokens, attended, pieces, shard_rows, hidden):
    rows, width = tokens.shape
    metas = metas_of(pieces)
    return pl.pallas_call(
        functools.partial(gate_kernel, metas, shard_rows),
        in_specs=[SMEM, VM, VM] + [ANY] * len(metas),
        out_specs=[VM] * 8,
        out_shape=[in_vmem((rows, hidden))] * 3
        + [
            in_vmem((rows, width)),
            in_vmem((rows, width)),
            in_vmem((rows, 128), f32),
            in_vmem((8, width), f32),
            in_vmem((width, width)),
        ],
        scratch_shapes=[
            pltpu.VMEM((width, 2 * hidden), bf16),
            pltpu.VMEM((width, 128), bf16),
            pltpu.SemaphoreType.DMA((hidden // 768, 2, len(metas))),
            pltpu.SemaphoreType.DMA((2, len(metas))),
        ],
        compiler_params=limit(19),
        cost_estimate=cost(4 * rows * width * hidden, 10_000_000, rows * hidden),
        name="out_gate_up",
    )(me, tokens, attended, *arrays_of(pieces))


def down_kernel(metas, shard_rows, me_ref, h_ref, n1_ref, cot_ref, vec_ref, *rest):
    refs = rest[: len(metas)]
    out_ref, low_ref, sums_ref, keep_ref, send_ref, w_ref, acc_ref, sems = rest[len(metas) :]
    me = me_ref[0]
    copies = piece_copies(metas, refs, me, shard_rows, w_ref, 0, 0, w_ref.shape[1], sems)
    start_all(copies)
    sums_ref[...] = jnp.zeros_like(sums_ref)
    wait_all(copies)
    block = 256

    @pl.loop(0, h_ref.shape[0] // block)
    def _(i):
        at = pl.ds(pl.multiple_of(i * block, block), block)
        mixed = n1_ref[at, :].astype(f32) * vec_ref[0:1] + vec_ref[1:2]
        n, inv = normalize(mixed + dot_nn(h_ref[at, :], w_ref[...]))
        out_ref[at, :] = (n * vec_ref[2:3] + vec_ref[3:4]).astype(bf16)
        cot = cot_ref[at, :].astype(f32)
        sums_ref[0:1] += jnp.sum(cot * n, 0, keepdims=True)
        sums_ref[1:2] += jnp.sum(cot, 0, keepdims=True)
        low_ref[at, :] = norm_back(cot * vec_ref[2:3], n, inv).astype(bf16)

    per_chip = acc_ref.shape[0]
    half = per_chip // 2
    core = me & 1

    @pl.loop(0, keep_ref.shape[0])
    def _(q):
        lo = pl.multiple_of(((me // 2) ^ q) * per_chip, 128)
        acc_ref[...] = dot_tn(h_ref[:, pl.ds(lo, per_chip)], low_ref[...])
        keep_ref[q] = acc_ref[pl.ds(pl.multiple_of(core * half, 8), half), :].astype(bf16)
        send_ref[q] = acc_ref[pl.ds(pl.multiple_of((1 - core) * half, 8), half), :].astype(bf16)


def down_forward(me, hidden_low, n1, cot, vec, pieces, shard_rows, chips):
    rows, hidden = hidden_low.shape
    width = n1.shape[1]
    metas = metas_of(pieces)
    per_chip = hidden // chips
    return pl.pallas_call(
        functools.partial(down_kernel, metas, shard_rows),
        in_specs=[SMEM, VM, VM, VM, VM] + [ANY] * len(metas),
        out_specs=[VM] * 6,
        out_shape=[
            jax.ShapeDtypeStruct((rows, width), bf16),
            in_vmem((rows, width)),
            in_vmem((8, width), f32),
            jax.ShapeDtypeStruct((chips, per_chip // 2, width), bf16),
            jax.ShapeDtypeStruct((chips, per_chip // 2, width), bf16),
            in_vmem((hidden, width)),
        ],
        scratch_shapes=[
            pltpu.VMEM((per_chip, width), f32),
            pltpu.SemaphoreType.DMA((len(metas),)),
        ],
        compiler_params=limit(19),
        cost_estimate=cost(4 * rows * width * hidden, 10_000_000, rows),
        name="down_norm_grad",
    )(me, hidden_low, n1, cot, vec, *arrays_of(pieces))


def hidden_grad_kernel(
    first, steps, me_ref, g_ref, x_ref, a_ref, b_ref, w_ref, gg_ref, gu_ref, _g, _w, keep_ref, send_ref, acc_ref
):
    block = 768

    @pl.loop(0, steps)
    def _(j):
        cols = pl.ds(pl.multiple_of((first + j) * block, block), block)
        half = g_ref.shape[0] // 2

        @pl.loop(0, 2)
        def _(r):
            rows = pl.ds(pl.multiple_of(r * half, half), half)
            gh = dot_nt(g_ref[rows, :], w_ref[cols, :])
            gg_ref[rows, cols] = (gh * a_ref[rows, cols].astype(f32)).astype(bf16)
            gu_ref[rows, cols] = (gh * b_ref[rows, cols].astype(f32)).astype(bf16)
        for part, ref in enumerate((gg_ref, gu_ref)):
            acc_ref[...] = dot_tn(x_ref[...], ref[:, cols])
            lo = pl.multiple_of((2 * j + part) * block, block)
            spread(me_ref[0], acc_ref, keep_ref, send_ref, pl.ds(lo, block))


def hidden_grad(me, g2low, low, a, b, w_down, first, steps, count, name):
    rows, width = g2low.shape
    block = 768
    chips, shard_rows = count // 2, width // count
    part = jax.ShapeDtypeStruct((chips, shard_rows, 2 * block * steps), bf16)
    return pl.pallas_call(
        functools.partial(hidden_grad_kernel, first, steps),
        in_specs=[SMEM, VM, VM, VM, VM, VM],
        out_specs=[VM] * 6,
        out_shape=[
            in_vmem(a.shape), in_vmem(b.shape), in_vmem(g2low.shape), in_vmem(w_down.shape), part, part
        ],
        input_output_aliases={3: 0, 4: 1, 1: 2, 5: 3},
        scratch_shapes=[pltpu.VMEM((width, block), f32)],
        compiler_params=limit(19),
        cost_estimate=cost(6 * rows * width * block * steps, 5_000_000),
        name=name,
    )(me, g2low, low, a, b, w_down)


def mixed_grad_kernel(
    metas, shard_rows, me_ref, gg_ref, gu_ref, g2_ref, n1_ref, inv_ref, vec_ref, wo_ref, *rest
):
    refs, rest = rest[: len(metas)], rest[len(metas) :]
    low_ref, gatt_ref, sums_ref, _gg, _gu, _g2, w_ref, sems = rest
    hidden = gg_ref.shape[1]
    block = 256
    copies = [
        piece_copies(
            metas, refs, me_ref[0], shard_rows, w_ref, c * hidden, c * hidden, hidden, sems.at[c]
        )
        for c in range(2)
    ]
    start_all(copies[0])
    start_all(copies[1])
    sums_ref[...] = jnp.zeros_like(sums_ref)

    @pl.loop(0, gg_ref.shape[0] // block)
    def _(i):
        at = pl.ds(pl.multiple_of(i * block, block), block)

        @pl.when(i == 0)
        def _():
            wait_all(copies[0])

        gm = g2_ref[at, :].astype(f32) + dot_nt(gg_ref[at, :], w_ref[:, :hidden])

        @pl.when(i == 0)
        def _():
            wait_all(copies[1])

        gm += dot_nt(gu_ref[at, :], w_ref[:, hidden:])
        n = n1_ref[at, :].astype(f32)
        sums_ref[0:1] += jnp.sum(gm * n, 0, keepdims=True)
        sums_ref[1:2] += jnp.sum(gm, 0, keepdims=True)
        low = norm_back(gm * vec_ref[0:1], n, inv_ref[at, 0:1]).astype(bf16)
        low_ref[at, :] = low
        gatt_ref[at, :] = dot_nt(low, wo_ref[...]).astype(bf16)


def mixed_grad(me, gg, gu, g2, n1, inv1, vec, w_out, pieces, shard_rows):
    rows, width = g2.shape
    hidden = gg.shape[1]
    metas = metas_of(pieces)
    return pl.pallas_call(
        functools.partial(mixed_grad_kernel, metas, shard_rows),
        in_specs=[SMEM] + [VM] * 7 + [ANY] * len(metas),
        out_specs=[VM] * 6,
        out_shape=[
            jax.ShapeDtypeStruct((rows, width), bf16),
            jax.ShapeDtypeStruct((rows, width), bf16),
            jax.ShapeDtypeStruct((8, width), f32),
            in_vmem(gg.shape),
            in_vmem(gu.shape),
            in_vmem(g2.shape),
        ],
        input_output_aliases={1: 3, 2: 4, 3: 5},
        scratch_shapes=[
            pltpu.VMEM((width, 2 * hidden), bf16),
            pltpu.SemaphoreType.DMA((2, len(metas))),
        ],
        compiler_params=limit(19),
        cost_estimate=cost(4 * rows * width * hidden + 2 * rows * width * width, 15_000_000),
        name="mixed_grad",
    )(me, gg, gu, g2, n1, inv1, vec, w_out, *arrays_of(pieces))[:3]


def attend_back_kernel(
    q_ref, k_ref, v_ref, o_ref, g_ref, p_ref, table_ref, d_ref
):
    heads = p_ref.shape[1]
    lane = lax.broadcasted_iota(jnp.int32, (1, 128), 1)
    first = half_mask(table_ref.shape)
    cos, sin = spread_tables(table_ref[...])

    def unrotate(g):
        t = g * sin
        return g * cos + jnp.where(first, pltpu.roll(t, 96, 1), -pltpu.roll(t, 32, 1))

    for pair in range(heads // 2):
        cols = slice(pair * 128, (pair + 1) * 128)
        q, k, v, g = q_ref[:, cols], k_ref[:, cols], v_ref[:, cols], g_ref[:, cols]
        go = g.astype(f32) * o_ref[:, cols].astype(f32)
        dq = dk = dv = None
        for side in range(2):
            mine = (lane // HEAD_DIM) == side
            keep = mine.astype(bf16)
            p = p_ref[0, pair * 2 + side]
            row = jnp.sum(jnp.where(mine, go, 0.0), -1, keepdims=True)
            gp = dot_nt(g, v * keep)
            gs = (p.astype(f32) * (gp - row)).astype(bf16)
            parts = (dot_nn(gs, k * keep), dot_tn(gs, q * keep), dot_tn(p, g * keep))
            if dq is None:
                dq, dk, dv = parts
            else:
                dq, dk, dv = dq + parts[0], dk + parts[1], dv + parts[2]
        d_ref[0, :, cols] = unrotate(dq * 0.125).astype(bf16)
        d_ref[1, :, cols] = unrotate(dk).astype(bf16)
        d_ref[2, :, cols] = dv.astype(bf16)


def attend_backward(q, k, v, attended, gatt, probs, table, first, steps, name):
    rows, _ = attended.shape
    seqs, _, seq, _ = probs.shape
    quad = 4
    lanes = quad * HEAD_DIM
    spec_in = pl.BlockSpec((seq, lanes), lambda s, g: (s, first + g))
    return pl.pallas_call(
        attend_back_kernel,
        grid=(seqs, steps),
        in_specs=[spec_in] * 5
        + [
            pl.BlockSpec((1, quad, seq, seq), lambda s, g: (s, first + g, 0, 0)),
            pl.BlockSpec(table.shape, lambda s, g: (0, 0)),
        ],
        out_specs=pl.BlockSpec((3, seq, lanes), lambda s, g: (0, s, g)),
        out_shape=jax.ShapeDtypeStruct((3, rows, lanes * steps), bf16),
        compiler_params=limit(16),
        cost_estimate=cost(8 * seqs * quad * steps * seq * seq * 256, 9_000_000 * steps),
        name=name,
    )(q, k, v, attended, gatt, probs, table)


def qkv_grad_kernel(extra, me_ref, x_ref, d_ref, *rest):
    me = me_ref[0]
    if extra:
        att_ref, g1_ref, s2_ref, s1_ref = rest[:4]
    keep_ref, send_ref, acc_ref = rest[-3:]
    width = x_ref.shape[1]

    def put(value, lo):
        cols = value.shape[1]
        acc_ref[:, :cols] = value
        spread(me, acc_ref.at[:, :cols], keep_ref, send_ref, slice(lo, lo + cols))
        return lo + cols

    cols = d_ref.shape[2]

    @pl.loop(0, 3)
    def _(part):
        acc_ref[:, :cols] = dot_tn(x_ref[...], d_ref[part])
        lo = pl.multiple_of(part * cols, 128)
        spread(me, acc_ref.at[:, :cols], keep_ref, send_ref, pl.ds(lo, cols))

    lo = 3 * cols
    if extra:
        lo = put(dot_tn(att_ref[...], g1_ref[...]), lo)
        row = lax.broadcasted_iota(jnp.int32, (8, width), 0)
        rows = jnp.where(row < 2, s2_ref[...], pltpu.roll(s1_ref[...], 2, 0)).astype(bf16)
        put(dot_tn(rows, unit_rows()), lo)


def qkv_grad(me, x, parts, extra, count, name):
    rows, width = x.shape
    cols = parts.shape[2]
    chips, shard_rows = count // 2, width // count
    total = 3 * cols + (width + 128 if extra else 0)
    shape = jax.ShapeDtypeStruct((chips, shard_rows, total), bf16)
    vmem = pl.BlockSpec(memory_space=pltpu.VMEM)
    return pl.pallas_call(
        functools.partial(qkv_grad_kernel, bool(extra)),
        in_specs=[SMEM] + [vmem] * (2 + len(extra)),
        out_specs=[vmem, vmem],
        out_shape=[shape, shape],
        scratch_shapes=[pltpu.VMEM((width, width), f32)],
        compiler_params=limit(20),
        cost_estimate=cost(2 * rows * width * total, 12_000_000),
        name=name,
    )(me, x, parts, *extra)


def input_grad_kernel(g1_ref, w_ref, *rest):
    out_ref = rest[-1]
    width = out_ref.shape[1]
    total = g1_ref[...].astype(f32)
    for p in range(3):
        lo = p * width
        for ref in rest[:-1]:
            total += dot_nt(ref[p], w_ref[:, lo : lo + ref.shape[2]])
            lo += ref.shape[2]
    out_ref[...] = total.astype(bf16)


def input_grad(g1, w_qkv, parts):
    rows, width = g1.shape
    block = 512
    by_row = pl.BlockSpec((block, width), lambda i: (i, 0))
    return pl.pallas_call(
        input_grad_kernel,
        grid=(rows // block,),
        in_specs=[by_row, whole(w_qkv.shape)]
        + [pl.BlockSpec((3, block, p.shape[2]), lambda i: (0, i, 0)) for p in parts],
        out_specs=by_row,
        out_shape=jax.ShapeDtypeStruct((rows, width), bf16),
        compiler_params=limit(20),
        cost_estimate=cost(6 * rows * width * width, 14_000_000),
        name="input_grad",
    )(g1, w_qkv, *parts)


def rope_tables(seq_len):
    frequency = rope_base ** (-np.arange(0, HEAD_DIM, 2, dtype=np.float32) / HEAD_DIM)
    frequency = jnp.asarray(np.tile(frequency.astype(np.float32), 4))[None, :]
    shape = (seq_len, 128)
    angles = lax.broadcasted_iota(jnp.int32, shape, 0).astype(f32) * frequency
    lane = lax.broadcasted_iota(jnp.int32, shape, 1)
    return jnp.where(lane // 32 % 2 == 0, jnp.cos(angles), jnp.sin(angles))


def spread_tables(table):
    shifted = pltpu.roll(table, 32, 1)
    even = lax.broadcasted_iota(jnp.int32, table.shape, 1) // 32 % 2 == 0
    return jnp.where(even, table, shifted), jnp.where(even, shifted, table)


def shards(
    tokens, segment_ids, qkv_weight, out_weight, gate_weight, up_weight, down_weight,
    norm1_gain, norm1_bias, norm2_gain, norm2_bias, out_grad,
):
    count = lax.axis_size("shard")
    me = lax.axis_index("shard").astype(jnp.int32).reshape(1)
    batches, seq, width = tokens.shape
    shard_rows = qkv_weight.shape[0]
    down_rows = down_weight.shape[0]
    hidden = gate_weight.shape[1]
    rows = batches * seq
    chips = count // 2

    x = tokens.reshape(rows, width)
    cot = out_grad.reshape(rows, width)
    table = rope_tables(seq)
    vectors = jnp.stack([norm1_gain, norm1_bias, norm2_gain, norm2_bias], 1)
    vectors = jnp.pad(vectors, ((0, 0), (0, 124)))
    odd = (lax.axis_index("rep") % 2 == 1).reshape(1, 1)

    pieces_a = gather_direct(qkv_weight)
    own_b = jnp.concatenate([gate_weight, up_weight, out_weight, vectors], 1)
    seg = segment_ids.reshape(batches, 1, seq)
    table, seg, own_b, odd, ready = tie((table, seg, own_b, odd, pieces_a[0][2]))
    pieces_a = [(r, lo, tie(p, ready, seg, odd, table)) for r, lo, p in pieces_a]
    far_a = tuple(p for _, _, p in pieces_a[1:])
    pieces_a = with_partner(pieces_a)
    own_b = tie(own_b, far_a)
    if count == 8:
        first_b = gather_first(own_b)
        first_c = gather_first(tie(down_weight, far_a))
    else:
        pieces_b = gather_direct(own_b)
        pieces_c = gather_direct(down_weight)
    q, k, v, attended, probs, w_qkv = front(me, x, table, seg, pieces_a, shard_rows)
    if count == 8:
        first_b = tie(first_b, attended)
        pieces_b = gather_second(own_b, first_b)
        half = down_rows // 2
        c_x, c_y = tie(first_c, first_b)
        c_low, c_high = lax.optimization_barrier((c_y[:half], c_x[half:]))
        pieces_b = pieces_b[:3] + [(r, lo, tie(p, c_low, c_high)) for r, lo, p in pieces_b[3:]]
        pieces_c = [
            (0, 0, down_weight), (2, 0, c_x), (4, 0, c_y),
            (6, 0, xor_permute(c_low, 2)), (6, half, xor_permute(c_high, 4)),
        ]
    pieces_b = with_partner(pieces_b)
    near_c = with_partner(pieces_c[:3])
    hidden_low, back_gate, back_up, low, n1, inv1, vec, w_out = gate_forward(
        me, x, attended, pieces_b, shard_rows, hidden
    )
    if count == 8:
        pieces_c = near_c + with_partner([(r, lo, tie(p, low)) for r, lo, p in pieces_c[3:]])
    else:
        pieces_c = with_partner(pieces_c)
    output, g2low, sums2, d_keep, d_send, w_down = down_forward(
        me, hidden_low, n1, cot, vec, pieces_c, down_rows, chips
    )
    steps = hidden // 768 // 2
    flow_d = Flow(d_keep, d_send, odd, False)
    ready = sums2
    grads1 = hidden_grad(
        me, tie(g2low, ready), low, back_gate, back_up, w_down, 0, steps, count, "hidden_grad_1"
    )
    flow_e = Flow(*grads1[4:], odd, False)
    ready = advance(grads1[0], flow_d)
    grads2 = hidden_grad(
        me, tie(grads1[2], ready), low, *grads1[:2], grads1[3], steps, steps, count, "hidden_grad_2"
    )
    flow_f = Flow(*grads2[4:], odd, False)
    ready = advance(grads2[0], flow_e)
    g1low, gatt, sums1 = mixed_grad(
        me, *grads2[:2], tie(grads2[2], ready), n1, inv1, vec, w_out, pieces_b, shard_rows
    )
    ready = advance(g1low, flow_f, flow_d)
    back_a = attend_backward(
        q, k, v, attended, tie(gatt, ready), probs, table, 0, 2, "attend_bwd_1"
    )
    ready = advance(back_a, flow_e, flow_d)
    a_keep, a_send = qkv_grad(
        me, x, tie(back_a, ready), (attended, g1low, sums2, sums1), count, "qkv_out_grad_1"
    )
    flow_a = Flow(a_keep, a_send, odd, False)
    ready = advance(a_keep, flow_f, flow_e, flow_d)
    back_b = attend_backward(
        q, k, v, attended, tie(gatt, ready), probs, table, 2, 1, "attend_bwd_2"
    )
    ready = advance(back_b, flow_a, flow_f, flow_e, flow_d)
    b_keep, b_send = qkv_grad(me, x, tie(back_b, ready), (), count, "qkv_grad_2")
    flow_b = Flow(b_keep, b_send, odd, True)
    ready = advance(b_keep, flow_d)
    ready = advance(ready, flow_b)
    in_grad = input_grad(tie(g1low, ready), w_qkv, [back_a, back_b])
    ready = advance(in_grad, flow_a)
    ready = advance(ready, flow_f, flow_e)
    flow_a.pass_on = True
    flow_b.other = flow_a.step(ready)
    ready = advance(ready, flow_b, flow_f, flow_e)
    d_sum, e_sum, f_sum = [flow.finish() for flow in (flow_d, flow_e, flow_f)]
    total = flow_b.finish()
    a_sum, b_sum = total[:, : a_keep.shape[2]], total[:, a_keep.shape[2] :]

    block = 768
    hidden_sums = (e_sum, f_sum)
    pick = lambda part: jnp.concatenate(
        [
            s[:, (2 * j + part) * block : (2 * j + part + 1) * block]
            for s in hidden_sums
            for j in range(steps)
        ],
        1,
    )
    cols_a, cols_b = back_a.shape[2], back_b.shape[2]
    qkv_sum = jnp.concatenate(
        [
            s[:, p * c : (p + 1) * c]
            for p in range(3)
            for s, c in ((a_sum, cols_a), (b_sum, cols_b))
        ],
        1,
    )
    out_sum = a_sum[:, 3 * cols_a : 3 * cols_a + width]
    vec_sum = a_sum[:, 3 * cols_a + width :]
    return (
        output.reshape(tokens.shape),
        in_grad.reshape(tokens.shape),
        qkv_sum,
        out_sum,
        pick(0),
        pick(1),
        d_sum,
        vec_sum[:, 2],
        vec_sum[:, 3],
        vec_sum[:, 0],
        vec_sum[:, 1],
    )


def solution(mesh):
    rows3 = P(None, ("shard", "rep"), None)
    rows2 = P("shard", None)
    rows1 = P("shard")
    in_specs = (rows3, P(None, ("shard", "rep"))) + (rows2,) * 5 + (rows1,) * 4 + (rows3,)
    out_specs = (rows3, rows3) + (rows2,) * 5 + (rows1,) * 4
    return jax.shard_map(shards, mesh=mesh, in_specs=in_specs, out_specs=out_specs, check_vma=False)
```

```python
import functools

import jax
import jax.numpy as jnp
import numpy as np
from jax import lax
from jax.experimental import pallas as pl
from jax.experimental.pallas import tpu as pltpu
from jax.sharding import PartitionSpec as P

HEAD_DIM = 64
norm_eps = 1e-12
rope_base = 1000.0
masked_score = -1e30
f32 = jnp.float32
bf16 = jnp.bfloat16
ANY = pl.BlockSpec(memory_space=pl.ANY)
SMEM = pl.BlockSpec(memory_space=pltpu.SMEM)


def dot_nn(a, b):
    return lax.dot_general(a, b, (((1,), (0,)), ((), ())), preferred_element_type=f32)


def dot_nt(a, b):
    return lax.dot_general(a, b, (((1,), (1,)), ((), ())), preferred_element_type=f32)


def dot_tn(a, b):
    return lax.dot_general(a, b, (((0,), (0,)), ((), ())), preferred_element_type=f32)


def whole(shape):
    return pl.BlockSpec(shape, lambda *_: (0,) * len(shape))


def tie(value, *deps):
    return lax.optimization_barrier((value, deps))[0]


def xor_permute(x, bit):
    count = lax.axis_size("shard")
    return lax.ppermute(x, "shard", [(i, i ^ bit) for i in range(count)])


def with_partner(pieces):
    return pieces + [(r | 1, lo, xor_permute(p, 1)) for r, lo, p in pieces]


def gather_direct(own):
    return [(0, 0, own)] + [(r, 0, xor_permute(own, r)) for r in range(2, lax.axis_size("shard"), 2)]


def gather_first(own):
    return xor_permute(own, 2), xor_permute(own, 4)


def gather_second(own, first):
    half = own.shape[0] // 2
    from_x, from_y = first
    far = (xor_permute(from_y[:half], 2), xor_permute(from_x[half:], 4))
    return [(0, 0, own), (2, 0, from_x), (4, 0, from_y), (6, 0, far[0]), (6, half, far[1])]


def add_parts(parts):
    return functools.reduce(jnp.add, [p.astype(f32) for p in parts]).astype(bf16)


def rep_permute(x, pairs):
    return lax.ppermute(x, "rep", pairs)


def load_kernel(jobs, body, *refs):
    operands, rest = refs[: body.operands], refs[body.operands :]
    outs, (hold, sems) = rest[: body.outs], rest[body.outs :]
    half = hold.shape[1]
    copies = []
    for i, (operand, block, part) in enumerate(jobs):
        ref = operands[operand]
        src = ref.at[block, pl.ds(part * half, half), :] if block is not None else ref
        copies.append(pltpu.make_async_copy(src, hold.at[i], sems.at[i]))
        copies[-1].start()
    for copy in copies:
        copy.wait()
    body(hold, *outs)


class Fold:
    def __init__(self, operands, outs, body):
        self.operands, self.outs, self.body = operands, outs, body

    def __call__(self, hold, *outs):
        self.body(hold, *outs)


def fold_call(arrays, jobs, out_shapes, body, half, cols, name):
    count = len(out_shapes)
    return pl.pallas_call(
        functools.partial(load_kernel, jobs, Fold(len(arrays), count, body)),
        in_specs=[pl.BlockSpec(memory_space=pl.ANY)] * len(arrays),
        out_specs=[pl.BlockSpec(memory_space=pltpu.VMEM)] * count,
        out_shape=[jax.ShapeDtypeStruct(s, bf16) for s in out_shapes],
        scratch_shapes=[
            pltpu.VMEM((len(jobs), half, cols), bf16),
            pltpu.SemaphoreType.DMA((len(jobs),)),
        ],
        compiler_params=pltpu.CompilerParams(vmem_limit_bytes=8 << 20),
        cost_estimate=cost(len(jobs) * half * cols, 3 * len(jobs) * half * cols),
        name=name,
    )(*arrays)


def each_rows(rows, step, body):
    @pl.loop(0, rows // step)
    def _(i):
        body(pl.ds(pl.multiple_of(i * step, step), step))


def plus(hold, at, *slots):
    return functools.reduce(jnp.add, [hold[s, at, :].astype(f32) for s in slots]).astype(bf16)


def row_step(half):
    return 16 if half % 16 == 0 else 8


def fold_first(keep, got):
    _, rows, cols = keep.shape
    half = rows // 2
    jobs = [(a, q, p) for q, p in ((1, 0), (3, 0), (2, 1), (3, 1)) for a in (0, 1)]

    def body(hold, x_ref, y_ref):
        def some(at):
            for n, ref in enumerate((x_ref, x_ref, y_ref, y_ref)):
                ref[n % 2, at, :] = plus(hold, at, 2 * n, 2 * n + 1)

        each_rows(half, row_step(half), some)

    return fold_call([keep, got], jobs, [(2, half, cols)] * 2, body, half, cols, "fold_first")


def fold_second(keep, got, from_x, from_y):
    _, rows, cols = keep.shape
    half = rows // 2
    jobs = [(0, 2, 0), (1, 2, 0), (2, 1, 0), (0, 1, 1), (1, 1, 1), (3, 1, 0)]

    def body(hold, y_ref, x_ref):
        def some(at):
            y_ref[at, :] = plus(hold, at, 0, 1, 2)
            x_ref[at, :] = plus(hold, at, 3, 4, 5)

        each_rows(half, row_step(half), some)

    return fold_call(
        [keep, got, from_x, from_y], jobs, [(half, cols)] * 2, body, half, cols, "fold_second"
    )


def fold_own(keep, got, from_x, from_y, last_y, last_x):
    _, rows, cols = keep.shape
    half = rows // 2
    jobs = [
        (0, 0, 0), (1, 0, 0), (2, 0, 0), (4, None, 0), (0, 0, 1), (1, 0, 1), (3, 0, 0), (5, None, 0)
    ]

    def body(hold, own_ref):
        def some(at):
            own_ref[0, at, :] = plus(hold, at, 0, 1, 2, 3)
            own_ref[1, at, :] = plus(hold, at, 4, 5, 6, 7)

        each_rows(half, row_step(half), some)

    own = fold_call(
        [keep, got, from_x, from_y, last_y, last_x], jobs, [(2, half, cols)], body, half, cols, "fold_own"
    )[0]
    return own.reshape(rows, cols)


def fold_call_whole(arrays, jobs, pairs, name):
    _, rows, cols = arrays[0].shape

    def body(hold, out_ref):
        def some(at):
            for n, slots in enumerate(pairs):
                out_ref[n, at, :] = plus(hold, at, *slots)

        each_rows(rows, row_step(rows), some)

    return fold_call(arrays, jobs, [(len(pairs), rows, cols)], body, rows, cols, name)[0]


def fold_line_first(keep, got, near):
    jobs = [(a, q, 0) for q in (near, 3) for a in (0, 1)]
    return fold_call_whole([keep, got], jobs, [(0, 1), (2, 3)], "fold_line_first")


def fold_line_second(keep, got, came, far):
    jobs = [(0, far, 0), (1, far, 0), (2, 1, 0)]
    return fold_call_whole([keep, got, came], jobs, [(0, 1, 2)], "fold_line_second")


def fold_line_own(keep, got, came, last):
    jobs = [(0, 0, 0), (1, 0, 0), (2, 0, 0), (3, 0, 0)]
    return fold_call_whole([keep, got, came, last], jobs, [(0, 1, 2, 3)], "fold_line_own")[0]


class Flow:
    def __init__(self, keep, send, odd, direct=False):
        self.held = keep
        self.odd = odd
        self.other = None
        self.pass_on = False
        self.pending = xor_permute(send, 1)
        self.stage = 0
        self.way = direct if keep.shape[0] == 4 and direct in (1, 2) and direct is not True else 0
        self.pair = keep.shape[0] == 4 and not direct
        self.line = lax.axis_size("rep") == 4

    def step(self, *deps):
        got = tie(self.pending, *deps) if deps else self.pending
        stage = self.stage
        if stage == 0:
            self.got = got
            if self.way:
                self.ready = fold_line_first(self.held, got, self.way)
                self.pending = xor_permute(self.ready, 2 * self.way)
            elif self.pair:
                self.ready = fold_first(self.held, got)
                self.pending = (xor_permute(self.ready[0], 2), xor_permute(self.ready[1], 4))
            else:
                self.ready = [self.held[q] + got[q] for q in range(got.shape[0])]
                self.pending = [xor_permute(self.ready[q], 2 * q) for q in range(1, got.shape[0])]
        elif stage == 1 and self.way:
            self.first = got
            self.ready = fold_line_second(self.held, self.got, got, 3 - self.way)
            self.pending = xor_permute(self.ready, 2 * (3 - self.way))
        elif stage == 1 and self.pair:
            self.first = got
            if self.pair:
                self.ready = fold_second(self.held, self.got, *got)
                self.pending = (xor_permute(self.ready[0], 4), xor_permute(self.ready[1], 2))
        elif stage <= 2:
            self.stage = 2
            if self.way:
                self.ready = fold_line_own(self.held, self.got, self.first, got)
            elif self.pair:
                self.ready = fold_own(self.held, self.got, *self.first, *got)
            else:
                self.ready = add_parts([self.ready[0]] + list(got))
            if self.other is not None:
                self.ready = jnp.concatenate([self.other, self.ready], 1)
            if self.pass_on:
                self.stage = 6
                return self.ready
            if self.line:
                half = self.ready.shape[0] // 2
                self.mine = jnp.where(self.odd, self.ready[half:], self.ready[:half])
                self.ready = jnp.where(self.odd, self.ready[:half], self.ready[half:])
                self.pending = rep_permute(self.ready, [(0, 1), (1, 0), (2, 3), (3, 2)])
            else:
                self.pending = lax.psum(self.ready, "rep")
        elif not self.line:
            self.ready = got
        elif stage == 3:
            self.ready = add_parts([self.mine, got])
            self.pending = rep_permute(self.ready, [(0, 2), (2, 0), (1, 3), (3, 1)])
        elif stage == 4:
            self.ready = add_parts([self.ready, got])
            self.pending = rep_permute(self.ready, [(0, 1), (1, 0), (2, 3), (3, 2)])
        else:
            low, high = (jnp.where(self.odd, a, b) for a, b in ((got, self.ready), (self.ready, got)))
            self.ready = jnp.concatenate([low, high]).astype(f32)
        self.stage += 1
        return self.ready

    def finish(self):
        while self.stage < 6:
            self.step()
        return self.ready.astype(f32)


def advance(dep, *flows):
    return tuple(flow.step(dep) for flow in flows)


def piece_copies(metas, refs, me, shard_rows, dst, src_lo, dst_lo, cols, sems):
    copies = []
    for i, ((rel, first, rows), ref) in enumerate(zip(metas, refs)):
        at = pl.multiple_of((me ^ rel) * shard_rows + first, 8)
        copies.append(
            pltpu.make_async_copy(
                ref.at[:, pl.ds(src_lo, cols)],
                dst.at[pl.ds(at, rows), pl.ds(dst_lo, cols)],
                sems.at[i],
            )
        )
    return copies


def start_all(copies):
    for copy in copies:
        copy.start()


def wait_all(copies):
    for copy in copies:
        copy.wait()


def metas_of(pieces):
    return tuple((rel, first, p.shape[0]) for rel, first, p in pieces)


def in_hbm(x):
    return pltpu.with_memory_space_constraint(x, pltpu.HBM)


def arrays_of(pieces):
    return [in_hbm(p) for _, _, p in pieces]


def half_mask(shape):
    lane = lax.broadcasted_iota(jnp.int32, shape, len(shape) - 1)
    return (lane % HEAD_DIM) < HEAD_DIM // 2


def unit_rows():
    shape = (8, 128)
    return (
        lax.broadcasted_iota(jnp.int32, shape, 0) == lax.broadcasted_iota(jnp.int32, shape, 1)
    ).astype(bf16)


def normalize(h):
    centre = h - jnp.mean(h, -1, keepdims=True)
    inv = lax.rsqrt(jnp.mean(centre * centre, -1, keepdims=True) + norm_eps)
    return centre * inv, inv


def norm_back(e, n, inv):
    return inv * (e - jnp.mean(e, -1, keepdims=True) - n * jnp.mean(e * n, -1, keepdims=True))


def spread(me, acc_ref, keep_ref, send_ref, cols):
    rows = keep_ref.shape[1]
    chip, core = me // 2, me & 1
    for q in range(keep_ref.shape[0]):
        base = (chip ^ q) * 2
        keep_ref[q, :, cols] = acc_ref[
            pl.ds(pl.multiple_of((base + core) * rows, 8), rows), :
        ].astype(bf16)
        send_ref[q, :, cols] = acc_ref[
            pl.ds(pl.multiple_of((base + 1 - core) * rows, 8), rows), :
        ].astype(bf16)


def cost(flops, read, transcendentals=0):
    return pl.CostEstimate(flops=1000, bytes_accessed=1000, transcendentals=0)


def front_kernel(metas, shard_rows, me_ref, x_ref, table_ref, row_ref, *rest):
    refs, rest = rest[: len(metas)], rest[len(metas) :]
    q_ref, k_ref, v_ref, att_ref, p_ref, w_out, w_ref, bias_ref, sems, back_sem = rest
    s, g = pl.program_id(0), pl.program_id(1)
    width = x_ref.shape[1]
    lanes = p_ref.shape[1] * HEAD_DIM
    copies = piece_copies(metas, refs, me_ref[0], shard_rows, w_ref, 0, 0, 3 * width, sems)
    back = pltpu.make_async_copy(w_ref, w_out, back_sem)

    @pl.when((s == 0) & (g == 0))
    def _():
        start_all(copies)
        wait_all(copies)
        back.start()

    @pl.when(g == 0)
    def _():
        across = jnp.broadcast_to(row_ref[0].astype(f32), bias_ref.shape)
        down = lax.broadcasted_iota(jnp.int32, bias_ref.shape, 0)
        own = lax.broadcasted_iota(jnp.int32, bias_ref.shape, 1) == down
        column = jnp.sum(jnp.where(own, across, 0.0), -1, keepdims=True)
        bias_ref[...] = jnp.where(across == column, 0.0, masked_score).astype(f32)
        x = x_ref[...]
        first = half_mask((x.shape[0], 128))
        cos, sin = spread_tables(table_ref[...])
        sin = jnp.where(first, -sin, sin)
        for part, ref in enumerate((q_ref, k_ref, v_ref)):
            y = dot_nn(x, w_ref[:, part * width : (part + 1) * width])
            for b in range(width // 128):
                cols = slice(b * 128, (b + 1) * 128)
                u = y[:, cols]
                if part < 2:
                    turned = jnp.where(first, pltpu.roll(u, 96, 1), pltpu.roll(u, 32, 1))
                    u = u * cos + turned * sin
                if part == 0:
                    u = u * 0.125
                ref[:, cols] = u.astype(bf16)

    lane = lax.broadcasted_iota(jnp.int32, (1, 128), 1)
    for pair in range(lanes // 128):
        at = pl.ds(pl.multiple_of(g * lanes + pair * 128, 128), 128)
        q, k, v = q_ref[:, at], k_ref[:, at], v_ref[:, at]
        acc = None
        for side in range(2):
            mine = ((lane // HEAD_DIM) == side).astype(bf16)
            score = dot_nt(q, k * mine) + bias_ref[...]
            e = jnp.exp(score - jnp.max(score, -1, keepdims=True))
            inv = 1.0 / jnp.sum(e, -1, keepdims=True)
            p = (e * inv).astype(bf16)
            p_ref[0, pair * 2 + side] = p
            part = dot_nn(p, v * mine)
            acc = part if acc is None else acc + part
        att_ref[:, pair * 128 : (pair + 1) * 128] = acc.astype(bf16)

    @pl.when((s == pl.num_programs(0) - 1) & (g == pl.num_programs(1) - 1))
    def _():
        back.wait()


def front(me, x, table, seg_row, pieces, shard_rows):
    rows, width = x.shape
    metas = metas_of(pieces)
    seqs, _, seq = seg_row.shape
    heads = width // HEAD_DIM
    quad = 4
    lanes = quad * HEAD_DIM
    by_seq = pl.BlockSpec((seq, width), lambda s, g: (s, 0))
    wide = jax.ShapeDtypeStruct((rows, width), bf16)
    return pl.pallas_call(
        functools.partial(front_kernel, metas, shard_rows),
        grid=(seqs, width // lanes),
        in_specs=[
            SMEM, by_seq, whole(table.shape),
            pl.BlockSpec((1, 1, seq), lambda s, g: (s, 0, 0)),
        ]
        + [ANY] * len(metas),
        out_specs=[by_seq] * 3
        + [
            pl.BlockSpec((seq, lanes), lambda s, g: (s, g)),
            pl.BlockSpec((1, quad, seq, seq), lambda s, g: (s, g, 0, 0)),
            ANY,
        ],
        out_shape=[wide] * 4
        + [
            jax.ShapeDtypeStruct((seqs, heads, seq, seq), bf16),
            jax.ShapeDtypeStruct((width, 3 * width), bf16),
        ],
        scratch_shapes=[
            pltpu.VMEM((width, 3 * width), bf16),
            pltpu.VMEM((seq, seq), f32),
            pltpu.SemaphoreType.DMA((len(metas),)),
            pltpu.SemaphoreType.DMA,
        ],
        cost_estimate=cost(
            6 * rows * width * width + 4 * seqs * heads * seq * seq * 256,
            30_000_000,
            seqs * heads * seq * seq,
        ),
        name="qkv_attend",
    )(me, x, table, seg_row, *[p for _, _, p in pieces])


VM = pl.BlockSpec(memory_space=pltpu.VMEM)
HBM = pl.BlockSpec(memory_space=pltpu.HBM)


def in_vmem(shape, dtype=bf16):
    return pltpu.VMEM(shape, dtype)


def limit(mib):
    return pltpu.CompilerParams(vmem_limit_bytes=mib << 20)


def gate_kernel(metas, shard_rows, me_ref, tok_ref, att_ref, *rest):
    refs, rest = rest[: len(metas)], rest[len(metas) :]
    h_ref, a_ref, b_ref, x_ref, n1_ref, inv_ref, vec_ref, wo_ref = rest[:8]
    wg_ref, wv_ref, sems, sems_o = rest[8:]
    hidden = a_ref.shape[1]
    width = wo_ref.shape[1]
    block = 768
    steps = hidden // block
    me = me_ref[0]

    def spans(j):
        return pl.multiple_of(j * block, block), pl.multiple_of(hidden + j * block, block)

    def copies(j):
        both = []
        for part, lo in enumerate(spans(j)):
            both += piece_copies(metas, refs, me, shard_rows, wg_ref, lo, lo, block, sems.at[j, part])
        return both

    copies_o = piece_copies(
        metas, refs, me, shard_rows, wo_ref, 2 * hidden, 0, width, sems_o.at[0]
    ) + piece_copies(metas, refs, me, shard_rows, wv_ref, 2 * hidden + width, 0, 128, sems_o.at[1])
    start_all(copies_o)

    @pl.loop(0, steps)
    def _(j):
        start_all(copies(j))

    wait_all(copies_o)
    vec_ref[...] = dot_nt(unit_rows(), wv_ref[...])

    @pl.loop(0, 2)
    def _(i):
        rows = tok_ref.shape[0] // 2
        at = pl.ds(pl.multiple_of(i * rows, 8), rows)
        n, inv = normalize(tok_ref[at, :].astype(f32) + dot_nn(att_ref[at, :], wo_ref[...]))
        n1_ref[at, :] = n.astype(bf16)
        inv_ref[at, :] = jnp.broadcast_to(inv, (rows, inv_ref.shape[1]))
        x_ref[at, :] = (n * vec_ref[0:1] + vec_ref[1:2]).astype(bf16)

    @pl.loop(0, steps)
    def _(j):
        wait_all(copies(j))
        gate_at, up_at = (pl.ds(lo, block) for lo in spans(j))
        half = x_ref.shape[0] // 2
        for r in range(2):
            rows = slice(r * half, (r + 1) * half)
            gate = dot_nn(x_ref[rows, :], wg_ref[:, gate_at])
            up = dot_nn(x_ref[rows, :], wg_ref[:, up_at])
            s = 0.5 * jnp.tanh(0.5 * gate) + 0.5
            act = gate * s
            h_ref[rows, gate_at] = (act * up).astype(bf16)
            b_ref[rows, gate_at] = act.astype(bf16)
            a_ref[rows, gate_at] = (up * (s + act * (1.0 - s))).astype(bf16)


def gate_forward(me, tokens, attended, pieces, shard_rows, hidden):
    rows, width = tokens.shape
    metas = metas_of(pieces)
    return pl.pallas_call(
        functools.partial(gate_kernel, metas, shard_rows),
        in_specs=[SMEM, VM, VM] + [ANY] * len(metas),
        out_specs=[VM] * 8,
        out_shape=[in_vmem((rows, hidden))] * 3
        + [
            in_vmem((rows, width)),
            in_vmem((rows, width)),
            in_vmem((rows, 128), f32),
            in_vmem((8, width), f32),
            in_vmem((width, width)),
        ],
        scratch_shapes=[
            pltpu.VMEM((width, 2 * hidden), bf16),
            pltpu.VMEM((width, 128), bf16),
            pltpu.SemaphoreType.DMA((hidden // 768, 2, len(metas))),
            pltpu.SemaphoreType.DMA((2, len(metas))),
        ],
        compiler_params=limit(19),
        cost_estimate=cost(4 * rows * width * hidden, 10_000_000, rows * hidden),
        name="out_gate_up",
    )(me, tokens, attended, *arrays_of(pieces))


def down_kernel(metas, shard_rows, me_ref, h_ref, n1_ref, cot_ref, vec_ref, *rest):
    refs = rest[: len(metas)]
    out_ref, low_ref, sums_ref, keep_ref, send_ref, w_ref, acc_ref, sems = rest[len(metas) :]
    me = me_ref[0]
    copies = piece_copies(metas, refs, me, shard_rows, w_ref, 0, 0, w_ref.shape[1], sems)
    start_all(copies)
    sums_ref[...] = jnp.zeros_like(sums_ref)
    wait_all(copies)
    block = 256

    @pl.loop(0, h_ref.shape[0] // block)
    def _(i):
        at = pl.ds(pl.multiple_of(i * block, block), block)
        mixed = n1_ref[at, :].astype(f32) * vec_ref[0:1] + vec_ref[1:2]
        n, inv = normalize(mixed + dot_nn(h_ref[at, :], w_ref[...]))
        out_ref[at, :] = (n * vec_ref[2:3] + vec_ref[3:4]).astype(bf16)
        cot = cot_ref[at, :].astype(f32)
        sums_ref[0:1] += jnp.sum(cot * n, 0, keepdims=True)
        sums_ref[1:2] += jnp.sum(cot, 0, keepdims=True)
        low_ref[at, :] = norm_back(cot * vec_ref[2:3], n, inv).astype(bf16)

    per_chip = acc_ref.shape[0]
    half = per_chip // 2
    core = me & 1

    @pl.loop(0, keep_ref.shape[0])
    def _(q):
        lo = pl.multiple_of(((me // 2) ^ q) * per_chip, 128)
        acc_ref[...] = dot_tn(h_ref[:, pl.ds(lo, per_chip)], low_ref[...])
        keep_ref[q] = acc_ref[pl.ds(pl.multiple_of(core * half, 8), half), :].astype(bf16)
        send_ref[q] = acc_ref[pl.ds(pl.multiple_of((1 - core) * half, 8), half), :].astype(bf16)


def down_forward(me, hidden_low, n1, cot, vec, pieces, shard_rows, chips):
    rows, hidden = hidden_low.shape
    width = n1.shape[1]
    metas = metas_of(pieces)
    per_chip = hidden // chips
    return pl.pallas_call(
        functools.partial(down_kernel, metas, shard_rows),
        in_specs=[SMEM, VM, VM, VM, VM] + [ANY] * len(metas),
        out_specs=[VM] * 6,
        out_shape=[
            jax.ShapeDtypeStruct((rows, width), bf16),
            in_vmem((rows, width)),
            in_vmem((8, width), f32),
            jax.ShapeDtypeStruct((chips, per_chip // 2, width), bf16),
            jax.ShapeDtypeStruct((chips, per_chip // 2, width), bf16),
            in_vmem((hidden, width)),
        ],
        scratch_shapes=[
            pltpu.VMEM((per_chip, width), f32),
            pltpu.SemaphoreType.DMA((len(metas),)),
        ],
        compiler_params=limit(19),
        cost_estimate=cost(4 * rows * width * hidden, 10_000_000, rows),
        name="down_norm_grad",
    )(me, hidden_low, n1, cot, vec, *arrays_of(pieces))


def hidden_grad_kernel(
    first, steps, me_ref, g_ref, x_ref, a_ref, b_ref, w_ref, gg_ref, gu_ref, _g, _w, keep_ref, send_ref, acc_ref
):
    block = 768

    @pl.loop(0, steps)
    def _(j):
        cols = pl.ds(pl.multiple_of((first + j) * block, block), block)
        half = g_ref.shape[0] // 2
        for r in range(2):
            rows = slice(r * half, (r + 1) * half)
            gh = dot_nt(g_ref[rows, :], w_ref[cols, :])
            gg_ref[rows, cols] = (gh * a_ref[rows, cols].astype(f32)).astype(bf16)
            gu_ref[rows, cols] = (gh * b_ref[rows, cols].astype(f32)).astype(bf16)
        for part, ref in enumerate((gg_ref, gu_ref)):
            acc_ref[...] = dot_tn(x_ref[...], ref[:, cols])
            lo = pl.multiple_of((2 * j + part) * block, block)
            spread(me_ref[0], acc_ref, keep_ref, send_ref, pl.ds(lo, block))


def hidden_grad(me, g2low, low, a, b, w_down, first, steps, count, name):
    rows, width = g2low.shape
    block = 768
    chips, shard_rows = count // 2, width // count
    part = jax.ShapeDtypeStruct((chips, shard_rows, 2 * block * steps), bf16)
    return pl.pallas_call(
        functools.partial(hidden_grad_kernel, first, steps),
        in_specs=[SMEM, VM, VM, VM, VM, VM],
        out_specs=[VM] * 6,
        out_shape=[
            in_vmem(a.shape), in_vmem(b.shape), in_vmem(g2low.shape), in_vmem(w_down.shape), part, part
        ],
        input_output_aliases={3: 0, 4: 1, 1: 2, 5: 3},
        scratch_shapes=[pltpu.VMEM((width, block), f32)],
        compiler_params=limit(19),
        cost_estimate=cost(6 * rows * width * block * steps, 5_000_000),
        name=name,
    )(me, g2low, low, a, b, w_down)


def mixed_grad_kernel(
    metas, shard_rows, me_ref, gg_ref, gu_ref, g2_ref, n1_ref, inv_ref, vec_ref, wo_ref, *rest
):
    refs, rest = rest[: len(metas)], rest[len(metas) :]
    low_ref, gatt_ref, sums_ref, _gg, _gu, _g2, w_ref, sems = rest
    hidden = gg_ref.shape[1]
    block = 256
    copies = [
        piece_copies(
            metas, refs, me_ref[0], shard_rows, w_ref, c * hidden, c * hidden, hidden, sems.at[c]
        )
        for c in range(2)
    ]
    start_all(copies[0])
    start_all(copies[1])
    sums_ref[...] = jnp.zeros_like(sums_ref)

    def rows(at, waits):
        if waits:
            wait_all(copies[0])
        gm = g2_ref[at, :].astype(f32) + dot_nt(gg_ref[at, :], w_ref[:, :hidden])
        if waits:
            wait_all(copies[1])
        gm += dot_nt(gu_ref[at, :], w_ref[:, hidden:])
        n = n1_ref[at, :].astype(f32)
        sums_ref[0:1] += jnp.sum(gm * n, 0, keepdims=True)
        sums_ref[1:2] += jnp.sum(gm, 0, keepdims=True)
        low = norm_back(gm * vec_ref[0:1], n, inv_ref[at, 0:1]).astype(bf16)
        low_ref[at, :] = low
        gatt_ref[at, :] = dot_nt(low, wo_ref[...]).astype(bf16)

    rows(slice(0, block), True)

    @pl.loop(1, gg_ref.shape[0] // block)
    def _(i):
        rows(pl.ds(pl.multiple_of(i * block, block), block), False)


def mixed_grad(me, gg, gu, g2, n1, inv1, vec, w_out, pieces, shard_rows):
    rows, width = g2.shape
    hidden = gg.shape[1]
    metas = metas_of(pieces)
    return pl.pallas_call(
        functools.partial(mixed_grad_kernel, metas, shard_rows),
        in_specs=[SMEM] + [VM] * 7 + [ANY] * len(metas),
        out_specs=[VM] * 6,
        out_shape=[
            jax.ShapeDtypeStruct((rows, width), bf16),
            jax.ShapeDtypeStruct((rows, width), bf16),
            jax.ShapeDtypeStruct((8, width), f32),
            in_vmem(gg.shape),
            in_vmem(gu.shape),
            in_vmem(g2.shape),
        ],
        input_output_aliases={1: 3, 2: 4, 3: 5},
        scratch_shapes=[
            pltpu.VMEM((width, 2 * hidden), bf16),
            pltpu.SemaphoreType.DMA((2, len(metas))),
        ],
        compiler_params=limit(19),
        cost_estimate=cost(4 * rows * width * hidden + 2 * rows * width * width, 15_000_000),
        name="mixed_grad",
    )(me, gg, gu, g2, n1, inv1, vec, w_out, *arrays_of(pieces))[:3]


def attend_back_kernel(
    q_ref, k_ref, v_ref, o_ref, g_ref, p_ref, table_ref, d_ref
):
    heads = p_ref.shape[1]
    lane = lax.broadcasted_iota(jnp.int32, (1, 128), 1)
    first = half_mask(table_ref.shape)
    cos, sin = spread_tables(table_ref[...])

    def unrotate(g):
        t = g * sin
        return g * cos + jnp.where(first, pltpu.roll(t, 96, 1), -pltpu.roll(t, 32, 1))

    for pair in range(heads // 2):
        cols = slice(pair * 128, (pair + 1) * 128)
        q, k, v, g = q_ref[:, cols], k_ref[:, cols], v_ref[:, cols], g_ref[:, cols]
        go = g.astype(f32) * o_ref[:, cols].astype(f32)
        dq = dk = dv = None
        for side in range(2):
            mine = (lane // HEAD_DIM) == side
            keep = mine.astype(bf16)
            p = p_ref[0, pair * 2 + side]
            row = jnp.sum(jnp.where(mine, go, 0.0), -1, keepdims=True)
            gp = dot_nt(g, v * keep)
            gs = (p.astype(f32) * (gp - row)).astype(bf16)
            parts = (dot_nn(gs, k * keep), dot_tn(gs, q * keep), dot_tn(p, g * keep))
            if dq is None:
                dq, dk, dv = parts
            else:
                dq, dk, dv = dq + parts[0], dk + parts[1], dv + parts[2]
        d_ref[0, :, cols] = unrotate(dq * 0.125).astype(bf16)
        d_ref[1, :, cols] = unrotate(dk).astype(bf16)
        d_ref[2, :, cols] = dv.astype(bf16)


def attend_backward(q, k, v, attended, gatt, probs, table, first, steps, name):
    rows, _ = attended.shape
    seqs, _, seq, _ = probs.shape
    quad = 4
    lanes = quad * HEAD_DIM
    spec_in = pl.BlockSpec((seq, lanes), lambda s, g: (s, first + g))
    return pl.pallas_call(
        attend_back_kernel,
        grid=(seqs, steps),
        in_specs=[spec_in] * 5
        + [
            pl.BlockSpec((1, quad, seq, seq), lambda s, g: (s, first + g, 0, 0)),
            pl.BlockSpec(table.shape, lambda s, g: (0, 0)),
        ],
        out_specs=pl.BlockSpec((3, seq, lanes), lambda s, g: (0, s, g)),
        out_shape=jax.ShapeDtypeStruct((3, rows, lanes * steps), bf16),
        compiler_params=limit(16),
        cost_estimate=cost(8 * seqs * quad * steps * seq * seq * 256, 9_000_000 * steps),
        name=name,
    )(q, k, v, attended, gatt, probs, table)


def qkv_grad_kernel(extra, me_ref, x_ref, d_ref, *rest):
    me = me_ref[0]
    if extra:
        att_ref, g1_ref, s2_ref, s1_ref = rest[:4]
    keep_ref, send_ref, acc_ref = rest[-3:]
    width = x_ref.shape[1]

    def put(value, lo):
        cols = value.shape[1]
        acc_ref[:, :cols] = value
        spread(me, acc_ref.at[:, :cols], keep_ref, send_ref, slice(lo, lo + cols))
        return lo + cols

    cols = d_ref.shape[2]

    @pl.loop(0, 3)
    def _(part):
        acc_ref[:, :cols] = dot_tn(x_ref[...], d_ref[part])
        lo = pl.multiple_of(part * cols, 128)
        spread(me, acc_ref.at[:, :cols], keep_ref, send_ref, pl.ds(lo, cols))

    lo = 3 * cols
    if extra:
        lo = put(dot_tn(att_ref[...], g1_ref[...]), lo)
        row = lax.broadcasted_iota(jnp.int32, (8, width), 0)
        rows = jnp.where(row < 2, s2_ref[...], pltpu.roll(s1_ref[...], 2, 0)).astype(bf16)
        put(dot_tn(rows, unit_rows()), lo)


def qkv_grad(me, x, parts, extra, count, name):
    rows, width = x.shape
    cols = parts.shape[2]
    chips, shard_rows = count // 2, width // count
    total = 3 * cols + (width + 128 if extra else 0)
    shape = jax.ShapeDtypeStruct((chips, shard_rows, total), bf16)
    vmem = pl.BlockSpec(memory_space=pltpu.VMEM)
    return pl.pallas_call(
        functools.partial(qkv_grad_kernel, bool(extra)),
        in_specs=[SMEM] + [vmem] * (2 + len(extra)),
        out_specs=[vmem, vmem],
        out_shape=[shape, shape],
        scratch_shapes=[pltpu.VMEM((width, width), f32)],
        compiler_params=limit(20),
        cost_estimate=cost(2 * rows * width * total, 12_000_000),
        name=name,
    )(me, x, parts, *extra)


def input_grad_kernel(g1_ref, w_ref, *rest):
    out_ref = rest[-1]
    width = out_ref.shape[1]
    total = g1_ref[...].astype(f32)
    for p in range(3):
        lo = p * width
        for ref in rest[:-1]:
            total += dot_nt(ref[p], w_ref[:, lo : lo + ref.shape[2]])
            lo += ref.shape[2]
    out_ref[...] = total.astype(bf16)


def input_grad(g1, w_qkv, parts):
    rows, width = g1.shape
    block = 512
    by_row = pl.BlockSpec((block, width), lambda i: (i, 0))
    return pl.pallas_call(
        input_grad_kernel,
        grid=(rows // block,),
        in_specs=[by_row, whole(w_qkv.shape)]
        + [pl.BlockSpec((3, block, p.shape[2]), lambda i: (0, i, 0)) for p in parts],
        out_specs=by_row,
        out_shape=jax.ShapeDtypeStruct((rows, width), bf16),
        compiler_params=limit(20),
        cost_estimate=cost(6 * rows * width * width, 14_000_000),
        name="input_grad",
    )(g1, w_qkv, *parts)


def rope_tables(seq_len):
    frequency = rope_base ** (-np.arange(0, HEAD_DIM, 2, dtype=np.float32) / HEAD_DIM)
    frequency = jnp.asarray(np.tile(frequency.astype(np.float32), 4))[None, :]
    shape = (seq_len, 128)
    angles = lax.broadcasted_iota(jnp.int32, shape, 0).astype(f32) * frequency
    lane = lax.broadcasted_iota(jnp.int32, shape, 1)
    return jnp.where(lane // 32 % 2 == 0, jnp.cos(angles), jnp.sin(angles))


def spread_tables(table):
    shifted = pltpu.roll(table, 32, 1)
    even = lax.broadcasted_iota(jnp.int32, table.shape, 1) // 32 % 2 == 0
    return jnp.where(even, table, shifted), jnp.where(even, shifted, table)


def shards(
    tokens, segment_ids, qkv_weight, out_weight, gate_weight, up_weight, down_weight,
    norm1_gain, norm1_bias, norm2_gain, norm2_bias, out_grad,
):
    count = lax.axis_size("shard")
    me = lax.axis_index("shard").astype(jnp.int32).reshape(1)
    batches, seq, width = tokens.shape
    shard_rows = qkv_weight.shape[0]
    down_rows = down_weight.shape[0]
    hidden = gate_weight.shape[1]
    rows = batches * seq
    chips = count // 2

    x = tokens.reshape(rows, width)
    cot = out_grad.reshape(rows, width)
    table = rope_tables(seq)
    vectors = jnp.stack([norm1_gain, norm1_bias, norm2_gain, norm2_bias], 1)
    vectors = jnp.pad(vectors, ((0, 0), (0, 124)))
    odd = (lax.axis_index("rep") % 2 == 1).reshape(1, 1)

    pieces_a = gather_direct(qkv_weight)
    own_b = jnp.concatenate([gate_weight, up_weight, out_weight, vectors], 1)
    seg = segment_ids.reshape(batches, 1, seq)
    table, seg, own_b, odd, ready = tie((table, seg, own_b, odd, pieces_a[0][2]))
    pieces_a = [(r, lo, tie(p, ready, seg, odd, table)) for r, lo, p in pieces_a]
    far_a = tuple(p for _, _, p in pieces_a[1:])
    pieces_a = with_partner(pieces_a)
    own_b = tie(own_b, far_a)
    if count == 8:
        first_b = gather_first(own_b)
        first_c = gather_first(tie(down_weight, far_a))
    else:
        pieces_b = gather_direct(own_b)
        pieces_c = gather_direct(down_weight)
    q, k, v, attended, probs, w_qkv = front(me, x, table, seg, pieces_a, shard_rows)
    if count == 8:
        first_b = tie(first_b, attended)
        pieces_b = gather_second(own_b, first_b)
        half = down_rows // 2
        c_x, c_y = tie(first_c, first_b)
        c_low, c_high = lax.optimization_barrier((c_y[:half], c_x[half:]))
        pieces_b = pieces_b[:3] + [(r, lo, tie(p, c_low, c_high)) for r, lo, p in pieces_b[3:]]
        pieces_c = [
            (0, 0, down_weight), (2, 0, c_x), (4, 0, c_y),
            (6, 0, xor_permute(c_low, 2)), (6, half, xor_permute(c_high, 4)),
        ]
    pieces_b = with_partner(pieces_b)
    near_c = with_partner(pieces_c[:3])
    hidden_low, back_gate, back_up, low, n1, inv1, vec, w_out = gate_forward(
        me, x, attended, pieces_b, shard_rows, hidden
    )
    if count == 8:
        pieces_c = near_c + with_partner([(r, lo, tie(p, low)) for r, lo, p in pieces_c[3:]])
    else:
        pieces_c = with_partner(pieces_c)
    output, g2low, sums2, d_keep, d_send, w_down = down_forward(
        me, hidden_low, n1, cot, vec, pieces_c, down_rows, chips
    )
    steps = hidden // 768 // 2
    flow_d = Flow(d_keep, d_send, odd, False)
    ready = sums2
    grads1 = hidden_grad(
        me, tie(g2low, ready), low, back_gate, back_up, w_down, 0, steps, count, "hidden_grad_1"
    )
    flow_e = Flow(*grads1[4:], odd, False)
    ready = advance(grads1[0], flow_d)
    grads2 = hidden_grad(
        me, tie(grads1[2], ready), low, *grads1[:2], grads1[3], steps, steps, count, "hidden_grad_2"
    )
    flow_f = Flow(*grads2[4:], odd, False)
    ready = advance(grads2[0], flow_e)
    g1low, gatt, sums1 = mixed_grad(
        me, *grads2[:2], tie(grads2[2], ready), n1, inv1, vec, w_out, pieces_b, shard_rows
    )
    ready = advance(g1low, flow_f, flow_d)
    back_a = attend_backward(
        q, k, v, attended, tie(gatt, ready), probs, table, 0, 2, "attend_bwd_1"
    )
    ready = advance(back_a, flow_e, flow_d)
    a_keep, a_send = qkv_grad(
        me, x, tie(back_a, ready), (attended, g1low, sums2, sums1), count, "qkv_out_grad_1"
    )
    flow_a = Flow(a_keep, a_send, odd, False)
    ready = advance(a_keep, flow_f, flow_e, flow_d)
    back_b = attend_backward(
        q, k, v, attended, tie(gatt, ready), probs, table, 2, 1, "attend_bwd_2"
    )
    ready = advance(back_b, flow_a, flow_f, flow_e, flow_d)
    b_keep, b_send = qkv_grad(me, x, tie(back_b, ready), (), count, "qkv_grad_2")
    flow_b = Flow(b_keep, b_send, odd, True)
    ready = advance(b_keep, flow_d)
    ready = advance(ready, flow_b)
    in_grad = input_grad(tie(g1low, ready), w_qkv, [back_a, back_b])
    ready = advance(in_grad, flow_a)
    ready = advance(ready, flow_f, flow_e)
    flow_a.pass_on = True
    flow_b.other = flow_a.step(ready)
    ready = advance(ready, flow_b, flow_f, flow_e)
    d_sum, e_sum, f_sum = [flow.finish() for flow in (flow_d, flow_e, flow_f)]
    total = flow_b.finish()
    a_sum, b_sum = total[:, : a_keep.shape[2]], total[:, a_keep.shape[2] :]

    block = 768
    hidden_sums = (e_sum, f_sum)
    pick = lambda part: jnp.concatenate(
        [
            s[:, (2 * j + part) * block : (2 * j + part + 1) * block]
            for s in hidden_sums
            for j in range(steps)
        ],
        1,
    )
    cols_a, cols_b = back_a.shape[2], back_b.shape[2]
    qkv_sum = jnp.concatenate(
        [
            s[:, p * c : (p + 1) * c]
            for p in range(3)
            for s, c in ((a_sum, cols_a), (b_sum, cols_b))
        ],
        1,
    )
    out_sum = a_sum[:, 3 * cols_a : 3 * cols_a + width]
    vec_sum = a_sum[:, 3 * cols_a + width :]
    return (
        output.reshape(tokens.shape),
        in_grad.reshape(tokens.shape),
        qkv_sum,
        out_sum,
        pick(0),
        pick(1),
        d_sum,
        vec_sum[:, 2],
        vec_sum[:, 3],
        vec_sum[:, 0],
        vec_sum[:, 1],
    )


def solution(mesh):
    rows3 = P(None, ("shard", "rep"), None)
    rows2 = P("shard", None)
    rows1 = P("shard")
    in_specs = (rows3, P(None, ("shard", "rep"))) + (rows2,) * 5 + (rows1,) * 4 + (rows3,)
    out_specs = (rows3, rows3) + (rows2,) * 5 + (rows1,) * 4
    return jax.shard_map(shards, mesh=mesh, in_specs=in_specs, out_specs=out_specs, check_vma=False)
```

```python
import functools

import jax
import jax.numpy as jnp
import numpy as np
from jax import lax
from jax.experimental import pallas as pl
from jax.experimental.pallas import tpu as pltpu
from jax.sharding import PartitionSpec as P

HEAD_DIM = 64
norm_eps = 1e-12
rope_base = 1000.0
masked_score = -1e30
f32 = jnp.float32
bf16 = jnp.bfloat16
ANY = pl.BlockSpec(memory_space=pl.ANY)
SMEM = pl.BlockSpec(memory_space=pltpu.SMEM)


def dot_nn(a, b):
    return lax.dot_general(a, b, (((1,), (0,)), ((), ())), preferred_element_type=f32)


def dot_nt(a, b):
    return lax.dot_general(a, b, (((1,), (1,)), ((), ())), preferred_element_type=f32)


def dot_tn(a, b):
    return lax.dot_general(a, b, (((0,), (0,)), ((), ())), preferred_element_type=f32)


def whole(shape):
    return pl.BlockSpec(shape, lambda *_: (0,) * len(shape))


def tie(value, *deps):
    return lax.optimization_barrier((value, deps))[0]


def xor_permute(x, bit):
    count = lax.axis_size("shard")
    return lax.ppermute(x, "shard", [(i, i ^ bit) for i in range(count)])


def with_partner(pieces):
    return pieces + [(r | 1, lo, xor_permute(p, 1)) for r, lo, p in pieces]


def gather_direct(own):
    return [(0, 0, own)] + [(r, 0, xor_permute(own, r)) for r in range(2, lax.axis_size("shard"), 2)]


def gather_first(own):
    return xor_permute(own, 2), xor_permute(own, 4)


def gather_second(own, first):
    half = own.shape[0] // 2
    from_x, from_y = first
    far = (xor_permute(from_y[:half], 2), xor_permute(from_x[half:], 4))
    return [(0, 0, own), (2, 0, from_x), (4, 0, from_y), (6, 0, far[0]), (6, half, far[1])]


def add_parts(parts):
    return functools.reduce(jnp.add, [p.astype(f32) for p in parts]).astype(bf16)


def rep_permute(x, pairs):
    return lax.ppermute(x, "rep", pairs)


def load_kernel(jobs, body, *refs):
    operands, rest = refs[: body.operands], refs[body.operands :]
    outs, (hold, sems) = rest[: body.outs], rest[body.outs :]
    half = hold.shape[1]
    copies = []
    for i, (operand, block, part) in enumerate(jobs):
        ref = operands[operand]
        src = ref.at[block, pl.ds(part * half, half), :] if block is not None else ref
        copies.append(pltpu.make_async_copy(src, hold.at[i], sems.at[i]))
        copies[-1].start()
    for copy in copies:
        copy.wait()
    body(hold, *outs)


class Fold:
    def __init__(self, operands, outs, body):
        self.operands, self.outs, self.body = operands, outs, body

    def __call__(self, hold, *outs):
        self.body(hold, *outs)


def fold_call(arrays, jobs, out_shapes, body, half, cols, name):
    count = len(out_shapes)
    return pl.pallas_call(
        functools.partial(load_kernel, jobs, Fold(len(arrays), count, body)),
        in_specs=[pl.BlockSpec(memory_space=pl.ANY)] * len(arrays),
        out_specs=[pl.BlockSpec(memory_space=pltpu.VMEM)] * count,
        out_shape=[jax.ShapeDtypeStruct(s, bf16) for s in out_shapes],
        scratch_shapes=[
            pltpu.VMEM((len(jobs), half, cols), bf16),
            pltpu.SemaphoreType.DMA((len(jobs),)),
        ],
        compiler_params=pltpu.CompilerParams(vmem_limit_bytes=8 << 20),
        cost_estimate=cost(len(jobs) * half * cols, 3 * len(jobs) * half * cols),
        name=name,
    )(*arrays)


def plus(hold, *slots):
    return functools.reduce(jnp.add, [hold[s].astype(f32) for s in slots]).astype(bf16)


def fold_first(keep, got):
    _, rows, cols = keep.shape
    half = rows // 2
    jobs = [(a, q, p) for q, p in ((1, 0), (3, 0), (2, 1), (3, 1)) for a in (0, 1)]

    def body(hold, x_ref, y_ref):
        for n, ref in enumerate((x_ref, x_ref, y_ref, y_ref)):
            ref[n % 2] = plus(hold, 2 * n, 2 * n + 1)

    return fold_call([keep, got], jobs, [(2, half, cols)] * 2, body, half, cols, "fold_first")


def fold_second(keep, got, from_x, from_y):
    _, rows, cols = keep.shape
    half = rows // 2
    jobs = [(0, 2, 0), (1, 2, 0), (2, 1, 0), (0, 1, 1), (1, 1, 1), (3, 1, 0)]

    def body(hold, y_ref, x_ref):
        y_ref[...] = plus(hold, 0, 1, 2)
        x_ref[...] = plus(hold, 3, 4, 5)

    return fold_call(
        [keep, got, from_x, from_y], jobs, [(half, cols)] * 2, body, half, cols, "fold_second"
    )


def fold_own(keep, got, from_x, from_y, last_y, last_x):
    _, rows, cols = keep.shape
    half = rows // 2
    jobs = [
        (0, 0, 0), (1, 0, 0), (2, 0, 0), (4, None, 0), (0, 0, 1), (1, 0, 1), (3, 0, 0), (5, None, 0)
    ]

    def body(hold, own_ref):
        own_ref[:half] = plus(hold, 0, 1, 2, 3)
        own_ref[half:] = plus(hold, 4, 5, 6, 7)

    return fold_call(
        [keep, got, from_x, from_y, last_y, last_x], jobs, [(rows, cols)], body, half, cols, "fold_own"
    )[0]


class Flow:
    def __init__(self, keep, send, odd, direct=False):
        self.held = keep
        self.odd = odd
        self.other = None
        self.pass_on = False
        self.pending = xor_permute(send, 1)
        self.stage = 0
        self.way = direct if keep.shape[0] == 4 and direct in (1, 2) and direct is not True else 0
        self.pair = keep.shape[0] == 4 and not direct
        self.line = lax.axis_size("rep") == 4

    def step(self, *deps):
        got = tie(self.pending, *deps) if deps else self.pending
        stage = self.stage
        if stage == 0:
            self.got = got
            if self.pair:
                self.ready = fold_first(self.held, got)
                self.pending = (xor_permute(self.ready[0], 2), xor_permute(self.ready[1], 4))
            else:
                self.ready = [self.held[q] + got[q] for q in range(got.shape[0])]
                self.pending = [xor_permute(self.ready[q], 2 * q) for q in range(1, got.shape[0])]
        elif stage == 1 and self.way:
            self.first = got
            self.ready = fold_line_second(self.held, self.got, got, 3 - self.way)
            self.pending = xor_permute(self.ready, 2 * (3 - self.way))
        elif stage == 1 and self.pair:
            self.first = got
            if self.pair:
                self.ready = fold_second(self.held, self.got, *got)
                self.pending = (xor_permute(self.ready[0], 4), xor_permute(self.ready[1], 2))
        elif stage <= 2:
            self.stage = 2
            if self.way:
                self.ready = fold_line_own(self.held, self.got, self.first, got)
            elif self.pair:
                self.ready = fold_own(self.held, self.got, *self.first, *got)
            else:
                self.ready = add_parts([self.ready[0]] + list(got))
            if self.other is not None:
                self.ready = jnp.concatenate([self.other, self.ready], 1)
            if self.pass_on:
                self.stage = 6
                return self.ready
            if self.line:
                half = self.ready.shape[0] // 2
                self.mine = jnp.where(self.odd, self.ready[half:], self.ready[:half])
                self.ready = jnp.where(self.odd, self.ready[:half], self.ready[half:])
                self.pending = rep_permute(self.ready, [(0, 1), (1, 0), (2, 3), (3, 2)])
            else:
                self.pending = lax.psum(self.ready, "rep")
        elif not self.line:
            self.ready = got
        elif stage == 3:
            self.ready = add_parts([self.mine, got])
            self.pending = rep_permute(self.ready, [(0, 2), (2, 0), (1, 3), (3, 1)])
        elif stage == 4:
            self.ready = add_parts([self.ready, got])
            self.pending = rep_permute(self.ready, [(0, 1), (1, 0), (2, 3), (3, 2)])
        else:
            low, high = (jnp.where(self.odd, a, b) for a, b in ((got, self.ready), (self.ready, got)))
            self.ready = jnp.concatenate([low, high]).astype(f32)
        self.stage += 1
        return self.ready

    def finish(self):
        while self.stage < 6:
            self.step()
        return self.ready.astype(f32)


def advance(dep, *flows):
    return tuple(flow.step(dep) for flow in flows)


def piece_copies(metas, refs, me, shard_rows, dst, src_lo, dst_lo, cols, sems):
    copies = []
    for i, ((rel, first, rows), ref) in enumerate(zip(metas, refs)):
        at = pl.multiple_of((me ^ rel) * shard_rows + first, 8)
        copies.append(
            pltpu.make_async_copy(
                ref.at[:, pl.ds(src_lo, cols)],
                dst.at[pl.ds(at, rows), pl.ds(dst_lo, cols)],
                sems.at[i],
            )
        )
    return copies


def start_all(copies):
    for copy in copies:
        copy.start()


def wait_all(copies):
    for copy in copies:
        copy.wait()


def metas_of(pieces):
    return tuple((rel, first, p.shape[0]) for rel, first, p in pieces)


def in_hbm(x):
    return pltpu.with_memory_space_constraint(x, pltpu.HBM)


def arrays_of(pieces):
    return [in_hbm(p) for _, _, p in pieces]


def half_mask(shape):
    lane = lax.broadcasted_iota(jnp.int32, shape, len(shape) - 1)
    return (lane % HEAD_DIM) < HEAD_DIM // 2


def unit_rows():
    shape = (8, 128)
    return (
        lax.broadcasted_iota(jnp.int32, shape, 0) == lax.broadcasted_iota(jnp.int32, shape, 1)
    ).astype(bf16)


def normalize(h):
    centre = h - jnp.mean(h, -1, keepdims=True)
    inv = lax.rsqrt(jnp.mean(centre * centre, -1, keepdims=True) + norm_eps)
    return centre * inv, inv


def norm_back(e, n, inv):
    return inv * (e - jnp.mean(e, -1, keepdims=True) - n * jnp.mean(e * n, -1, keepdims=True))


def spread(me, acc_ref, keep_ref, send_ref, cols):
    rows = keep_ref.shape[1]
    chip, core = me // 2, me & 1
    for q in range(keep_ref.shape[0]):
        base = (chip ^ q) * 2
        keep_ref[q, :, cols] = acc_ref[
            pl.ds(pl.multiple_of((base + core) * rows, 8), rows), :
        ].astype(bf16)
        send_ref[q, :, cols] = acc_ref[
            pl.ds(pl.multiple_of((base + 1 - core) * rows, 8), rows), :
        ].astype(bf16)


def cost(flops, read, transcendentals=0):
    return pl.CostEstimate(flops=1000, bytes_accessed=1000, transcendentals=0)


def front_kernel(metas, shard_rows, me_ref, x_ref, table_ref, row_ref, *rest):
    refs, rest = rest[: len(metas)], rest[len(metas) :]
    q_ref, k_ref, v_ref, att_ref, p_ref, w_out, w_ref, bias_ref, sems, back_sem = rest
    s, g = pl.program_id(0), pl.program_id(1)
    width = x_ref.shape[1]
    lanes = p_ref.shape[1] * HEAD_DIM
    copies = piece_copies(metas, refs, me_ref[0], shard_rows, w_ref, 0, 0, 3 * width, sems)
    back = pltpu.make_async_copy(w_ref, w_out, back_sem)

    @pl.when((s == 0) & (g == 0))
    def _():
        start_all(copies)
        wait_all(copies)
        back.start()

    @pl.when(g == 0)
    def _():
        across = jnp.broadcast_to(row_ref[0].astype(f32), bias_ref.shape)
        down = lax.broadcasted_iota(jnp.int32, bias_ref.shape, 0)
        own = lax.broadcasted_iota(jnp.int32, bias_ref.shape, 1) == down
        column = jnp.sum(jnp.where(own, across, 0.0), -1, keepdims=True)
        bias_ref[...] = jnp.where(across == column, 0.0, masked_score).astype(f32)
        x = x_ref[...]
        first = half_mask((x.shape[0], 128))
        cos, sin = spread_tables(table_ref[...])
        sin = jnp.where(first, -sin, sin)
        for part, ref in enumerate((q_ref, k_ref, v_ref)):
            y = dot_nn(x, w_ref[:, part * width : (part + 1) * width])
            for b in range(width // 128):
                cols = slice(b * 128, (b + 1) * 128)
                u = y[:, cols]
                if part < 2:
                    turned = jnp.where(first, pltpu.roll(u, 96, 1), pltpu.roll(u, 32, 1))
                    u = u * cos + turned * sin
                if part == 0:
                    u = u * 0.125
                ref[:, cols] = u.astype(bf16)

    lane = lax.broadcasted_iota(jnp.int32, (1, 128), 1)
    for pair in range(lanes // 128):
        at = pl.ds(pl.multiple_of(g * lanes + pair * 128, 128), 128)
        q, k, v = q_ref[:, at], k_ref[:, at], v_ref[:, at]
        acc = None
        for side in range(2):
            mine = ((lane // HEAD_DIM) == side).astype(bf16)
            score = dot_nt(q, k * mine) + bias_ref[...]
            e = jnp.exp(score - jnp.max(score, -1, keepdims=True))
            inv = 1.0 / jnp.sum(e, -1, keepdims=True)
            p = (e * inv).astype(bf16)
            p_ref[0, pair * 2 + side] = p
            part = dot_nn(p, v * mine)
            acc = part if acc is None else acc + part
        att_ref[:, pair * 128 : (pair + 1) * 128] = acc.astype(bf16)

    @pl.when((s == pl.num_programs(0) - 1) & (g == pl.num_programs(1) - 1))
    def _():
        back.wait()


def front(me, x, table, seg_row, pieces, shard_rows):
    rows, width = x.shape
    metas = metas_of(pieces)
    seqs, _, seq = seg_row.shape
    heads = width // HEAD_DIM
    quad = 4
    lanes = quad * HEAD_DIM
    by_seq = pl.BlockSpec((seq, width), lambda s, g: (s, 0))
    wide = jax.ShapeDtypeStruct((rows, width), bf16)
    return pl.pallas_call(
        functools.partial(front_kernel, metas, shard_rows),
        grid=(seqs, width // lanes),
        in_specs=[
            SMEM, by_seq, whole(table.shape),
            pl.BlockSpec((1, 1, seq), lambda s, g: (s, 0, 0)),
        ]
        + [ANY] * len(metas),
        out_specs=[by_seq] * 3
        + [
            pl.BlockSpec((seq, lanes), lambda s, g: (s, g)),
            pl.BlockSpec((1, quad, seq, seq), lambda s, g: (s, g, 0, 0)),
            ANY,
        ],
        out_shape=[wide] * 4
        + [
            jax.ShapeDtypeStruct((seqs, heads, seq, seq), bf16),
            jax.ShapeDtypeStruct((width, 3 * width), bf16),
        ],
        scratch_shapes=[
            pltpu.VMEM((width, 3 * width), bf16),
            pltpu.VMEM((seq, seq), f32),
            pltpu.SemaphoreType.DMA((len(metas),)),
            pltpu.SemaphoreType.DMA,
        ],
        cost_estimate=cost(
            6 * rows * width * width + 4 * seqs * heads * seq * seq * 256,
            30_000_000,
            seqs * heads * seq * seq,
        ),
        name="qkv_attend",
    )(me, x, table, seg_row, *[p for _, _, p in pieces])


VM = pl.BlockSpec(memory_space=pltpu.VMEM)
HBM = pl.BlockSpec(memory_space=pltpu.HBM)


def in_vmem(shape, dtype=bf16):
    return pltpu.VMEM(shape, dtype)


def limit(mib):
    return pltpu.CompilerParams(vmem_limit_bytes=mib << 20)


def gate_kernel(metas, shard_rows, me_ref, tok_ref, att_ref, *rest):
    refs, rest = rest[: len(metas)], rest[len(metas) :]
    h_ref, a_ref, b_ref, x_ref, n1_ref, inv_ref, vec_ref, wo_ref = rest[:8]
    wg_ref, wv_ref, sems, sems_o = rest[8:]
    hidden = a_ref.shape[1]
    width = wo_ref.shape[1]
    block = 768
    steps = hidden // block
    me = me_ref[0]

    def spans(j):
        return pl.multiple_of(j * block, block), pl.multiple_of(hidden + j * block, block)

    def copies(j):
        both = []
        for part, lo in enumerate(spans(j)):
            both += piece_copies(metas, refs, me, shard_rows, wg_ref, lo, lo, block, sems.at[j, part])
        return both

    copies_o = piece_copies(
        metas, refs, me, shard_rows, wo_ref, 2 * hidden, 0, width, sems_o.at[0]
    ) + piece_copies(metas, refs, me, shard_rows, wv_ref, 2 * hidden + width, 0, 128, sems_o.at[1])
    start_all(copies_o)

    @pl.loop(0, steps)
    def _(j):
        start_all(copies(j))

    wait_all(copies_o)
    vec_ref[...] = dot_nt(unit_rows(), wv_ref[...])

    @pl.loop(0, 2)
    def _(i):
        rows = tok_ref.shape[0] // 2
        at = pl.ds(pl.multiple_of(i * rows, 8), rows)
        n, inv = normalize(tok_ref[at, :].astype(f32) + dot_nn(att_ref[at, :], wo_ref[...]))
        n1_ref[at, :] = n.astype(bf16)
        inv_ref[at, :] = jnp.broadcast_to(inv, (rows, inv_ref.shape[1]))
        x_ref[at, :] = (n * vec_ref[0:1] + vec_ref[1:2]).astype(bf16)

    @pl.loop(0, steps)
    def _(j):
        wait_all(copies(j))
        gate_at, up_at = (pl.ds(lo, block) for lo in spans(j))
        half = x_ref.shape[0] // 2
        for r in range(2):
            rows = slice(r * half, (r + 1) * half)
            gate = dot_nn(x_ref[rows, :], wg_ref[:, gate_at])
            up = dot_nn(x_ref[rows, :], wg_ref[:, up_at])
            s = 0.5 * jnp.tanh(0.5 * gate) + 0.5
            act = gate * s
            h_ref[rows, gate_at] = (act * up).astype(bf16)
            b_ref[rows, gate_at] = act.astype(bf16)
            a_ref[rows, gate_at] = (up * (s + act * (1.0 - s))).astype(bf16)


def gate_forward(me, tokens, attended, pieces, shard_rows, hidden):
    rows, width = tokens.shape
    metas = metas_of(pieces)
    return pl.pallas_call(
        functools.partial(gate_kernel, metas, shard_rows),
        in_specs=[SMEM, VM, VM] + [ANY] * len(metas),
        out_specs=[VM] * 8,
        out_shape=[in_vmem((rows, hidden))] * 3
        + [
            in_vmem((rows, width)),
            in_vmem((rows, width)),
            in_vmem((rows, 128), f32),
            in_vmem((8, width), f32),
            in_vmem((width, width)),
        ],
        scratch_shapes=[
            pltpu.VMEM((width, 2 * hidden), bf16),
            pltpu.VMEM((width, 128), bf16),
            pltpu.SemaphoreType.DMA((hidden // 768, 2, len(metas))),
            pltpu.SemaphoreType.DMA((2, len(metas))),
        ],
        compiler_params=limit(19),
        cost_estimate=cost(4 * rows * width * hidden, 10_000_000, rows * hidden),
        name="out_gate_up",
    )(me, tokens, attended, *arrays_of(pieces))


def down_kernel(metas, shard_rows, me_ref, h_ref, n1_ref, cot_ref, vec_ref, *rest):
    refs = rest[: len(metas)]
    out_ref, low_ref, sums_ref, keep_ref, send_ref, w_ref, acc_ref, sems = rest[len(metas) :]
    me = me_ref[0]
    copies = piece_copies(metas, refs, me, shard_rows, w_ref, 0, 0, w_ref.shape[1], sems)
    start_all(copies)
    sums_ref[...] = jnp.zeros_like(sums_ref)
    wait_all(copies)
    block = 256

    @pl.loop(0, h_ref.shape[0] // block)
    def _(i):
        at = pl.ds(pl.multiple_of(i * block, block), block)
        mixed = n1_ref[at, :].astype(f32) * vec_ref[0:1] + vec_ref[1:2]
        n, inv = normalize(mixed + dot_nn(h_ref[at, :], w_ref[...]))
        out_ref[at, :] = (n * vec_ref[2:3] + vec_ref[3:4]).astype(bf16)
        cot = cot_ref[at, :].astype(f32)
        sums_ref[0:1] += jnp.sum(cot * n, 0, keepdims=True)
        sums_ref[1:2] += jnp.sum(cot, 0, keepdims=True)
        low_ref[at, :] = norm_back(cot * vec_ref[2:3], n, inv).astype(bf16)

    per_chip = acc_ref.shape[0]
    half = per_chip // 2
    core = me & 1

    @pl.loop(0, keep_ref.shape[0])
    def _(q):
        lo = pl.multiple_of(((me // 2) ^ q) * per_chip, 128)
        acc_ref[...] = dot_tn(h_ref[:, pl.ds(lo, per_chip)], low_ref[...])
        keep_ref[q] = acc_ref[pl.ds(pl.multiple_of(core * half, 8), half), :].astype(bf16)
        send_ref[q] = acc_ref[pl.ds(pl.multiple_of((1 - core) * half, 8), half), :].astype(bf16)


def down_forward(me, hidden_low, n1, cot, vec, pieces, shard_rows, chips):
    rows, hidden = hidden_low.shape
    width = n1.shape[1]
    metas = metas_of(pieces)
    per_chip = hidden // chips
    return pl.pallas_call(
        functools.partial(down_kernel, metas, shard_rows),
        in_specs=[SMEM, VM, VM, VM, VM] + [ANY] * len(metas),
        out_specs=[VM] * 6,
        out_shape=[
            jax.ShapeDtypeStruct((rows, width), bf16),
            in_vmem((rows, width)),
            in_vmem((8, width), f32),
            jax.ShapeDtypeStruct((chips, per_chip // 2, width), bf16),
            jax.ShapeDtypeStruct((chips, per_chip // 2, width), bf16),
            in_vmem((hidden, width)),
        ],
        scratch_shapes=[
            pltpu.VMEM((per_chip, width), f32),
            pltpu.SemaphoreType.DMA((len(metas),)),
        ],
        compiler_params=limit(19),
        cost_estimate=cost(4 * rows * width * hidden, 10_000_000, rows),
        name="down_norm_grad",
    )(me, hidden_low, n1, cot, vec, *arrays_of(pieces))


def hidden_grad_kernel(
    first, steps, me_ref, g_ref, x_ref, a_ref, b_ref, w_ref, gg_ref, gu_ref, _g, _w, keep_ref, send_ref, acc_ref
):
    block = 768

    @pl.loop(0, steps)
    def _(j):
        cols = pl.ds(pl.multiple_of((first + j) * block, block), block)
        half = g_ref.shape[0] // 2
        for r in range(2):
            rows = slice(r * half, (r + 1) * half)
            gh = dot_nt(g_ref[rows, :], w_ref[cols, :])
            gg_ref[rows, cols] = (gh * a_ref[rows, cols].astype(f32)).astype(bf16)
            gu_ref[rows, cols] = (gh * b_ref[rows, cols].astype(f32)).astype(bf16)
        for part, ref in enumerate((gg_ref, gu_ref)):
            acc_ref[...] = dot_tn(x_ref[...], ref[:, cols])
            lo = pl.multiple_of((2 * j + part) * block, block)
            spread(me_ref[0], acc_ref, keep_ref, send_ref, pl.ds(lo, block))


def hidden_grad(me, g2low, low, a, b, w_down, first, steps, count, name):
    rows, width = g2low.shape
    block = 768
    chips, shard_rows = count // 2, width // count
    part = jax.ShapeDtypeStruct((chips, shard_rows, 2 * block * steps), bf16)
    return pl.pallas_call(
        functools.partial(hidden_grad_kernel, first, steps),
        in_specs=[SMEM, VM, VM, VM, VM, VM],
        out_specs=[VM] * 6,
        out_shape=[
            in_vmem(a.shape), in_vmem(b.shape), in_vmem(g2low.shape), in_vmem(w_down.shape), part, part
        ],
        input_output_aliases={3: 0, 4: 1, 1: 2, 5: 3},
        scratch_shapes=[pltpu.VMEM((width, block), f32)],
        compiler_params=limit(19),
        cost_estimate=cost(6 * rows * width * block * steps, 5_000_000),
        name=name,
    )(me, g2low, low, a, b, w_down)


def mixed_grad_kernel(
    metas, shard_rows, me_ref, gg_ref, gu_ref, g2_ref, n1_ref, inv_ref, vec_ref, wo_ref, *rest
):
    refs, rest = rest[: len(metas)], rest[len(metas) :]
    low_ref, gatt_ref, sums_ref, _gg, _gu, _g2, w_ref, sems = rest
    hidden = gg_ref.shape[1]
    block = 256
    copies = [
        piece_copies(
            metas, refs, me_ref[0], shard_rows, w_ref, c * hidden, c * hidden, hidden, sems.at[c]
        )
        for c in range(2)
    ]
    start_all(copies[0])
    start_all(copies[1])
    sums_ref[...] = jnp.zeros_like(sums_ref)

    def rows(at, waits):
        if waits:
            wait_all(copies[0])
        gm = g2_ref[at, :].astype(f32) + dot_nt(gg_ref[at, :], w_ref[:, :hidden])
        if waits:
            wait_all(copies[1])
        gm += dot_nt(gu_ref[at, :], w_ref[:, hidden:])
        n = n1_ref[at, :].astype(f32)
        sums_ref[0:1] += jnp.sum(gm * n, 0, keepdims=True)
        sums_ref[1:2] += jnp.sum(gm, 0, keepdims=True)
        low = norm_back(gm * vec_ref[0:1], n, inv_ref[at, 0:1]).astype(bf16)
        low_ref[at, :] = low
        gatt_ref[at, :] = dot_nt(low, wo_ref[...]).astype(bf16)

    rows(slice(0, block), True)

    @pl.loop(1, gg_ref.shape[0] // block)
    def _(i):
        rows(pl.ds(pl.multiple_of(i * block, block), block), False)


def mixed_grad(me, gg, gu, g2, n1, inv1, vec, w_out, pieces, shard_rows):
    rows, width = g2.shape
    hidden = gg.shape[1]
    metas = metas_of(pieces)
    return pl.pallas_call(
        functools.partial(mixed_grad_kernel, metas, shard_rows),
        in_specs=[SMEM] + [VM] * 7 + [ANY] * len(metas),
        out_specs=[VM] * 6,
        out_shape=[
            jax.ShapeDtypeStruct((rows, width), bf16),
            jax.ShapeDtypeStruct((rows, width), bf16),
            jax.ShapeDtypeStruct((8, width), f32),
            in_vmem(gg.shape),
            in_vmem(gu.shape),
            in_vmem(g2.shape),
        ],
        input_output_aliases={1: 3, 2: 4, 3: 5},
        scratch_shapes=[
            pltpu.VMEM((width, 2 * hidden), bf16),
            pltpu.SemaphoreType.DMA((2, len(metas))),
        ],
        compiler_params=limit(19),
        cost_estimate=cost(4 * rows * width * hidden + 2 * rows * width * width, 15_000_000),
        name="mixed_grad",
    )(me, gg, gu, g2, n1, inv1, vec, w_out, *arrays_of(pieces))[:3]


def attend_back_kernel(
    q_ref, k_ref, v_ref, o_ref, g_ref, p_ref, table_ref, d_ref
):
    heads = p_ref.shape[1]
    lane = lax.broadcasted_iota(jnp.int32, (1, 128), 1)
    first = half_mask(table_ref.shape)
    cos, sin = spread_tables(table_ref[...])

    def unrotate(g):
        t = g * sin
        return g * cos + jnp.where(first, pltpu.roll(t, 96, 1), -pltpu.roll(t, 32, 1))

    for pair in range(heads // 2):
        cols = slice(pair * 128, (pair + 1) * 128)
        q, k, v, g = q_ref[:, cols], k_ref[:, cols], v_ref[:, cols], g_ref[:, cols]
        go = g.astype(f32) * o_ref[:, cols].astype(f32)
        dq = dk = dv = None
        for side in range(2):
            mine = (lane // HEAD_DIM) == side
            keep = mine.astype(bf16)
            p = p_ref[0, pair * 2 + side]
            row = jnp.sum(jnp.where(mine, go, 0.0), -1, keepdims=True)
            gp = dot_nt(g, v * keep)
            gs = (p.astype(f32) * (gp - row)).astype(bf16)
            parts = (dot_nn(gs, k * keep), dot_tn(gs, q * keep), dot_tn(p, g * keep))
            if dq is None:
                dq, dk, dv = parts
            else:
                dq, dk, dv = dq + parts[0], dk + parts[1], dv + parts[2]
        d_ref[0, :, cols] = unrotate(dq * 0.125).astype(bf16)
        d_ref[1, :, cols] = unrotate(dk).astype(bf16)
        d_ref[2, :, cols] = dv.astype(bf16)


def attend_backward(q, k, v, attended, gatt, probs, table, first, steps, name):
    rows, _ = attended.shape
    seqs, _, seq, _ = probs.shape
    quad = 4
    lanes = quad * HEAD_DIM
    spec_in = pl.BlockSpec((seq, lanes), lambda s, g: (s, first + g))
    return pl.pallas_call(
        attend_back_kernel,
        grid=(seqs, steps),
        in_specs=[spec_in] * 5
        + [
            pl.BlockSpec((1, quad, seq, seq), lambda s, g: (s, first + g, 0, 0)),
            pl.BlockSpec(table.shape, lambda s, g: (0, 0)),
        ],
        out_specs=pl.BlockSpec((3, seq, lanes), lambda s, g: (0, s, g)),
        out_shape=jax.ShapeDtypeStruct((3, rows, lanes * steps), bf16),
        compiler_params=limit(16),
        cost_estimate=cost(8 * seqs * quad * steps * seq * seq * 256, 9_000_000 * steps),
        name=name,
    )(q, k, v, attended, gatt, probs, table)


def qkv_grad_kernel(extra, me_ref, x_ref, d_ref, *rest):
    me = me_ref[0]
    if extra:
        att_ref, g1_ref, s2_ref, s1_ref = rest[:4]
    keep_ref, send_ref, acc_ref = rest[-3:]
    width = x_ref.shape[1]

    def put(value, lo):
        cols = value.shape[1]
        acc_ref[:, :cols] = value
        spread(me, acc_ref.at[:, :cols], keep_ref, send_ref, slice(lo, lo + cols))
        return lo + cols

    cols = d_ref.shape[2]

    @pl.loop(0, 3)
    def _(part):
        acc_ref[:, :cols] = dot_tn(x_ref[...], d_ref[part])
        lo = pl.multiple_of(part * cols, 128)
        spread(me, acc_ref.at[:, :cols], keep_ref, send_ref, pl.ds(lo, cols))

    lo = 3 * cols
    if extra:
        lo = put(dot_tn(att_ref[...], g1_ref[...]), lo)
        row = lax.broadcasted_iota(jnp.int32, (8, width), 0)
        rows = jnp.where(row < 2, s2_ref[...], pltpu.roll(s1_ref[...], 2, 0)).astype(bf16)
        put(dot_tn(rows, unit_rows()), lo)


def qkv_grad(me, x, parts, extra, count, name):
    rows, width = x.shape
    cols = parts.shape[2]
    chips, shard_rows = count // 2, width // count
    total = 3 * cols + (width + 128 if extra else 0)
    shape = jax.ShapeDtypeStruct((chips, shard_rows, total), bf16)
    vmem = pl.BlockSpec(memory_space=pltpu.VMEM)
    return pl.pallas_call(
        functools.partial(qkv_grad_kernel, bool(extra)),
        in_specs=[SMEM] + [vmem] * (2 + len(extra)),
        out_specs=[vmem, vmem],
        out_shape=[shape, shape],
        scratch_shapes=[pltpu.VMEM((width, width), f32)],
        compiler_params=limit(20),
        cost_estimate=cost(2 * rows * width * total, 12_000_000),
        name=name,
    )(me, x, parts, *extra)


def input_grad_kernel(g1_ref, w_ref, *rest):
    out_ref = rest[-1]
    width = out_ref.shape[1]
    total = g1_ref[...].astype(f32)
    for p in range(3):
        lo = p * width
        for ref in rest[:-1]:
            total += dot_nt(ref[p], w_ref[:, lo : lo + ref.shape[2]])
            lo += ref.shape[2]
    out_ref[...] = total.astype(bf16)


def input_grad(g1, w_qkv, parts):
    rows, width = g1.shape
    block = 512
    by_row = pl.BlockSpec((block, width), lambda i: (i, 0))
    return pl.pallas_call(
        input_grad_kernel,
        grid=(rows // block,),
        in_specs=[by_row, whole(w_qkv.shape)]
        + [pl.BlockSpec((3, block, p.shape[2]), lambda i: (0, i, 0)) for p in parts],
        out_specs=by_row,
        out_shape=jax.ShapeDtypeStruct((rows, width), bf16),
        compiler_params=limit(20),
        cost_estimate=cost(6 * rows * width * width, 14_000_000),
        name="input_grad",
    )(g1, w_qkv, *parts)


def rope_tables(seq_len):
    frequency = rope_base ** (-np.arange(0, HEAD_DIM, 2, dtype=np.float32) / HEAD_DIM)
    frequency = jnp.asarray(np.tile(frequency.astype(np.float32), 4))[None, :]
    shape = (seq_len, 128)
    angles = lax.broadcasted_iota(jnp.int32, shape, 0).astype(f32) * frequency
    lane = lax.broadcasted_iota(jnp.int32, shape, 1)
    return jnp.where(lane // 32 % 2 == 0, jnp.cos(angles), jnp.sin(angles))


def spread_tables(table):
    shifted = pltpu.roll(table, 32, 1)
    even = lax.broadcasted_iota(jnp.int32, table.shape, 1) // 32 % 2 == 0
    return jnp.where(even, table, shifted), jnp.where(even, shifted, table)


def shards(
    tokens, segment_ids, qkv_weight, out_weight, gate_weight, up_weight, down_weight,
    norm1_gain, norm1_bias, norm2_gain, norm2_bias, out_grad,
):
    count = lax.axis_size("shard")
    me = lax.axis_index("shard").astype(jnp.int32).reshape(1)
    batches, seq, width = tokens.shape
    shard_rows = qkv_weight.shape[0]
    down_rows = down_weight.shape[0]
    hidden = gate_weight.shape[1]
    rows = batches * seq
    chips = count // 2

    x = tokens.reshape(rows, width)
    cot = out_grad.reshape(rows, width)
    table = rope_tables(seq)
    vectors = jnp.stack([norm1_gain, norm1_bias, norm2_gain, norm2_bias], 1)
    vectors = jnp.pad(vectors, ((0, 0), (0, 124)))
    odd = (lax.axis_index("rep") % 2 == 1).reshape(1, 1)

    pieces_a = gather_direct(qkv_weight)
    own_b = jnp.concatenate([gate_weight, up_weight, out_weight, vectors], 1)
    seg = segment_ids.reshape(batches, 1, seq)
    table, seg, own_b, odd, ready = tie((table, seg, own_b, odd, pieces_a[0][2]))
    pieces_a = [(r, lo, tie(p, ready, seg, odd, table)) for r, lo, p in pieces_a]
    far_a = tuple(p for _, _, p in pieces_a[1:])
    pieces_a = with_partner(pieces_a)
    own_b = tie(own_b, far_a)
    if count == 8:
        first_b = gather_first(own_b)
        first_c = gather_first(tie(down_weight, far_a))
    else:
        pieces_b = gather_direct(own_b)
        pieces_c = gather_direct(down_weight)
    q, k, v, attended, probs, w_qkv = front(me, x, table, seg, pieces_a, shard_rows)
    if count == 8:
        first_b = tie(first_b, attended)
        pieces_b = gather_second(own_b, first_b)
        half = down_rows // 2
        c_x, c_y = tie(first_c, first_b)
        c_low, c_high = lax.optimization_barrier((c_y[:half], c_x[half:]))
        pieces_b = pieces_b[:3] + [(r, lo, tie(p, c_low, c_high)) for r, lo, p in pieces_b[3:]]
        pieces_c = [
            (0, 0, down_weight), (2, 0, c_x), (4, 0, c_y),
            (6, 0, xor_permute(c_low, 2)), (6, half, xor_permute(c_high, 4)),
        ]
    pieces_b = with_partner(pieces_b)
    near_c = with_partner(pieces_c[:3])
    hidden_low, back_gate, back_up, low, n1, inv1, vec, w_out = gate_forward(
        me, x, attended, pieces_b, shard_rows, hidden
    )
    if count == 8:
        pieces_c = near_c + with_partner([(r, lo, tie(p, low)) for r, lo, p in pieces_c[3:]])
    else:
        pieces_c = with_partner(pieces_c)
    output, g2low, sums2, d_keep, d_send, w_down = down_forward(
        me, hidden_low, n1, cot, vec, pieces_c, down_rows, chips
    )
    steps = hidden // 768 // 2
    flow_d = Flow(d_keep, d_send, odd, False)
    ready = sums2
    grads1 = hidden_grad(
        me, tie(g2low, ready), low, back_gate, back_up, w_down, 0, steps, count, "hidden_grad_1"
    )
    flow_e = Flow(*grads1[4:], odd, False)
    ready = advance(grads1[0], flow_d)
    grads2 = hidden_grad(
        me, tie(grads1[2], ready), low, *grads1[:2], grads1[3], steps, steps, count, "hidden_grad_2"
    )
    flow_f = Flow(*grads2[4:], odd, False)
    ready = advance(grads2[0], flow_e)
    g1low, gatt, sums1 = mixed_grad(
        me, *grads2[:2], tie(grads2[2], ready), n1, inv1, vec, w_out, pieces_b, shard_rows
    )
    ready = advance(g1low, flow_f, flow_d)
    back_a = attend_backward(
        q, k, v, attended, tie(gatt, ready), probs, table, 0, 2, "attend_bwd_1"
    )
    ready = advance(back_a, flow_e, flow_d)
    a_keep, a_send = qkv_grad(
        me, x, tie(back_a, ready), (attended, g1low, sums2, sums1), count, "qkv_out_grad_1"
    )
    flow_a = Flow(a_keep, a_send, odd, False)
    ready = advance(a_keep, flow_f, flow_e, flow_d)
    back_b = attend_backward(
        q, k, v, attended, tie(gatt, ready), probs, table, 2, 1, "attend_bwd_2"
    )
    ready = advance(back_b, flow_a, flow_f, flow_e, flow_d)
    b_keep, b_send = qkv_grad(me, x, tie(back_b, ready), (), count, "qkv_grad_2")
    flow_b = Flow(b_keep, b_send, odd, True)
    ready = advance(b_keep, flow_d)
    ready = advance(ready, flow_b)
    in_grad = input_grad(tie(g1low, ready), w_qkv, [back_a, back_b])
    ready = advance(in_grad, flow_a)
    ready = advance(ready, flow_f, flow_e)
    flow_a.pass_on = True
    flow_b.other = flow_a.step(ready)
    ready = advance(ready, flow_b, flow_f, flow_e)
    d_sum, e_sum, f_sum = [flow.finish() for flow in (flow_d, flow_e, flow_f)]
    total = flow_b.finish()
    a_sum, b_sum = total[:, : a_keep.shape[2]], total[:, a_keep.shape[2] :]

    block = 768
    hidden_sums = (e_sum, f_sum)
    pick = lambda part: jnp.concatenate(
        [
            s[:, (2 * j + part) * block : (2 * j + part + 1) * block]
            for s in hidden_sums
            for j in range(steps)
        ],
        1,
    )
    cols_a, cols_b = back_a.shape[2], back_b.shape[2]
    qkv_sum = jnp.concatenate(
        [
            s[:, p * c : (p + 1) * c]
            for p in range(3)
            for s, c in ((a_sum, cols_a), (b_sum, cols_b))
        ],
        1,
    )
    out_sum = a_sum[:, 3 * cols_a : 3 * cols_a + width]
    vec_sum = a_sum[:, 3 * cols_a + width :]
    return (
        output.reshape(tokens.shape),
        in_grad.reshape(tokens.shape),
        qkv_sum,
        out_sum,
        pick(0),
        pick(1),
        d_sum,
        vec_sum[:, 2],
        vec_sum[:, 3],
        vec_sum[:, 0],
        vec_sum[:, 1],
    )


def solution(mesh):
    rows3 = P(None, ("shard", "rep"), None)
    rows2 = P("shard", None)
    rows1 = P("shard")
    in_specs = (rows3, P(None, ("shard", "rep"))) + (rows2,) * 5 + (rows1,) * 4 + (rows3,)
    out_specs = (rows3, rows3) + (rows2,) * 5 + (rows1,) * 4
    return jax.shard_map(shards, mesh=mesh, in_specs=in_specs, out_specs=out_specs, check_vma=False)
```
